256 devices in a mesh: gx: 32 (over y, x, core), gz: 8 (over z).
Axes of the slice: x: 4, y: 4, z: 8, core: 2. Of those that a mesh axis runs over, the one named last changes fastest.
Arguments:
- charge: float32 [512, 128, 128], P('gx', 'gz'), may hold values from -4 to 4
- region_codes: int32 [512, 128, 128], P('gx', 'gz'), may hold values from 0 to 7
- eps_table: float32 [8], replicated, may hold values from 0.025 to 1
- screen_table: float32 [8], replicated, may hold values from 0.005 to 0.05
Outputs:
- potential: float32 [512, 128, 128], P('gx', 'gz')
The draws below stay inside these ranges and needn't reach their ends.
All inputs are finite; a program needn't handle non-finite values.
Results may differ from the reference program's by a relative error of at most 0.0001.
Values sent between devices are 32-bit elements; how exact they have to be, the bound alone decides.
A program may use at most 128 MiB of HBM per device.

```python
import math
import jax
import jax.numpy as jnp
from jax import lax

NY = 128
REGIONS = 8
LEVELS = 6
COARSE_SWEEPS = 8
NX = 512
NZ = 128


def draw_charge(key, part):
    noise_key = jax.random.fold_in(key, 11)
    phase_key = jax.random.fold_in(key, 23)
    phase = jax.random.uniform(phase_key, (), jnp.float32, -3.0, 3.0)
    xs = jnp.arange(NX, dtype=jnp.float32)[:, None, None] / NX
    zs = jnp.arange(NZ, dtype=jnp.float32)[None, :, None] / NZ
    noise = 0.5 * jnp.clip(jax.random.normal(noise_key, (NX, NZ, NY), jnp.float32), -6.0, 6.0)
    level = 0.1
    smooth = level * (1.0 + 0.5 * jnp.sin(6.2831853 * xs + phase) * jnp.cos(6.2831853 * zs))
    return noise + smooth


def draw_region_codes(key, part):
    block_key = jax.random.fold_in(key, 31)
    fine_key = jax.random.fold_in(key, 37)
    pick_key = jax.random.fold_in(key, 41)
    blocks = jax.random.randint(block_key, (NX // 16, NZ // 16, NY // 16), 0, REGIONS)
    blocky = jnp.repeat(jnp.repeat(jnp.repeat(blocks, 16, axis=0), 16, axis=1), 16, axis=2)
    fine = jax.random.randint(fine_key, (NX, NZ, NY), 0, REGIONS)
    pick = jax.random.randint(pick_key, (NX, NZ, NY), 0, 4)
    return jnp.where(pick == 0, fine, blocky).astype(jnp.int32)


def setup_inputs(seed: int = 0) -> dict:
    keys = jax.random.split(jax.random.key(seed), 5)
    return {
        "charge": draw_charge(jax.random.fold_in(keys[4], 71), 0),
        "region_codes": draw_region_codes(jax.random.fold_in(keys[4], 71), 0),
        "eps_table": jnp.clip(jnp.exp(jax.random.uniform(keys[2], (REGIONS,), jnp.float32, math.log(0.025), math.log(1.0))), 0.025, 1.0),
        "screen_table": jnp.clip(jnp.exp(jax.random.uniform(keys[3], (REGIONS,), jnp.float32, math.log(0.005), math.log(0.05))), 0.005, 0.05),
    }


OMEGA = 0.8

def lookup(region_codes, lookup_table):
    summed = jnp.zeros(region_codes.shape, jnp.float32)
    for region in range(lookup_table.shape[0]):
        summed = summed + jnp.where(region_codes == region, lookup_table[region], jnp.zeros((), jnp.float32))
    return summed

def face_weights(padded, screen, spacing):
    wide_x = spacing * 0.5 * (padded[1:, 1:-1, 1:-1] + padded[:-1, 1:-1, 1:-1])
    wide_z = spacing * 0.5 * (padded[1:-1, 1:, 1:-1] + padded[1:-1, :-1, 1:-1])
    wide_y = spacing * 0.5 * (padded[1:-1, 1:-1, 1:] + padded[1:-1, 1:-1, :-1])
    diagonal = wide_x[1:] + wide_x[:-1] + wide_z[:, 1:] + wide_z[:, :-1] + wide_y[:, :, 1:] + wide_y[:, :, :-1] + screen
    return (wide_x, wide_z, wide_y, diagonal)

def operate(padded, diagonal, wide_x, wide_z, wide_y):
    centre = padded[1:-1, 1:-1, 1:-1]
    beside = wide_x[1:] * padded[2:, 1:-1, 1:-1] + wide_x[:-1] * padded[:-2, 1:-1, 1:-1]
    beside = beside + wide_z[:, 1:] * padded[1:-1, 2:, 1:-1] + wide_z[:, :-1] * padded[1:-1, :-2, 1:-1]
    beside = beside + wide_y[:, :, 1:] * padded[1:-1, 1:-1, 2:] + wide_y[:, :, :-1] * padded[1:-1, 1:-1, :-2]
    return diagonal * centre - beside

def turned(values):
    return jnp.transpose(values, (0, 2, 1))

def line_solve(sub_diag, diagonal, super_diag, right_side):
    sub_diag = sub_diag.at[:, 0, :].set(0.0)
    super_diag = super_diag.at[:, -1, :].set(0.0)
    solved = lax.linalg.tridiagonal_solve(turned(sub_diag), turned(diagonal), turned(super_diag), turned(right_side)[..., None])
    return turned(solved[..., 0])

def restrict(values):
    size_x, size_z, size_y = values.shape
    blocks = values.reshape(size_x // 2, 2, size_z // 2, 2, size_y // 2, 2)
    return jnp.mean(blocks, axis=(1, 3, 5))

def prolong(values):
    return jnp.repeat(jnp.repeat(jnp.repeat(values, 2, axis=0), 2, axis=1), 2, axis=2)

def vcycle(source, eps_cell, screen, level_index):
    wide_x, wide_z, wide_y, diagonal = face_weights(jnp.pad(eps_cell, 1), screen, 0.5 ** level_index)
    sub_diag = -wide_z[:, :-1]
    super_diag = -wide_z[:, 1:]
    if level_index == LEVELS:
        potential = jnp.zeros_like(source)
        for sweep_index in range(COARSE_SWEEPS):
            residual = source - operate(jnp.pad(potential, 1), diagonal, wide_x, wide_z, wide_y)
            potential = potential + OMEGA * line_solve(sub_diag, diagonal, super_diag, residual)
        return potential
    potential = OMEGA * line_solve(sub_diag, diagonal, super_diag, source)
    residual = source - operate(jnp.pad(potential, 1), diagonal, wide_x, wide_z, wide_y)
    coarse = vcycle(restrict(residual), restrict(eps_cell), restrict(screen), level_index + 1)
    potential = potential + prolong(coarse)
    residual = source - operate(jnp.pad(potential, 1), diagonal, wide_x, wide_z, wide_y)
    potential = potential + OMEGA * line_solve(sub_diag, diagonal, super_diag, residual)
    return potential

def reference(charge, region_codes, eps_table, screen_table):
    eps_cell = lookup(region_codes, eps_table)
    screen = lookup(region_codes, screen_table)
    return vcycle(charge, eps_cell, screen, 0)
```

```python
import jax
import jax.numpy as jnp
from jax import lax
from jax.experimental import pallas as pl
from jax.experimental.pallas import tpu as pltpu
from jax.sharding import PartitionSpec as P

OMEGA = 0.8
SWEEPS = 8
LAST = 6
F32 = jnp.float32
MESH = pl.DeviceIdType.MESH


def iota(shape, dim):
    return lax.broadcasted_iota(jnp.int32, shape, dim)


def roll(v, shift, axis):
    size = v.shape[axis]
    return pltpu.roll(v, shift % size, axis)


class Level:
    def __init__(self, index, refs, whole, slab):
        (self.E, self.S, self.WXM, self.WXP, self.WYM, self.WYP, self.WZ, self.D, self.A, self.M, self.F, self.U, self.R, self.Y,
         self.V, self.C) = refs
        self.index, self.whole, self.n = index, whole, slab
        self.Z, self.X = self.S.shape[0], self.S.shape[1]
        self.mask = None

    @staticmethod
    def scratch(Z, X):
        sizes = (Z + 2, Z, Z, Z, Z, Z, Z + 1, Z, Z + 1, Z, Z, Z, Z, Z, Z + 2, Z + 2)
        return [pltpu.VMEM((s, X, 128), F32) for s in sizes]


def loop(count, body):
    def step(i, carry):
        body(i)
        return carry

    lax.fori_loop(0, count, step, 0)


def couplings(lev, z0, n):
    h = 0.5 ** lev.index * 0.5
    sh = 2 ** lev.index
    X = lev.X
    e = lev.E[pl.ds(z0 + 1, n)]
    lane = iota((n, X, 128), 2)
    first, last = lane < sh, lane >= 128 - sh
    up, down = roll(e, 1, 1), roll(e, -1, 1)
    if lev.whole:
        row = iota((n, X, 128), 1)
        up, down = jnp.where(row == 0, 0.0, up), jnp.where(row == X - 1, 0.0, down)
    left, right = jnp.where(first, 0.0, roll(e, sh, 2)), jnp.where(last, 0.0, roll(e, -sh, 2))
    wxm, wxp, wym, wyp = h * (e + up), h * (e + down), h * (e + left), h * (e + right)
    wzm, wzp = h * (e + lev.E[pl.ds(z0, n)]), h * (e + lev.E[pl.ds(z0 + 2, n)])
    lev.D[pl.ds(z0, n)] = wxm + wxp + wzm + wzp + wym + wyp + lev.S[pl.ds(z0, n)]
    if lev.whole:
        wxm, wxp = jnp.where(row == 0, 0.0, wxm), jnp.where(row == X - 1, 0.0, wxp)
    lev.WXM[pl.ds(z0, n)] = wxm
    lev.WXP[pl.ds(z0, n)] = wxp
    lev.WYM[pl.ds(z0, n)] = jnp.where(first, 0.0, wym)
    lev.WYP[pl.ds(z0, n)] = jnp.where(last, 0.0, wyp)
    lev.WZ[pl.ds(z0, n)] = wzm
    return wzp


def lateral(lev, u, z0, n):
    sh = 2 ** lev.index
    return (
        lev.WXM[pl.ds(z0, n)] * roll(u, 1, 1)
        + lev.WXP[pl.ds(z0, n)] * roll(u, -1, 1)
        + lev.WYM[pl.ds(z0, n)] * roll(u, sh, 2)
        + lev.WYP[pl.ds(z0, n)] * roll(u, -sh, 2)
    )


def steps_of(count):
    for s in (8, 4, 2):
        if count % s == 0:
            return s
    return 1


def prepare(lev):
    Z, X, n = lev.Z, lev.X, lev.n
    zero = jnp.zeros((1, X, 128), F32)
    lev.E[0:1] = zero
    lev.E[Z + 1 : Z + 2] = zero
    loop(Z // n, lambda i: couplings(lev, i * n, n))
    lev.WZ[0:1] = zero
    lev.WZ[Z : Z + 1] = zero
    lev.A[Z : Z + 1] = zero
    s = steps_of(Z)

    def body(i, m):
        for j in range(s):
            z = i * s + j
            w = lev.WZ[z]
            a = w * m
            m = 1.0 / (lev.D[z] - w * a)
            lev.A[z] = a
            lev.M[z] = m
        return m

    lax.fori_loop(0, Z // s, body, jnp.zeros((X, 128), F32))


def sweep(lev, src, finish):
    Z, X = lev.Z, lev.X
    s = steps_of(Z)

    def forward(i, y):
        for j in range(s):
            z = i * s + j
            y = src[z] + lev.A[z] * y
            lev.Y[z] = y
        return y

    def backward(i, x):
        for j in range(s):
            z = Z - 1 - (i * s + j)
            x = lev.M[z] * lev.Y[z] + lev.A[z + 1] * x
            finish(z, x)
        return x

    lax.fori_loop(0, Z // s, forward, jnp.zeros((X, 128), F32))
    lax.fori_loop(0, Z // s, backward, jnp.zeros((X, 128), F32))


def pair_lanes(v, index):
    sh = 2 ** index
    lane = iota(v.shape, v.ndim - 1)
    other = jnp.where((lane & sh) == 0, roll(v, -sh, v.ndim - 1), roll(v, sh, v.ndim - 1))
    return v + other


def halve(v, index, tmp):
    n, X = v.shape[0], v.shape[1]
    v = v.reshape(n // 2, 2, X, 128)
    v = pair_lanes(v[:, 0] + v[:, 1], index)
    tmp[0 : n // 2, 0:X, :] = v
    return 0.125 * (tmp[0 : n // 2, pl.ds(0, X // 2, stride=2), :] + tmp[0 : n // 2, pl.ds(1, X // 2, stride=2), :])


def pre(lev):
    def finish(z, x):
        lev.U[z] = OMEGA * x

    sweep(lev, lev.F, finish)
    n = lev.n

    def body(i):
        z0 = i * n
        r = (1.0 - OMEGA) * lev.F[pl.ds(z0, n)] + lateral(lev, lev.U[pl.ds(z0, n)], z0, n)
        if lev.mask is not None:
            r = jnp.where(lev.mask[None] > 0, r, 0.0)
        lev.R[pl.ds(z0, n)] = r

    loop(lev.Z // n, body)


def post(lev):
    n, Z = lev.n, lev.Z
    zero = jnp.zeros((1, lev.X, 128), F32)
    lev.V[0:1] = zero
    lev.V[Z + 1 : Z + 2] = zero

    def body(i):
        z0 = i * n
        v = lev.V[pl.ds(z0 + 1, n)]
        around = lateral(lev, v, z0, n) + lev.WZ[pl.ds(z0, n)] * lev.V[pl.ds(z0, n)] + lev.WZ[pl.ds(z0 + 1, n)] * lev.V[pl.ds(z0 + 2, n)]
        r = lev.R[pl.ds(z0, n)] - (lev.D[pl.ds(z0, n)] * v - around)
        if lev.mask is not None:
            r = jnp.where(lev.mask[None] > 0, r, 0.0)
        lev.F[pl.ds(z0, n)] = r

    loop(Z // n, body)

    def finish(z, x):
        lev.C[z + 1] = lev.U[z] + lev.V[z + 1] + OMEGA * x

    sweep(lev, lev.F, finish)


def coarsest(lev):
    Z = lev.Z

    def first(z, x):
        lev.U[z] = OMEGA * x

    def again(z, x):
        lev.U[z] = (1.0 - OMEGA) * lev.U[z] + OMEGA * x

    def last(z, x):
        lev.C[z + 1] = (1.0 - OMEGA) * lev.U[z] + OMEGA * x

    sweep(lev, lev.F, first)

    def once(finish):
        lev.R[...] = lev.F[...] + lateral(lev, lev.U[...], 0, Z)
        sweep(lev, lev.R, finish)

    loop(SWEEPS - 2, lambda i: once(again))
    once(last)


def spread_rows(dst, z, c, rows):
    for source, count, target in rows:
        part = c[source : source + count]
        for k in range(2):
            for j in range(2):
                dst[z + k, pl.ds(target + j, count, stride=2), :] = part


def kernel(ngx, ngz, *refs):
    codes, charge, eps_t, scr_t, out = refs[:5]
    refs = list(refs[5:])

    def take(count):
        got = refs[:count]
        del refs[:count]
        return got

    l0 = Level(0, take(16), False, 4)
    l1 = Level(1, take(16), False, 8)
    l2 = Level(2, take(16), False, 8)
    l3 = Level(3, take(16), True, 4)
    l4 = Level(4, take(16), True, 4)
    l5 = Level(5, take(16), True, 4)
    l6 = Level(6, take(16), True, 2)
    (tmp, xs, xr, zs, zr, ds, dr, es, f1, red, post_red, ub, rm, ra, av, bv, es3, f3) = take(18)
    (s_r1, r_r1, s_es, r_es, s_f1, r_f1, s_red, r_red, s_post, r_post, s_e3, r_e3, s_f3, r_f3) = take(14)

    gx, gz = lax.axis_index("gx"), lax.axis_index("gz")

    def gx_at(k):
        return lax.rem(gx + (k + ngx), ngx)

    def gz_at(k):
        return lax.rem(gz + (k + ngz), ngz)

    def remote(src, dst, ss, rs, tx, tz):
        return pltpu.make_async_remote_copy(src, dst, ss, rs, device_id=(tx, tz), device_id_type=MESH)

    barrier = pltpu.get_barrier_semaphore()

    def hello(tx, tz):
        pl.semaphore_signal(barrier, 1, device_id=(tx, tz), device_id_type=MESH)

    loop(ngz - 1, lambda k: hello(gx, gz_at(k + 1)))
    loop(ngz, lambda k: hello(gx_at(1), gz_at(k)))
    loop(ngz, lambda k: hello(gx_at(-1), gz_at(k)))
    loop(ngx - 3, lambda k: hello(gx_at(k + 2), gz))

    row24, row16 = iota((24, 128), 0), iota((16, 128), 0)
    has_right, has_left = gx < ngx - 1, gx > 0
    lane = iota((1, 8, 128), 2)

    def look(i):
        c = codes[pl.ds(i, 16, stride=16), :]
        e = jnp.zeros((16, 128), F32)
        s = jnp.zeros((16, 128), F32)
        for k in range(eps_t.shape[0]):
            e = jnp.where(c == k, eps_t[k], e)
            s = jnp.where(c == k, scr_t[k], s)
        l0.E[i + 1, 0:16, :] = e
        l0.S[i, 0:16, :] = s
        l0.F[i, 0:16, :] = charge[pl.ds(i, 16, stride=16), :]

    loop(16, look)

    xs[0, :, 0:2, :] = l0.E[1:17, 14:16, :]
    xs[0, :, 2:3, :] = l0.S[:, 15:16, :]
    xs[0, :, 3:4, :] = l0.F[:, 15:16, :]
    xs[1, :, 0:2, :] = l0.E[1:17, 0:2, :]
    xs[1, :, 2:3, :] = l0.S[:, 0:1, :]
    xs[1, :, 3:4, :] = l0.F[:, 0:1, :]
    zs[0] = l0.E[16, 0:16, :]
    zs[1] = l0.E[1, 0:16, :]
    ds[0] = l0.E[16, 8:16, :]
    ds[1] = l0.E[16, 0:8, :]
    ds[2] = l0.E[1, 8:16, :]
    ds[3] = l0.E[1, 0:8, :]

    def r1_copies():
        return [
            remote(xs.at[0], xr.at[0], s_r1.at[0], r_r1.at[0], gx_at(1), gz),
            remote(xs.at[1], xr.at[1], s_r1.at[1], r_r1.at[1], gx_at(-1), gz),
            remote(zs.at[0], zr.at[0], s_r1.at[2], r_r1.at[2], gx, gz_at(1)),
            remote(zs.at[1], zr.at[1], s_r1.at[3], r_r1.at[3], gx, gz_at(-1)),
            remote(ds.at[0], dr.at[0], s_r1.at[4], r_r1.at[4], gx_at(1), gz_at(1)),
            remote(ds.at[1], dr.at[1], s_r1.at[5], r_r1.at[5], gx_at(-1), gz_at(1)),
            remote(ds.at[2], dr.at[2], s_r1.at[6], r_r1.at[6], gx_at(1), gz_at(-1)),
            remote(ds.at[3], dr.at[3], s_r1.at[7], r_r1.at[7], gx_at(-1), gz_at(-1)),
        ]

    pl.semaphore_wait(barrier, 3 * ngz - 1 + ngx - 3)
    for copy in r1_copies():
        copy.start()

    def pack2(v):
        v = v.reshape(4, 2, 8, 128)
        return jnp.where((lane & 1) == 0, v[:, 0], v[:, 1])

    es[0, gz, 0:4] = pack2(halve(l0.E[1:17, 0:16, :], 0, tmp))
    es[0, gz, 4:8] = pack2(halve(l0.S[:, 0:16, :], 0, tmp))

    def to_lines(buf, ss, rs, act):
        mine = buf.at[0, gz]

        def go(slot, k, tx):
            act(remote(mine, buf.at[slot, gz], ss.at[slot, k], rs.at[slot, gz], tx, gz_at(k)))

        loop(ngz - 1, lambda k: go(0, k + 1, gx))
        loop(ngz, lambda k: go(2, k, gx_at(1)))
        loop(ngz, lambda k: go(1, k, gx_at(-1)))

    def from_lines(buf, ss, rs):
        mine = buf.at[0, gz]

        def get(slot, k):
            p = gz_at(k)
            remote(mine, buf.at[slot, p], ss.at[slot, k], rs.at[slot, p], gx, gz_at(1)).wait_recv()

        loop(ngz - 1, lambda k: get(0, k + 1))
        loop(ngz, lambda k: get(1, k))
        loop(ngz, lambda k: get(2, k))

    to_lines(es, s_es, r_es, lambda c: c.start())

    for copy in r1_copies():
        copy.wait_recv()

    above, below = gz > 0, gz < ngz - 1
    zero16 = jnp.zeros((16, 24, 128), F32)
    l0.E[0:1] = zero16[0:1]
    l0.E[17:18] = zero16[0:1]
    l0.E[1:17, 16:24, :] = zero16[:, 0:8]
    l0.S[:, 16:24, :] = jnp.ones((16, 8, 128), F32)
    l0.F[:, 16:24, :] = zero16[:, 0:8]
    l0.E[1:17, 22:24, :] = jnp.where(has_left, xr[0, :, 0:2, :], 0.0)
    l0.S[:, 23:24, :] = jnp.where(has_left, xr[0, :, 2:3, :], 1.0)
    l0.F[:, 23:24, :] = jnp.where(has_left, xr[0, :, 3:4, :], 0.0)
    l0.E[1:17, 16:18, :] = jnp.where(has_right, xr[1, :, 0:2, :], 0.0)
    l0.S[:, 16:17, :] = jnp.where(has_right, xr[1, :, 2:3, :], 1.0)
    l0.F[:, 16:17, :] = jnp.where(has_right, xr[1, :, 3:4, :], 0.0)
    l0.E[0, 0:16, :] = jnp.where(above, zr[0], 0.0)
    l0.E[17, 0:16, :] = jnp.where(below, zr[1], 0.0)
    l0.E[0, 23:24, :] = jnp.where(above & has_left, dr[0, 7:8, :], 0.0)
    l0.E[0, 16:17, :] = jnp.where(above & has_right, dr[1, 0:1, :], 0.0)
    l0.E[17, 23:24, :] = jnp.where(below & has_left, dr[2, 7:8, :], 0.0)
    l0.E[17, 16:17, :] = jnp.where(below & has_right, dr[3, 0:1, :], 0.0)

    for i in range(4):
        wzp = couplings(l0, i * 4, 4)
    l0.WZ[16:17] = wzp[3:4]

    m = 1.0 / l0.D[0]
    l0.M[0] = m
    for z in range(1, 15):
        w = l0.WZ[z]
        a = w * m
        m = 1.0 / (l0.D[z] - w * a)
        l0.A[z] = a
        l0.M[z] = m
    lead = jnp.where(above, l0.WZ[0], 0.0)
    tail = l0.WZ[15]

    y = lead
    av[0] = y
    for z in range(1, 15):
        y = l0.A[z] * y
        av[z] = y
    x = l0.M[14] * y
    b = l0.M[14] * tail
    av[14] = x
    bv[14] = b
    for z in range(13, -1, -1):
        x = l0.M[z] * av[z] + l0.A[z + 1] * x
        b = l0.A[z + 1] * b
        av[z] = x
        bv[z] = b

    def inner(src):
        y = src[0]
        l0.Y[0] = y
        for z in range(1, 15):
            y = src[z] + l0.A[z] * y
            l0.Y[z] = y
        x = l0.M[14] * y
        l0.Y[14] = x
        for z in range(13, -1, -1):
            x = l0.M[z] * l0.Y[z] + l0.A[z + 1] * x
            l0.Y[z] = x

    inner(l0.F)

    def put(k, v):
        red[gz, pl.ds(k * 18, 17), :] = v[0:17]
        red[gz, pl.ds(k * 18 + 17, 1), :] = v[23:24]

    put(0, tail * av[14])
    put(1, l0.D[15] - tail * bv[14])
    put(2, lead * av[0])
    put(3, l0.F[15] + tail * l0.Y[14])
    put(4, lead * l0.Y[0])

    def gather(buf, ss, rs, act):
        loop(ngz - 1, lambda k: act(remote(buf.at[gz], buf.at[gz], ss.at[k + 1], rs.at[gz], gx, gz_at(k + 1))))

    def gathered(buf, ss, rs):
        def get(k):
            p = gz_at(k)
            remote(buf.at[gz], buf.at[p], ss.at[k], rs.at[p], gx, p).wait_recv()

        loop(ngz - 1, lambda k: get(k + 1))

    gather(red, s_red, r_red, lambda c: c.start())

    from_lines(es, s_es, r_es)
    mask1 = jnp.where(row24 < 8, 1.0, jnp.where(row24 < 16, jnp.where(has_right, 1.0, 0.0), jnp.where(has_left, 1.0, 0.0)))
    mask2 = jnp.where(
        row16 < 4,
        1.0,
        jnp.where(row16 < 8, jnp.where(has_right, 1.0, 0.0), jnp.where(row16 < 12, 0.0, jnp.where(has_left, 1.0, 0.0))),
    )
    l1.mask, l2.mask = mask1, mask2

    def unpack2(v):
        even = jnp.where((lane & 1) == 0, v, roll(v, 1, 2))
        odd = jnp.where((lane & 1) == 1, v, roll(v, -1, 2))
        return jnp.stack([even, odd], axis=1).reshape(2 * v.shape[0], 8, 128)

    here = (None, has_right, has_left)

    def place(buf, start, dst, offset, outside):
        for slot in range(3):

            def body(p, slot=slot):
                v = unpack2(buf[slot, p, start : start + 4])
                if slot:
                    v = jnp.where(here[slot], v, outside)
                dst[pl.ds(p * 8 + offset, 8), slot * 8 : slot * 8 + 8, :] = v

            loop(ngz, body)

    place(es, 0, l1.E, 1, 0.0)
    place(es, 4, l1.S, 0, 1.0)

    def coarsen(src, offset, fine, coarse, dst, dst_offset, split):
        n = fine.n

        def body(i):
            v = halve(src[pl.ds(i * n + offset, n)], fine.index, tmp)
            at = pl.ds(i * (n // 2) + dst_offset, n // 2)
            if split:
                dst[at, 0:8, :] = v[:, 0:8]
                dst[at, 12:16, :] = v[:, 8:12]
            else:
                dst[at] = v

        loop(fine.Z // n, body)

    def filler(ref, value):
        ref[:, 8:12, :] = jnp.full((ref.shape[0], 4, 128), value, F32)

    filler(l2.E, 0.0)
    filler(l2.S, 1.0)
    filler(l2.F, 0.0)
    coarsen(l1.E, 1, l1, l2, l2.E, 1, True)
    coarsen(l1.S, 0, l1, l2, l2.S, 0, True)

    lane3 = iota((4, 2, 128), 2)

    def pack4(src, offset, buf, first):
        for i in range(2):
            v = halve(src[i * 16 + offset : i * 16 + offset + 16], 2, tmp)[:, 0:2]
            tmp[i * 8 : i * 8 + 8, 32:34, :] = v
        v = tmp[0:16, 32:34, :].reshape(4, 4, 2, 128)
        k = (lane3 >> 1) & 3
        v = jnp.where(k == 0, v[:, 0], jnp.where(k == 1, v[:, 1], jnp.where(k == 2, v[:, 2], v[:, 3])))
        for zz in range(4):
            buf[gx, first + zz * 2 : first + zz * 2 + 2, :] = v[zz]

    pack4(l2.E, 1, es3, 0)
    pack4(l2.S, 0, es3, 8)

    def spread(buf, ss, rs, act):
        loop(ngx - 1, lambda k: act(remote(buf.at[gx], buf.at[gx], ss.at[k + 1], rs.at[gx], gx_at(k + 1), gz)))

    def collected(buf, ss, rs):
        def get(k):
            p = gx_at(k)
            remote(buf.at[gx], buf.at[p], ss.at[k], rs.at[p], p, gz).wait_recv()

        loop(ngx - 1, lambda k: get(k + 1))

    spread(es3, s_e3, r_e3, lambda c: c.start())

    gathered(red, s_red, r_red)

    def got(p, k):
        return red[p, pl.ds(k * 18, 18), :]

    m, y = None, None
    for p in range(ngz):
        diag, right = got(p, 1), got(p, 3)
        if p + 1 < ngz:
            diag, right = diag - got(p + 1, 2), right + got(p + 1, 4)
        if p:
            c = got(p, 0)
            a = c * m
            diag, right = diag - c * a, right + a * y
            ra[p] = a
        m, y = 1.0 / diag, right
        rm[p] = m
        ub[p + 1, 0:18, :] = y
    x = m * y
    for p in range(ngz - 1, -1, -1):
        if p + 1 < ngz:
            x = rm[p] * ub[p + 1, 0:18, :] + ra[p + 1] * x
        ub[p + 1, 0:17, :] = x[0:17]
        ub[p + 1, 23:24, :] = x[17:18]
        ub[p + 1, 17:23, :] = jnp.zeros((6, 128), F32)
    ub[0] = jnp.zeros((24, 128), F32)

    before, own = ub[gz], ub[gz + 1]
    for z in range(15):
        l0.U[z] = OMEGA * (l0.Y[z] + av[z] * before + bv[z] * own)
    l0.U[15] = OMEGA * own

    def first_residual(i):
        z0 = i * 4
        l0.R[pl.ds(z0, 4)] = (1.0 - OMEGA) * l0.F[pl.ds(z0, 4)] + lateral(l0, l0.U[pl.ds(z0, 4)], z0, 4)

    loop(4, first_residual)
    f1[0, gz] = pack2(halve(l0.R[:, 0:16, :], 0, tmp))
    to_lines(f1, s_f1, r_f1, lambda c: c.start())

    prepare(l1)
    prepare(l2)

    lane32 = iota((32, 128), 1)

    def swap(v, s):
        return jnp.where((lane32 & s) == 0, roll(v, -s, 1), roll(v, s, 1))

    def place4(buf, rows, first, dst, offset):
        for zz in range(4):
            for xp in range(2):
                v = buf[:, first + zz * 2 + xp, :]
                w = swap(v, 2)
                for k0 in range(2):
                    v1 = jnp.where(((lane32 >> 1) & 1) == k0, v, w)
                    w1 = swap(v1, 4)
                    for k1 in range(2):
                        v2 = jnp.where(((lane32 >> 2) & 1) == k1, v1, w1)
                        dst[offset + zz * 4 + k1 * 2 + k0, pl.ds(xp, ngx, stride=2), :] = v2

    from_lines(f1, s_f1, r_f1)
    place(f1, 0, l1.F, 0, 0.0)
    pre(l1)
    coarsen(l1.R, 0, l1, l2, l2.F, 0, True)
    pre(l2)
    pack4(l2.R, 0, f3, 0)
    spread(f3, s_f3, r_f3, lambda c: c.start())

    collected(es3, s_e3, r_e3)
    place4(es3, 16, 0, l3.E, 1)
    place4(es3, 16, 8, l3.S, 0)
    deep = [l3, l4, l5, l6]
    for fine, coarse in zip(deep[:-1], deep[1:]):
        coarsen(fine.E, 1, fine, coarse, coarse.E, 1, False)
        coarsen(fine.S, 0, fine, coarse, coarse.S, 0, False)
    for lev in deep:
        prepare(lev)

    collected(f3, s_f3, r_f3)
    place4(f3, 8, 0, l3.F, 0)
    for fine, coarse in zip(deep[:-1], deep[1:]):
        pre(fine)
        coarsen(fine.R, 0, fine, coarse, coarse.F, 0, False)
    coarsest(l6)
    for fine, coarse in zip(deep[-2::-1], deep[:0:-1]):
        loop(coarse.Z, lambda z, fine=fine, coarse=coarse: spread_rows(fine.V, 2 * z + 1, coarse.C[z + 1], ((0, coarse.X, 0),)))
        post(fine)

    def down3(z):
        c = pltpu.roll(l3.C[z + 1], lax.rem(2 * (ngx - gx), 2 * ngx), 0)
        spread_rows(l2.V, 2 * z + 1, c, ((0, 4, 0), (62, 2, 12)))

    filler(l2.V, 0.0)
    loop(l3.Z, down3)

    def clear(i):
        l2.V[i + 1] = jnp.where(mask2 > 0, l2.V[i + 1], 0.0)

    loop(l2.Z, clear)
    post(l2)
    loop(l2.Z, lambda z: spread_rows(l1.V, 2 * z + 1, l2.C[z + 1], ((0, 4, 0), (4, 4, 8), (12, 4, 16))))
    post(l1)
    l1.C[0] = jnp.zeros((24, 128), F32)
    l1.C[l1.Z + 1] = jnp.zeros((24, 128), F32)

    for i in range(10):
        c = l1.C[gz * 8 + i]
        for z in (2 * i - 1, 2 * i):
            if 0 <= z < 18:
                for j in range(2):
                    l0.V[z, pl.ds(j, 8, stride=2), :] = c[0:8]
                l0.V[z, 16:17, :] = c[8:9]
                l0.V[z, 17:23, :] = jnp.zeros((6, 128), F32)
                l0.V[z, 23:24, :] = c[23:24]

    def second_residual(i):
        z0 = i * 4
        v = l0.V[pl.ds(z0 + 1, 4)]
        around = lateral(l0, v, z0, 4) + l0.WZ[pl.ds(z0, 4)] * l0.V[pl.ds(z0, 4)] + l0.WZ[pl.ds(z0 + 1, 4)] * l0.V[pl.ds(z0 + 2, 4)]
        l0.F[pl.ds(z0, 4)] = l0.R[pl.ds(z0, 4)] - (l0.D[pl.ds(z0, 4)] * v - around)

    loop(4, second_residual)
    inner(l0.F)
    post_red[gz, 0:16, :] = (l0.F[15] + tail * l0.Y[14])[0:16]
    post_red[gz, 16:32, :] = (lead * l0.Y[0])[0:16]
    gather(post_red, s_post, r_post, lambda c: c.start())
    gathered(post_red, s_post, r_post)
    y = None
    for p in range(ngz):
        right = post_red[p, 0:16, :]
        if p + 1 < ngz:
            right = right + post_red[p + 1, 16:32, :]
        if p:
            right = right + ra[p, 0:16, :] * y
        y = right
        ub[p + 1, 0:16, :] = y
    x = rm[ngz - 1, 0:16, :] * y
    for p in range(ngz - 1, -1, -1):
        if p + 1 < ngz:
            x = rm[p, 0:16, :] * ub[p + 1, 0:16, :] + ra[p + 1, 0:16, :] * x
        ub[p + 1, 0:16, :] = x
    before, own = ub[gz, 0:16, :], ub[gz + 1, 0:16, :]
    for z in range(16):
        if z < 15:
            x = l0.Y[z, 0:16, :] + av[z, 0:16, :] * before + bv[z, 0:16, :] * own
        else:
            x = own
        out[pl.ds(z, 16, stride=16), :] = l0.U[z, 0:16, :] + l0.V[z + 1, 0:16, :] + OMEGA * x

    for copy in r1_copies():
        copy.wait_send()
    to_lines(es, s_es, r_es, lambda c: c.wait_send())
    to_lines(f1, s_f1, r_f1, lambda c: c.wait_send())
    gather(red, s_red, r_red, lambda c: c.wait_send())
    gather(post_red, s_post, r_post, lambda c: c.wait_send())
    spread(es3, s_e3, r_e3, lambda c: c.wait_send())
    spread(f3, s_f3, r_f3, lambda c: c.wait_send())


def solution(mesh):
    ngx, ngz = mesh.shape["gx"], mesh.shape["gz"]

    def per_device(charge, codes, eps_table, screen_table):
        nx, nz, ny = charge.shape
        whole_z, whole_x = nz * ngz, nx * ngx
        levels = [
            (nz, 24),
            (whole_z // 2, 24),
            (whole_z // 4, 16),
            (whole_z // 8, whole_x // 8),
            (whole_z // 16, whole_x // 16),
            (whole_z // 32, whole_x // 32),
            (whole_z // 64, whole_x // 64),
        ]
        scratch = []
        for Z, X in levels:
            scratch += Level.scratch(Z, X)
        vm = lambda *shape: pltpu.VMEM(shape, F32)
        scratch += [
            vm(16, 64, 128),
            vm(2, 16, 4, 128),
            vm(2, 16, 4, 128),
            vm(2, 16, 128),
            vm(2, 16, 128),
            vm(4, 8, 128),
            vm(4, 8, 128),
            vm(3, ngz, 8, 8, 128),
            vm(3, ngz, 4, 8, 128),
            vm(ngz, 96, 128),
            vm(ngz, 32, 128),
            vm(ngz + 1, 24, 128),
            vm(ngz, 18, 128),
            vm(ngz, 18, 128),
            vm(16, 24, 128),
            vm(16, 24, 128),
            vm(ngx, 16, 128),
            vm(ngx, 8, 128),
        ]
        for shape in ((8,), (3, ngz), (3, ngz), (ngz,), (ngz,), (ngx,), (ngx,)):
            scratch += [pltpu.SemaphoreType.DMA(shape)] * 2
        result = pl.pallas_call(
            lambda *refs: kernel(ngx, ngz, *refs),
            out_shape=jax.ShapeDtypeStruct((nx * nz, ny), F32),
            in_specs=[
                pl.BlockSpec(memory_space=pltpu.VMEM),
                pl.BlockSpec(memory_space=pltpu.VMEM),
                pl.BlockSpec(memory_space=pltpu.SMEM),
                pl.BlockSpec(memory_space=pltpu.SMEM),
            ],
            out_specs=pl.BlockSpec(memory_space=pltpu.VMEM),
            scratch_shapes=scratch,
            compiler_params=pltpu.CompilerParams(collective_id=0, has_side_effects=True, vmem_limit_bytes=56 << 20),
            name="vcycle",
        )(codes.reshape(nx * nz, ny), charge.reshape(nx * nz, ny), eps_table, screen_table)
        return result.reshape(nx, nz, ny)

    return jax.shard_map(
        per_device,
        mesh=mesh,
        in_specs=(P("gx", "gz", None), P("gx", "gz", None), P(), P()),
        out_specs=P("gx", "gz", None),
        check_vma=False,
    )
```

```python
import jax
import jax.numpy as jnp
from jax import lax
from jax.experimental import pallas as pl
from jax.experimental.pallas import tpu as pltpu
from jax.sharding import PartitionSpec as P

OMEGA = 0.8
SWEEPS = 8
LAST = 6
F32 = jnp.float32
MESH = pl.DeviceIdType.MESH


def iota(shape, dim):
    return lax.broadcasted_iota(jnp.int32, shape, dim)


def roll(v, shift, axis):
    size = v.shape[axis]
    return pltpu.roll(v, shift % size, axis)


class Level:
    def __init__(self, index, refs, whole, slab):
        (self.E, self.S, self.WXM, self.WXP, self.WYM, self.WYP, self.WZ, self.D, self.A, self.M, self.F, self.U, self.R, self.Y,
         self.V, self.C) = refs
        self.index, self.whole, self.n = index, whole, slab
        self.Z, self.X = self.S.shape[0], self.S.shape[1]
        self.mask = None

    @staticmethod
    def scratch(Z, X):
        sizes = (Z + 2, Z, Z, Z, Z, Z, Z + 1, Z, Z + 1, Z, Z, Z, Z, Z, Z + 2, Z + 2)
        return [pltpu.VMEM((s, X, 128), F32) for s in sizes]


def loop(count, body):
    def step(i, carry):
        body(i)
        return carry

    lax.fori_loop(0, count, step, 0)


def unrolled(count, body):
    for i in range(count):
        body(i)


def couplings(lev, z0, n):
    h = 0.5 ** lev.index * 0.5
    sh = 2 ** lev.index
    X = lev.X
    e = lev.E[pl.ds(z0 + 1, n)]
    lane = iota((n, X, 128), 2)
    first, last = lane < sh, lane >= 128 - sh
    up, down = roll(e, 1, 1), roll(e, -1, 1)
    if lev.whole:
        row = iota((n, X, 128), 1)
        up, down = jnp.where(row == 0, 0.0, up), jnp.where(row == X - 1, 0.0, down)
    left, right = jnp.where(first, 0.0, roll(e, sh, 2)), jnp.where(last, 0.0, roll(e, -sh, 2))
    wxm, wxp, wym, wyp = h * (e + up), h * (e + down), h * (e + left), h * (e + right)
    wzm, wzp = h * (e + lev.E[pl.ds(z0, n)]), h * (e + lev.E[pl.ds(z0 + 2, n)])
    lev.D[pl.ds(z0, n)] = wxm + wxp + wzm + wzp + wym + wyp + lev.S[pl.ds(z0, n)]
    if lev.whole:
        wxm, wxp = jnp.where(row == 0, 0.0, wxm), jnp.where(row == X - 1, 0.0, wxp)
    lev.WXM[pl.ds(z0, n)] = wxm
    lev.WXP[pl.ds(z0, n)] = wxp
    lev.WYM[pl.ds(z0, n)] = jnp.where(first, 0.0, wym)
    lev.WYP[pl.ds(z0, n)] = jnp.where(last, 0.0, wyp)
    lev.WZ[pl.ds(z0, n)] = wzm
    return wzp


def lateral(lev, u, z0, n):
    sh = 2 ** lev.index
    return (
        lev.WXM[pl.ds(z0, n)] * roll(u, 1, 1)
        + lev.WXP[pl.ds(z0, n)] * roll(u, -1, 1)
        + lev.WYM[pl.ds(z0, n)] * roll(u, sh, 2)
        + lev.WYP[pl.ds(z0, n)] * roll(u, -sh, 2)
    )


def steps_of(count):
    for s in (8, 4, 2):
        if count % s == 0:
            return s
    return 1


def prepare(lev):
    Z, X, n = lev.Z, lev.X, lev.n
    zero = jnp.zeros((1, X, 128), F32)
    lev.E[0:1] = zero
    lev.E[Z + 1 : Z + 2] = zero
    (loop if Z // n > 8 else unrolled)(Z // n, lambda i: couplings(lev, i * n, n))
    lev.WZ[0:1] = zero
    lev.WZ[Z : Z + 1] = zero
    lev.A[Z : Z + 1] = zero
    s = steps_of(Z)

    def body(i, m):
        for j in range(s):
            z = i * s + j
            w = lev.WZ[z]
            a = w * m
            m = 1.0 / (lev.D[z] - w * a)
            lev.A[z] = a
            lev.M[z] = m
        return m

    lax.fori_loop(0, Z // s, body, jnp.zeros((X, 128), F32))


def sweep(lev, src, finish):
    Z, X = lev.Z, lev.X
    s = steps_of(Z)

    def forward(i, y):
        for j in range(s):
            z = i * s + j
            y = src[z] + lev.A[z] * y
            lev.Y[z] = y
        return y

    def backward(i, x):
        for j in range(s):
            z = Z - 1 - (i * s + j)
            x = lev.M[z] * lev.Y[z] + lev.A[z + 1] * x
            finish(z, x)
        return x

    lax.fori_loop(0, Z // s, forward, jnp.zeros((X, 128), F32))
    lax.fori_loop(0, Z // s, backward, jnp.zeros((X, 128), F32))


def pair_lanes(v, index):
    sh = 2 ** index
    lane = iota(v.shape, v.ndim - 1)
    other = jnp.where((lane & sh) == 0, roll(v, -sh, v.ndim - 1), roll(v, sh, v.ndim - 1))
    return v + other


def halve(v, index, tmp, at=0):
    n, X = v.shape[0], v.shape[1]
    v = v.reshape(n // 2, 2, X, 128)
    v = pair_lanes(v[:, 0] + v[:, 1], index)
    part = slice(at, at + n // 2)
    tmp[part, 0:X, :] = v
    return 0.125 * (tmp[part, pl.ds(0, X // 2, stride=2), :] + tmp[part, pl.ds(1, X // 2, stride=2), :])


def pre(lev):
    def finish(z, x):
        lev.U[z] = OMEGA * x

    sweep(lev, lev.F, finish)
    n = lev.n

    def body(i):
        z0 = i * n
        r = (1.0 - OMEGA) * lev.F[pl.ds(z0, n)] + lateral(lev, lev.U[pl.ds(z0, n)], z0, n)
        if lev.mask is not None:
            r = jnp.where(lev.mask[None] > 0, r, 0.0)
        lev.R[pl.ds(z0, n)] = r

    unrolled(lev.Z // n, body)


def post(lev):
    n, Z = lev.n, lev.Z
    zero = jnp.zeros((1, lev.X, 128), F32)
    lev.V[0:1] = zero
    lev.V[Z + 1 : Z + 2] = zero

    def body(i):
        z0 = i * n
        v = lev.V[pl.ds(z0 + 1, n)]
        around = lateral(lev, v, z0, n) + lev.WZ[pl.ds(z0, n)] * lev.V[pl.ds(z0, n)] + lev.WZ[pl.ds(z0 + 1, n)] * lev.V[pl.ds(z0 + 2, n)]
        r = lev.R[pl.ds(z0, n)] - (lev.D[pl.ds(z0, n)] * v - around)
        if lev.mask is not None:
            r = jnp.where(lev.mask[None] > 0, r, 0.0)
        lev.F[pl.ds(z0, n)] = r

    unrolled(Z // n, body)

    def finish(z, x):
        lev.C[z + 1] = lev.U[z] + lev.V[z + 1] + OMEGA * x

    sweep(lev, lev.F, finish)


def coarsest(lev):
    Z = lev.Z

    def first(z, x):
        lev.U[z] = OMEGA * x

    def again(z, x):
        lev.U[z] = (1.0 - OMEGA) * lev.U[z] + OMEGA * x

    def last(z, x):
        lev.C[z + 1] = (1.0 - OMEGA) * lev.U[z] + OMEGA * x

    sweep(lev, lev.F, first)

    def once(finish):
        lev.R[...] = lev.F[...] + lateral(lev, lev.U[...], 0, Z)
        sweep(lev, lev.R, finish)

    loop(SWEEPS - 2, lambda i: once(again))
    once(last)


def spread_rows(dst, z, c, rows):
    for source, count, target in rows:
        part = c[source : source + count]
        for k in range(2):
            for j in range(2):
                dst[z + k, pl.ds(target + j, count, stride=2), :] = part


def kernel(ngx, ngz, *refs):
    codes_in, charge_in, eps_t, scr_t, out = refs[:5]
    refs = list(refs[5:])

    def take(count):
        got = refs[:count]
        del refs[:count]
        return got

    l0 = Level(0, take(16), False, 4)
    l1 = Level(1, take(16), False, 8)
    l2 = Level(2, take(16), False, 8)
    l3 = Level(3, take(16), True, 4)
    l4 = Level(4, take(16), True, 4)
    l5 = Level(5, take(16), True, 4)
    l6 = Level(6, take(16), True, 2)
    (tmp, codes, charge, s_in, xs, xr, zs, zr, ds, dr, es, f1, red, post_red, ub, rm, ra, av, bv, es3, f3) = take(21)
    (s_r1, r_r1, s_es, r_es, s_f1, r_f1, s_red, r_red, s_post, r_post, s_e3, r_e3, s_f3, r_f3) = take(14)

    gx, gz = lax.axis_index("gx"), lax.axis_index("gz")

    def gx_at(k):
        return lax.rem(gx + (k + ngx), ngx)

    def gz_at(k):
        return lax.rem(gz + (k + ngz), ngz)

    def remote(src, dst, ss, rs, tx, tz):
        return pltpu.make_async_remote_copy(src, dst, ss, rs, device_id=(tx, tz), device_id_type=MESH)

    inputs = (pltpu.make_async_copy(codes_in, codes, s_in.at[0]), pltpu.make_async_copy(charge_in, charge, s_in.at[1]))
    for copy in inputs:
        copy.start()

    barrier = pltpu.get_barrier_semaphore()

    def hello(tx, tz):
        pl.semaphore_signal(barrier, 1, device_id=(tx, tz), device_id_type=MESH)

    loop(ngz - 1, lambda k: hello(gx, gz_at(k + 1)))
    loop(ngz, lambda k: hello(gx_at(1), gz_at(k)))
    loop(ngz, lambda k: hello(gx_at(-1), gz_at(k)))
    loop(ngx - 3, lambda k: hello(gx_at(k + 2), gz))

    row24, row16 = iota((24, 128), 0), iota((16, 128), 0)
    has_right, has_left = gx < ngx - 1, gx > 0
    lane = iota((1, 8, 128), 2)

    table_e = [jnp.full((16, 128), eps_t[k], F32) for k in range(eps_t.shape[0])]
    table_s = [jnp.full((16, 128), scr_t[k], F32) for k in range(eps_t.shape[0])]

    def look(i):
        c = codes[pl.ds(i, 16, stride=16), :]
        e = jnp.zeros((16, 128), F32)
        s = jnp.zeros((16, 128), F32)
        for k in range(eps_t.shape[0]):
            e = jnp.where(c == k, table_e[k], e)
            s = jnp.where(c == k, table_s[k], s)
        l0.E[i + 1, 0:16, :] = e
        l0.S[i, 0:16, :] = s
        l0.F[i, 0:16, :] = charge[pl.ds(i, 16, stride=16), :]

    for copy in inputs:
        copy.wait()
    unrolled(16, look)

    xs[0, :, 0:2, :] = l0.E[1:17, 14:16, :]
    xs[0, :, 2:3, :] = l0.S[:, 15:16, :]
    xs[0, :, 3:4, :] = l0.F[:, 15:16, :]
    xs[1, :, 0:2, :] = l0.E[1:17, 0:2, :]
    xs[1, :, 2:3, :] = l0.S[:, 0:1, :]
    xs[1, :, 3:4, :] = l0.F[:, 0:1, :]
    zs[0] = l0.E[16, 0:16, :]
    zs[1] = l0.E[1, 0:16, :]
    ds[0] = l0.E[16, 8:16, :]
    ds[1] = l0.E[16, 0:8, :]
    ds[2] = l0.E[1, 8:16, :]
    ds[3] = l0.E[1, 0:8, :]

    def r1_copies():
        return [
            remote(xs.at[0], xr.at[0], s_r1.at[0], r_r1.at[0], gx_at(1), gz),
            remote(xs.at[1], xr.at[1], s_r1.at[1], r_r1.at[1], gx_at(-1), gz),
            remote(zs.at[0], zr.at[0], s_r1.at[2], r_r1.at[2], gx, gz_at(1)),
            remote(zs.at[1], zr.at[1], s_r1.at[3], r_r1.at[3], gx, gz_at(-1)),
            remote(ds.at[0], dr.at[0], s_r1.at[4], r_r1.at[4], gx_at(1), gz_at(1)),
            remote(ds.at[1], dr.at[1], s_r1.at[5], r_r1.at[5], gx_at(-1), gz_at(1)),
            remote(ds.at[2], dr.at[2], s_r1.at[6], r_r1.at[6], gx_at(1), gz_at(-1)),
            remote(ds.at[3], dr.at[3], s_r1.at[7], r_r1.at[7], gx_at(-1), gz_at(-1)),
        ]

    pl.semaphore_wait(barrier, 3 * ngz - 1 + ngx - 3)
    for copy in r1_copies():
        copy.start()

    def pack2(v):
        v = v.reshape(4, 2, 8, 128)
        return jnp.where((lane & 1) == 0, v[:, 0], v[:, 1])

    es[0, gz, 0:4] = pack2(halve(l0.E[1:17, 0:16, :], 0, tmp))
    es[0, gz, 4:8] = pack2(halve(l0.S[:, 0:16, :], 0, tmp, 8))

    def to_lines(buf, ss, rs, act):
        mine = buf.at[0, gz]

        def go(slot, k, tx):
            act(remote(mine, buf.at[slot, gz], ss.at[slot, k], rs.at[slot, gz], tx, gz_at(k)))

        loop(ngz - 1, lambda k: go(0, k + 1, gx))
        loop(ngz, lambda k: go(2, k, gx_at(1)))
        loop(ngz, lambda k: go(1, k, gx_at(-1)))

    def from_lines(buf, ss, rs):
        mine = buf.at[0, gz]

        def get(slot, k):
            p = gz_at(k)
            remote(mine, buf.at[slot, p], ss.at[slot, k], rs.at[slot, p], gx, gz_at(1)).wait_recv()

        loop(ngz - 1, lambda k: get(0, k + 1))
        loop(ngz, lambda k: get(1, k))
        loop(ngz, lambda k: get(2, k))

    def es_lines(act):
        loop(ngz - 1, lambda k: act(remote(es.at[0, gz], es.at[0, gz], s_es.at[0, k + 1], r_es.at[0, gz], gx, gz_at(k + 1))))

    def es_planes():
        return [
            remote(es.at[0], es.at[2], s_es.at[2, 0], r_es.at[2, 0], gx_at(1), gz),
            remote(es.at[0], es.at[1], s_es.at[1, 0], r_es.at[1, 0], gx_at(-1), gz),
        ]

    es_lines(lambda c: c.start())

    for copy in r1_copies():
        copy.wait_recv()

    above, below = gz > 0, gz < ngz - 1
    zero16 = jnp.zeros((16, 24, 128), F32)
    l0.E[0:1] = zero16[0:1]
    l0.E[17:18] = zero16[0:1]
    l0.E[1:17, 16:24, :] = zero16[:, 0:8]
    l0.S[:, 16:24, :] = jnp.ones((16, 8, 128), F32)
    l0.F[:, 16:24, :] = zero16[:, 0:8]
    l0.E[1:17, 22:24, :] = jnp.where(has_left, xr[0, :, 0:2, :], 0.0)
    l0.S[:, 23:24, :] = jnp.where(has_left, xr[0, :, 2:3, :], 1.0)
    l0.F[:, 23:24, :] = jnp.where(has_left, xr[0, :, 3:4, :], 0.0)
    l0.E[1:17, 16:18, :] = jnp.where(has_right, xr[1, :, 0:2, :], 0.0)
    l0.S[:, 16:17, :] = jnp.where(has_right, xr[1, :, 2:3, :], 1.0)
    l0.F[:, 16:17, :] = jnp.where(has_right, xr[1, :, 3:4, :], 0.0)
    l0.E[0, 0:16, :] = jnp.where(above, zr[0], 0.0)
    l0.E[17, 0:16, :] = jnp.where(below, zr[1], 0.0)
    l0.E[0, 23:24, :] = jnp.where(above & has_left, dr[0, 7:8, :], 0.0)
    l0.E[0, 16:17, :] = jnp.where(above & has_right, dr[1, 0:1, :], 0.0)
    l0.E[17, 23:24, :] = jnp.where(below & has_left, dr[2, 7:8, :], 0.0)
    l0.E[17, 16:17, :] = jnp.where(below & has_right, dr[3, 0:1, :], 0.0)

    for i in range(4):
        wzp = couplings(l0, i * 4, 4)
    l0.WZ[16:17] = wzp[3:4]

    m = 1.0 / l0.D[0]
    l0.M[0] = m
    for z in range(1, 15):
        w = l0.WZ[z]
        a = w * m
        m = 1.0 / (l0.D[z] - w * a)
        l0.A[z] = a
        l0.M[z] = m
    lead = jnp.where(above, l0.WZ[0], 0.0)
    tail = l0.WZ[15]

    y = lead
    av[0] = y
    for z in range(1, 15):
        y = l0.A[z] * y
        av[z] = y
    x = l0.M[14] * y
    b = l0.M[14] * tail
    av[14] = x
    bv[14] = b
    for z in range(13, -1, -1):
        x = l0.M[z] * av[z] + l0.A[z + 1] * x
        b = l0.A[z + 1] * b
        av[z] = x
        bv[z] = b

    def inner(src):
        y = src[0]
        l0.Y[0] = y
        for z in range(1, 15):
            y = src[z] + l0.A[z] * y
            l0.Y[z] = y
        x = l0.M[14] * y
        l0.Y[14] = x
        for z in range(13, -1, -1):
            x = l0.M[z] * l0.Y[z] + l0.A[z + 1] * x
            l0.Y[z] = x

    inner(l0.F)

    def put(k, v):
        red[gz, pl.ds(k * 18, 17), :] = v[0:17]
        red[gz, pl.ds(k * 18 + 17, 1), :] = v[23:24]

    put(0, tail * av[14])
    put(1, l0.D[15] - tail * bv[14])
    put(2, lead * av[0])
    put(3, l0.F[15] + tail * l0.Y[14])
    put(4, lead * l0.Y[0])

    def gather(buf, ss, rs, act):
        loop(ngz - 1, lambda k: act(remote(buf.at[gz], buf.at[gz], ss.at[k + 1], rs.at[gz], gx, gz_at(k + 1))))

    def gathered(buf, ss, rs):
        def get(k):
            p = gz_at(k)
            remote(buf.at[gz], buf.at[p], ss.at[k], rs.at[p], gx, p).wait_recv()

        loop(ngz - 1, lambda k: get(k + 1))

    gather(red, s_red, r_red, lambda c: c.start())

    def es_line_in(k):
        p = gz_at(k + 1)
        remote(es.at[0, gz], es.at[0, p], s_es.at[0, k + 1], r_es.at[0, p], gx, p).wait_recv()

    loop(ngz - 1, es_line_in)
    for copy in es_planes():
        copy.start()

    mask1 = jnp.where(row24 < 8, 1.0, jnp.where(row24 < 16, jnp.where(has_right, 1.0, 0.0), jnp.where(has_left, 1.0, 0.0)))
    mask2 = jnp.where(
        row16 < 4,
        1.0,
        jnp.where(row16 < 8, jnp.where(has_right, 1.0, 0.0), jnp.where(row16 < 12, 0.0, jnp.where(has_left, 1.0, 0.0))),
    )
    l1.mask, l2.mask = mask1, mask2

    def unpack2(v):
        even = jnp.where((lane & 1) == 0, v, roll(v, 1, 2))
        odd = jnp.where((lane & 1) == 1, v, roll(v, -1, 2))
        return jnp.stack([even, odd], axis=1).reshape(2 * v.shape[0], 8, 128)

    here = (None, has_right, has_left)

    def place(buf, start, dst, offset, outside, slots):
        for slot in slots:
            for p in range(ngz):
                v = unpack2(buf[slot, p, start : start + 4])
                if slot:
                    v = jnp.where(here[slot], v, outside)
                dst[p * 8 + offset : p * 8 + offset + 8, slot * 8 : slot * 8 + 8, :] = v

    place(es, 0, l1.E, 1, 0.0, (0,))
    place(es, 4, l1.S, 0, 1.0, (0,))

    def coarsen(src, offset, fine, coarse, dst, dst_offset, split):
        n = fine.n

        def body(i):
            v = halve(src[i * n + offset : (i + 1) * n + offset], fine.index, tmp, i * (n // 2))
            at = slice(i * (n // 2) + dst_offset, (i + 1) * (n // 2) + dst_offset)
            if split:
                dst[at, 0:8, :] = v[:, 0:8]
                dst[at, 12:16, :] = v[:, 8:12]
            else:
                dst[at] = v

        unrolled(fine.Z // n, body)

    def filler(ref, value):
        ref[:, 8:12, :] = jnp.full((ref.shape[0], 4, 128), value, F32)

    filler(l2.E, 0.0)
    filler(l2.S, 1.0)
    filler(l2.F, 0.0)

    lane3 = iota((4, 2, 128), 2)

    def pack4(src, offset, buf, first):
        for i in range(2):
            v = halve(src[i * 16 + offset : i * 16 + offset + 16], 2, tmp, i * 8)[:, 0:2]
            tmp[i * 8 : i * 8 + 8, 32:34, :] = v
        v = tmp[0:16, 32:34, :].reshape(4, 4, 2, 128)
        k = (lane3 >> 1) & 3
        v = jnp.where(k == 0, v[:, 0], jnp.where(k == 1, v[:, 1], jnp.where(k == 2, v[:, 2], v[:, 3])))
        for zz in range(4):
            buf[gx, first + zz * 2 : first + zz * 2 + 2, :] = v[zz]

    def spread(buf, ss, rs, act):
        loop(ngx - 1, lambda k: act(remote(buf.at[gx], buf.at[gx], ss.at[k + 1], rs.at[gx], gx_at(k + 1), gz)))

    def collected(buf, ss, rs):
        def get(k):
            p = gx_at(k)
            remote(buf.at[gx], buf.at[p], ss.at[k], rs.at[p], p, gz).wait_recv()

        loop(ngx - 1, lambda k: get(k + 1))

    gathered(red, s_red, r_red)

    def got(p, k):
        return red[p, pl.ds(k * 18, 18), :]

    m, y = None, None
    for p in range(ngz):
        diag, right = got(p, 1), got(p, 3)
        if p + 1 < ngz:
            diag, right = diag - got(p + 1, 2), right + got(p + 1, 4)
        if p:
            c = got(p, 0)
            a = c * m
            diag, right = diag - c * a, right + a * y
            ra[p] = a
        m, y = 1.0 / diag, right
        rm[p] = m
        ub[p + 1, 0:18, :] = y
    x = m * y
    for p in range(ngz - 1, -1, -1):
        if p + 1 < ngz:
            x = rm[p] * ub[p + 1, 0:18, :] + ra[p + 1] * x
        ub[p + 1, 0:17, :] = x[0:17]
        ub[p + 1, 23:24, :] = x[17:18]
        ub[p + 1, 17:23, :] = jnp.zeros((6, 128), F32)
    ub[0] = jnp.zeros((24, 128), F32)

    before, own = ub[gz], ub[gz + 1]
    for z in range(15):
        l0.U[z] = OMEGA * (l0.Y[z] + av[z] * before + bv[z] * own)
    l0.U[15] = OMEGA * own

    def first_residual(i):
        z0 = i * 4
        l0.R[pl.ds(z0, 4)] = (1.0 - OMEGA) * l0.F[pl.ds(z0, 4)] + lateral(l0, l0.U[pl.ds(z0, 4)], z0, 4)

    unrolled(4, first_residual)
    f1[0, gz] = pack2(halve(l0.R[:, 0:16, :], 0, tmp))
    to_lines(f1, s_f1, r_f1, lambda c: c.start())

    for copy in es_planes():
        copy.wait_recv()
    place(es, 0, l1.E, 1, 0.0, (1, 2))
    place(es, 4, l1.S, 0, 1.0, (1, 2))
    coarsen(l1.E, 1, l1, l2, l2.E, 1, True)
    coarsen(l1.S, 0, l1, l2, l2.S, 0, True)
    pack4(l2.E, 1, es3, 0)
    pack4(l2.S, 0, es3, 8)
    spread(es3, s_e3, r_e3, lambda c: c.start())
    prepare(l1)
    prepare(l2)

    lane32 = iota((32, 128), 1)

    def swap(v, s):
        return jnp.where((lane32 & s) == 0, roll(v, -s, 1), roll(v, s, 1))

    def place4(buf, rows, first, dst, offset):
        for zz in range(4):
            for xp in range(2):
                v = buf[:, first + zz * 2 + xp, :]
                w = swap(v, 2)
                for k0 in range(2):
                    v1 = jnp.where(((lane32 >> 1) & 1) == k0, v, w)
                    w1 = swap(v1, 4)
                    for k1 in range(2):
                        v2 = jnp.where(((lane32 >> 2) & 1) == k1, v1, w1)
                        dst[offset + zz * 4 + k1 * 2 + k0, pl.ds(xp, ngx, stride=2), :] = v2

    from_lines(f1, s_f1, r_f1)
    place(f1, 0, l1.F, 0, 0.0, (0, 1, 2))
    pre(l1)
    coarsen(l1.R, 0, l1, l2, l2.F, 0, True)
    pre(l2)
    pack4(l2.R, 0, f3, 0)
    spread(f3, s_f3, r_f3, lambda c: c.start())

    collected(es3, s_e3, r_e3)
    place4(es3, 16, 0, l3.E, 1)
    place4(es3, 16, 8, l3.S, 0)
    deep = [l3, l4, l5, l6]
    for fine, coarse in zip(deep[:-1], deep[1:]):
        coarsen(fine.E, 1, fine, coarse, coarse.E, 1, False)
        coarsen(fine.S, 0, fine, coarse, coarse.S, 0, False)
    for lev in deep:
        prepare(lev)

    collected(f3, s_f3, r_f3)
    place4(f3, 8, 0, l3.F, 0)
    for fine, coarse in zip(deep[:-1], deep[1:]):
        pre(fine)
        coarsen(fine.R, 0, fine, coarse, coarse.F, 0, False)
    coarsest(l6)
    for fine, coarse in zip(deep[-2::-1], deep[:0:-1]):
        unrolled(coarse.Z, lambda z, fine=fine, coarse=coarse: spread_rows(fine.V, 2 * z + 1, coarse.C[z + 1], ((0, coarse.X, 0),)))
        post(fine)

    tiles = ngx // 4
    first = gx // 4
    shift = lax.rem(24 - 2 * lax.rem(gx, 4), 24)

    def tile_at(z, k):
        return l3.C[z, pl.ds(pl.multiple_of(lax.rem(first + (k + tiles), tiles) * 8, 8), 8), :]

    right_rows, left_rows = (iota((4, 128), 0) < 2) | has_right, has_left

    def down3(z):
        c = jnp.concatenate([tile_at(z + 1, 0), tile_at(z + 1, 1), tile_at(z + 1, -1)], axis=0)
        c = pltpu.roll(c, shift, 0)
        for k in range(2):
            for j in range(2):
                l2.V[2 * z + 1 + k, pl.ds(j, 4, stride=2), :] = jnp.where(right_rows, c[0:4], 0.0)
                l2.V[2 * z + 1 + k, pl.ds(12 + j, 2, stride=2), :] = jnp.where(left_rows, c[22:24], 0.0)

    filler(l2.V, 0.0)
    unrolled(l3.Z, down3)
    post(l2)
    unrolled(l2.Z, lambda z: spread_rows(l1.V, 2 * z + 1, l2.C[z + 1], ((0, 4, 0), (4, 4, 8), (12, 4, 16))))
    post(l1)
    l1.C[0] = jnp.zeros((24, 128), F32)
    l1.C[l1.Z + 1] = jnp.zeros((24, 128), F32)

    for i in range(10):
        c = l1.C[gz * 8 + i]
        for z in (2 * i - 1, 2 * i):
            if 0 <= z < 18:
                for j in range(2):
                    l0.V[z, pl.ds(j, 8, stride=2), :] = c[0:8]
                l0.V[z, 16:17, :] = c[8:9]
                l0.V[z, 17:23, :] = jnp.zeros((6, 128), F32)
                l0.V[z, 23:24, :] = c[23:24]

    def second_residual(i):
        z0 = i * 4
        v = l0.V[pl.ds(z0 + 1, 4)]
        around = lateral(l0, v, z0, 4) + l0.WZ[pl.ds(z0, 4)] * l0.V[pl.ds(z0, 4)] + l0.WZ[pl.ds(z0 + 1, 4)] * l0.V[pl.ds(z0 + 2, 4)]
        l0.F[pl.ds(z0, 4)] = l0.R[pl.ds(z0, 4)] - (l0.D[pl.ds(z0, 4)] * v - around)

    unrolled(4, second_residual)
    inner(l0.F)
    post_red[gz, 0:16, :] = (l0.F[15] + tail * l0.Y[14])[0:16]
    post_red[gz, 16:32, :] = (lead * l0.Y[0])[0:16]
    gather(post_red, s_post, r_post, lambda c: c.start())
    gathered(post_red, s_post, r_post)
    y = None
    for p in range(ngz):
        right = post_red[p, 0:16, :]
        if p + 1 < ngz:
            right = right + post_red[p + 1, 16:32, :]
        if p:
            right = right + ra[p, 0:16, :] * y
        y = right
        ub[p + 1, 0:16, :] = y
    x = rm[ngz - 1, 0:16, :] * y
    for p in range(ngz - 1, -1, -1):
        if p + 1 < ngz:
            x = rm[p, 0:16, :] * ub[p + 1, 0:16, :] + ra[p + 1, 0:16, :] * x
        ub[p + 1, 0:16, :] = x
    before, own = ub[gz, 0:16, :], ub[gz + 1, 0:16, :]
    for z in range(16):
        if z < 15:
            x = l0.Y[z, 0:16, :] + av[z, 0:16, :] * before + bv[z, 0:16, :] * own
        else:
            x = own
        out[pl.ds(z, 16, stride=16), :] = l0.U[z, 0:16, :] + l0.V[z + 1, 0:16, :] + OMEGA * x

    for copy in r1_copies():
        copy.wait_send()
    es_lines(lambda c: c.wait_send())
    for copy in es_planes():
        copy.wait_send()
    to_lines(f1, s_f1, r_f1, lambda c: c.wait_send())
    gather(red, s_red, r_red, lambda c: c.wait_send())
    gather(post_red, s_post, r_post, lambda c: c.wait_send())
    spread(es3, s_e3, r_e3, lambda c: c.wait_send())
    spread(f3, s_f3, r_f3, lambda c: c.wait_send())


def solution(mesh):
    ngx, ngz = mesh.shape["gx"], mesh.shape["gz"]

    def per_device(charge, codes, eps_table, screen_table):
        nx, nz, ny = charge.shape
        whole_z, whole_x = nz * ngz, nx * ngx
        levels = [
            (nz, 24),
            (whole_z // 2, 24),
            (whole_z // 4, 16),
            (whole_z // 8, whole_x // 8),
            (whole_z // 16, whole_x // 16),
            (whole_z // 32, whole_x // 32),
            (whole_z // 64, whole_x // 64),
        ]
        scratch = []
        for Z, X in levels:
            scratch += Level.scratch(Z, X)
        vm = lambda *shape: pltpu.VMEM(shape, F32)
        scratch += [
            vm(64, 64, 128),
            pltpu.VMEM((nx * nz, ny), jnp.int32),
            vm(nx * nz, ny),
            pltpu.SemaphoreType.DMA((2,)),
            vm(2, 16, 4, 128),
            vm(2, 16, 4, 128),
            vm(2, 16, 128),
            vm(2, 16, 128),
            vm(4, 8, 128),
            vm(4, 8, 128),
            vm(3, ngz, 8, 8, 128),
            vm(3, ngz, 4, 8, 128),
            vm(ngz, 96, 128),
            vm(ngz, 32, 128),
            vm(ngz + 1, 24, 128),
            vm(ngz, 18, 128),
            vm(ngz, 18, 128),
            vm(16, 24, 128),
            vm(16, 24, 128),
            vm(ngx, 16, 128),
            vm(ngx, 8, 128),
        ]
        for shape in ((8,), (3, ngz), (3, ngz), (ngz,), (ngz,), (ngx,), (ngx,)):
            scratch += [pltpu.SemaphoreType.DMA(shape)] * 2
        result = pl.pallas_call(
            lambda *refs: kernel(ngx, ngz, *refs),
            out_shape=jax.ShapeDtypeStruct((nx * nz, ny), F32),
            in_specs=[
                pl.BlockSpec(memory_space=pl.ANY),
                pl.BlockSpec(memory_space=pl.ANY),
                pl.BlockSpec(memory_space=pltpu.SMEM),
                pl.BlockSpec(memory_space=pltpu.SMEM),
            ],
            out_specs=pl.BlockSpec(memory_space=pltpu.VMEM),
            scratch_shapes=scratch,
            compiler_params=pltpu.CompilerParams(collective_id=0, has_side_effects=True, vmem_limit_bytes=56 << 20),
            name="vcycle",
        )(codes.reshape(nx * nz, ny), charge.reshape(nx * nz, ny), eps_table, screen_table)
        return result.reshape(nx, nz, ny)

    return jax.shard_map(
        per_device,
        mesh=mesh,
        in_specs=(P("gx", "gz", None), P("gx", "gz", None), P(), P()),
        out_specs=P("gx", "gz", None),
        check_vma=False,
    )
```

```python
import jax
import jax.numpy as jnp
from jax import lax
from jax.experimental import pallas as pl
from jax.experimental.pallas import tpu as pltpu
from jax.sharding import PartitionSpec as P

OMEGA = 0.8
SWEEPS = 8
LAST = 6
F32 = jnp.float32
MESH = pl.DeviceIdType.MESH


def iota(shape, dim):
    return lax.broadcasted_iota(jnp.int32, shape, dim)


def roll(v, shift, axis):
    size = v.shape[axis]
    return pltpu.roll(v, shift % size, axis)


class Level:
    def __init__(self, index, refs, whole, slab):
        (self.E, self.S, self.WXM, self.WXP, self.WYM, self.WYP, self.WZ, self.D, self.A, self.M, self.F, self.U, self.R, self.Y,
         self.V, self.C) = refs
        self.index, self.whole, self.n = index, whole, slab
        self.Z, self.X = self.S.shape[0], self.S.shape[1]
        self.mask = None

    @staticmethod
    def scratch(Z, X):
        sizes = (Z + 2, Z, Z, Z, Z, Z, Z + 1, Z, Z + 1, Z, Z, Z, Z, Z, Z + 2, Z + 2)
        return [pltpu.VMEM((s, X, 128), F32) for s in sizes]


def loop(count, body):
    def step(i, carry):
        body(i)
        return carry

    lax.fori_loop(0, count, step, 0)


def unrolled(count, body):
    for i in range(count):
        body(i)


def couplings(lev, z0, n):
    h = 0.5 ** lev.index * 0.5
    sh = 2 ** lev.index
    X = lev.X
    e = lev.E[pl.ds(z0 + 1, n)]
    lane = iota((n, X, 128), 2)
    first, last = lane < sh, lane >= 128 - sh
    up, down = roll(e, 1, 1), roll(e, -1, 1)
    if lev.whole:
        row = iota((n, X, 128), 1)
        up, down = jnp.where(row == 0, 0.0, up), jnp.where(row == X - 1, 0.0, down)
    left, right = jnp.where(first, 0.0, roll(e, sh, 2)), jnp.where(last, 0.0, roll(e, -sh, 2))
    wxm, wxp, wym, wyp = h * (e + up), h * (e + down), h * (e + left), h * (e + right)
    wzm, wzp = h * (e + lev.E[pl.ds(z0, n)]), h * (e + lev.E[pl.ds(z0 + 2, n)])
    lev.D[pl.ds(z0, n)] = wxm + wxp + wzm + wzp + wym + wyp + lev.S[pl.ds(z0, n)]
    if lev.whole:
        wxm, wxp = jnp.where(row == 0, 0.0, wxm), jnp.where(row == X - 1, 0.0, wxp)
    lev.WXM[pl.ds(z0, n)] = wxm
    lev.WXP[pl.ds(z0, n)] = wxp
    lev.WYM[pl.ds(z0, n)] = jnp.where(first, 0.0, wym)
    lev.WYP[pl.ds(z0, n)] = jnp.where(last, 0.0, wyp)
    lev.WZ[pl.ds(z0, n)] = wzm
    return wzp


def lateral(lev, u, z0, n):
    sh = 2 ** lev.index
    return (
        lev.WXM[pl.ds(z0, n)] * roll(u, 1, 1)
        + lev.WXP[pl.ds(z0, n)] * roll(u, -1, 1)
        + lev.WYM[pl.ds(z0, n)] * roll(u, sh, 2)
        + lev.WYP[pl.ds(z0, n)] * roll(u, -sh, 2)
    )


def steps_of(count):
    for s in (8, 4, 2):
        if count % s == 0:
            return s
    return 1


def prepare(lev):
    Z, X, n = lev.Z, lev.X, lev.n
    zero = jnp.zeros((1, X, 128), F32)
    lev.E[0:1] = zero
    lev.E[Z + 1 : Z + 2] = zero
    (loop if Z // n > 8 else unrolled)(Z // n, lambda i: couplings(lev, i * n, n))
    lev.WZ[0:1] = zero
    lev.WZ[Z : Z + 1] = zero
    lev.A[Z : Z + 1] = zero
    s = steps_of(Z)

    def body(i, m):
        for j in range(s):
            z = i * s + j
            w = lev.WZ[z]
            a = w * m
            m = 1.0 / (lev.D[z] - w * a)
            lev.A[z] = a
            lev.M[z] = m
        return m

    lax.fori_loop(0, Z // s, body, jnp.zeros((X, 128), F32))


def sweep(lev, src, finish):
    Z, X = lev.Z, lev.X
    s = steps_of(Z)

    def forward(i, y):
        for j in range(s):
            z = i * s + j
            y = src[z] + lev.A[z] * y
            lev.Y[z] = y
        return y

    def backward(i, x):
        for j in range(s):
            z = Z - 1 - (i * s + j)
            x = lev.M[z] * lev.Y[z] + lev.A[z + 1] * x
            finish(z, x)
        return x

    lax.fori_loop(0, Z // s, forward, jnp.zeros((X, 128), F32))
    lax.fori_loop(0, Z // s, backward, jnp.zeros((X, 128), F32))


def pair_lanes(v, index):
    sh = 2 ** index
    lane = iota(v.shape, v.ndim - 1)
    other = jnp.where((lane & sh) == 0, roll(v, -sh, v.ndim - 1), roll(v, sh, v.ndim - 1))
    return v + other


def halve(v, index, tmp, at=0):
    n, X = v.shape[0], v.shape[1]
    v = v.reshape(n // 2, 2, X, 128)
    v = pair_lanes(v[:, 0] + v[:, 1], index)
    part = slice(at, at + n // 2)
    tmp[part, 0:X, :] = v
    return 0.125 * (tmp[part, pl.ds(0, X // 2, stride=2), :] + tmp[part, pl.ds(1, X // 2, stride=2), :])


def pre(lev):
    def finish(z, x):
        lev.U[z] = OMEGA * x

    sweep(lev, lev.F, finish)
    n = lev.n

    def body(i):
        z0 = i * n
        r = (1.0 - OMEGA) * lev.F[pl.ds(z0, n)] + lateral(lev, lev.U[pl.ds(z0, n)], z0, n)
        if lev.mask is not None:
            r = jnp.where(lev.mask[None] > 0, r, 0.0)
        lev.R[pl.ds(z0, n)] = r

    unrolled(lev.Z // n, body)


def post(lev):
    n, Z = lev.n, lev.Z
    zero = jnp.zeros((1, lev.X, 128), F32)
    lev.V[0:1] = zero
    lev.V[Z + 1 : Z + 2] = zero

    def body(i):
        z0 = i * n
        v = lev.V[pl.ds(z0 + 1, n)]
        around = lateral(lev, v, z0, n) + lev.WZ[pl.ds(z0, n)] * lev.V[pl.ds(z0, n)] + lev.WZ[pl.ds(z0 + 1, n)] * lev.V[pl.ds(z0 + 2, n)]
        r = lev.R[pl.ds(z0, n)] - (lev.D[pl.ds(z0, n)] * v - around)
        if lev.mask is not None:
            r = jnp.where(lev.mask[None] > 0, r, 0.0)
        lev.F[pl.ds(z0, n)] = r

    unrolled(Z // n, body)

    def finish(z, x):
        lev.C[z + 1] = lev.U[z] + lev.V[z + 1] + OMEGA * x

    sweep(lev, lev.F, finish)


def coarsest(lev):
    Z = lev.Z

    def first(z, x):
        lev.U[z] = OMEGA * x

    def again(z, x):
        lev.U[z] = (1.0 - OMEGA) * lev.U[z] + OMEGA * x

    def last(z, x):
        lev.C[z + 1] = (1.0 - OMEGA) * lev.U[z] + OMEGA * x

    sweep(lev, lev.F, first)

    def once(finish):
        lev.R[...] = lev.F[...] + lateral(lev, lev.U[...], 0, Z)
        sweep(lev, lev.R, finish)

    loop(SWEEPS - 2, lambda i: once(again))
    once(last)


def spread_rows(dst, z, c, rows):
    for source, count, target in rows:
        part = c[source : source + count]
        for k in range(2):
            for j in range(2):
                dst[z + k, pl.ds(target + j, count, stride=2), :] = part


def kernel(ngx, ngz, *refs):
    codes_in, charge_in, eps_t, scr_t, out = refs[:5]
    refs = list(refs[5:])

    def take(count):
        got = refs[:count]
        del refs[:count]
        return got

    l0 = Level(0, take(16), False, 4)
    l1 = Level(1, take(16), False, 8)
    l2 = Level(2, take(16), False, 8)
    l3 = Level(3, take(16), True, 4)
    l4 = Level(4, take(16), True, 4)
    l5 = Level(5, take(16), True, 4)
    l6 = Level(6, take(16), True, 2)
    (tmp, codes, charge, s_in, xs, xr, zs, zr, ds, dr, es, f1, red, post_red, ub, rm, ra, av, bv, es3, f3, fh, fr, f2, f2r) = take(25)
    (s_r1, r_r1, s_es, r_es, s_f1, r_f1, s_red, r_red, s_post, r_post, s_e3, r_e3, s_f3, r_f3, s_f2, r_f2) = take(16)

    gx, gz = lax.axis_index("gx"), lax.axis_index("gz")

    def gx_at(k):
        return lax.rem(gx + (k + ngx), ngx)

    def gz_at(k):
        return lax.rem(gz + (k + ngz), ngz)

    def remote(src, dst, ss, rs, tx, tz):
        return pltpu.make_async_remote_copy(src, dst, ss, rs, device_id=(tx, tz), device_id_type=MESH)

    inputs = (pltpu.make_async_copy(codes_in, codes, s_in.at[0]), pltpu.make_async_copy(charge_in, charge, s_in.at[1]))
    for copy in inputs:
        copy.start()

    barrier = pltpu.get_barrier_semaphore()

    def hello(tx, tz):
        pl.semaphore_signal(barrier, 1, device_id=(tx, tz), device_id_type=MESH)

    loop(ngz - 1, lambda k: hello(gx, gz_at(k + 1)))
    loop(ngz, lambda k: hello(gx_at(1), gz_at(k)))
    loop(ngz, lambda k: hello(gx_at(-1), gz_at(k)))
    loop(ngx - 3, lambda k: hello(gx_at(k + 2), gz))

    row24, row16 = iota((24, 128), 0), iota((16, 128), 0)
    has_right, has_left = gx < ngx - 1, gx > 0
    lane = iota((1, 8, 128), 2)

    table_e = [jnp.full((16, 128), eps_t[k], F32) for k in range(eps_t.shape[0])]
    table_s = [jnp.full((16, 128), scr_t[k], F32) for k in range(eps_t.shape[0])]

    def look(i):
        c = codes[pl.ds(i, 16, stride=16), :]
        e = jnp.zeros((16, 128), F32)
        s = jnp.zeros((16, 128), F32)
        for k in range(eps_t.shape[0]):
            e = jnp.where(c == k, table_e[k], e)
            s = jnp.where(c == k, table_s[k], s)
        l0.E[i + 1, 0:16, :] = e
        l0.S[i, 0:16, :] = s
        l0.F[i, 0:16, :] = charge[pl.ds(i, 16, stride=16), :]

    for copy in inputs:
        copy.wait()
    unrolled(16, look)

    xs[0, :, 0:2, :] = l0.E[1:17, 14:16, :]
    xs[0, :, 2:3, :] = l0.S[:, 15:16, :]
    xs[0, :, 3:4, :] = l0.F[:, 15:16, :]
    xs[1, :, 0:2, :] = l0.E[1:17, 0:2, :]
    xs[1, :, 2:3, :] = l0.S[:, 0:1, :]
    xs[1, :, 3:4, :] = l0.F[:, 0:1, :]
    zs[0] = l0.E[16, 0:16, :]
    zs[1] = l0.E[1, 0:16, :]
    ds[0] = l0.E[16, 8:16, :]
    ds[1] = l0.E[16, 0:8, :]
    ds[2] = l0.E[1, 8:16, :]
    ds[3] = l0.E[1, 0:8, :]

    def r1_copies():
        return [
            remote(xs.at[0], xr.at[0], s_r1.at[0], r_r1.at[0], gx_at(1), gz),
            remote(xs.at[1], xr.at[1], s_r1.at[1], r_r1.at[1], gx_at(-1), gz),
            remote(zs.at[0], zr.at[0], s_r1.at[2], r_r1.at[2], gx, gz_at(1)),
            remote(zs.at[1], zr.at[1], s_r1.at[3], r_r1.at[3], gx, gz_at(-1)),
            remote(ds.at[0], dr.at[0], s_r1.at[4], r_r1.at[4], gx_at(1), gz_at(1)),
            remote(ds.at[1], dr.at[1], s_r1.at[5], r_r1.at[5], gx_at(-1), gz_at(1)),
            remote(ds.at[2], dr.at[2], s_r1.at[6], r_r1.at[6], gx_at(1), gz_at(-1)),
            remote(ds.at[3], dr.at[3], s_r1.at[7], r_r1.at[7], gx_at(-1), gz_at(-1)),
        ]

    pl.semaphore_wait(barrier, 3 * ngz - 1 + ngx - 3)
    for copy in r1_copies():
        copy.start()

    def pack2(v):
        v = v.reshape(4, 2, 8, 128)
        return jnp.where((lane & 1) == 0, v[:, 0], v[:, 1])

    es[0, gz, 0:4] = pack2(halve(l0.E[1:17, 0:16, :], 0, tmp))
    es[0, gz, 4:8] = pack2(halve(l0.S[:, 0:16, :], 0, tmp, 8))

    def f1_copies(act):
        def go(slot, k, src, dst, tx):
            act(remote(src, dst, s_f1.at[slot, k], r_f1.at[slot, gz], tx, gz_at(k)))

        loop(ngz - 1, lambda k: go(0, k + 1, f1.at[gz], f1.at[gz], gx))
        loop(ngz, lambda k: go(1, k, fh.at[0], fr.at[0, gz], gx_at(1)))
        loop(ngz, lambda k: go(2, k, fh.at[1], fr.at[1, gz], gx_at(-1)))

    def f1_arrive():
        def get(slot, dst, k):
            p = gz_at(k)
            remote(dst, dst, s_f1.at[slot, k], r_f1.at[slot, p], gx, gz_at(1)).wait_recv()

        loop(ngz - 1, lambda k: get(0, f1.at[gz], k + 1))
        loop(ngz, lambda k: get(1, fr.at[0, gz], k))
        loop(ngz, lambda k: get(2, fr.at[1, gz], k))

    def es_lines(act):
        loop(ngz - 1, lambda k: act(remote(es.at[0, gz], es.at[0, gz], s_es.at[0, k + 1], r_es.at[0, gz], gx, gz_at(k + 1))))

    def es_planes():
        return [
            remote(es.at[0], es.at[2], s_es.at[2, 0], r_es.at[2, 0], gx_at(1), gz),
            remote(es.at[0], es.at[1], s_es.at[1, 0], r_es.at[1, 0], gx_at(-1), gz),
        ]

    es_lines(lambda c: c.start())

    for copy in r1_copies():
        copy.wait_recv()

    above, below = gz > 0, gz < ngz - 1
    zero16 = jnp.zeros((16, 24, 128), F32)
    l0.E[0:1] = zero16[0:1]
    l0.E[17:18] = zero16[0:1]
    l0.E[1:17, 16:24, :] = zero16[:, 0:8]
    l0.S[:, 16:24, :] = jnp.ones((16, 8, 128), F32)
    l0.F[:, 16:24, :] = zero16[:, 0:8]
    l0.E[1:17, 22:24, :] = jnp.where(has_left, xr[0, :, 0:2, :], 0.0)
    l0.S[:, 23:24, :] = jnp.where(has_left, xr[0, :, 2:3, :], 1.0)
    l0.F[:, 23:24, :] = jnp.where(has_left, xr[0, :, 3:4, :], 0.0)
    l0.E[1:17, 16:18, :] = jnp.where(has_right, xr[1, :, 0:2, :], 0.0)
    l0.S[:, 16:17, :] = jnp.where(has_right, xr[1, :, 2:3, :], 1.0)
    l0.F[:, 16:17, :] = jnp.where(has_right, xr[1, :, 3:4, :], 0.0)
    l0.E[0, 0:16, :] = jnp.where(above, zr[0], 0.0)
    l0.E[17, 0:16, :] = jnp.where(below, zr[1], 0.0)
    l0.E[0, 23:24, :] = jnp.where(above & has_left, dr[0, 7:8, :], 0.0)
    l0.E[0, 16:17, :] = jnp.where(above & has_right, dr[1, 0:1, :], 0.0)
    l0.E[17, 23:24, :] = jnp.where(below & has_left, dr[2, 7:8, :], 0.0)
    l0.E[17, 16:17, :] = jnp.where(below & has_right, dr[3, 0:1, :], 0.0)

    for i in range(4):
        wzp = couplings(l0, i * 4, 4)
    l0.WZ[16:17] = wzp[3:4]

    m = 1.0 / l0.D[0]
    l0.M[0] = m
    for z in range(1, 15):
        w = l0.WZ[z]
        a = w * m
        m = 1.0 / (l0.D[z] - w * a)
        l0.A[z] = a
        l0.M[z] = m
    lead = jnp.where(above, l0.WZ[0], 0.0)
    tail = l0.WZ[15]

    y = lead
    av[0] = y
    for z in range(1, 15):
        y = l0.A[z] * y
        av[z] = y
    x = l0.M[14] * y
    b = l0.M[14] * tail
    av[14] = x
    bv[14] = b
    for z in range(13, -1, -1):
        x = l0.M[z] * av[z] + l0.A[z + 1] * x
        b = l0.A[z + 1] * b
        av[z] = x
        bv[z] = b

    def inner(src):
        y = src[0]
        l0.Y[0] = y
        for z in range(1, 15):
            y = src[z] + l0.A[z] * y
            l0.Y[z] = y
        x = l0.M[14] * y
        l0.Y[14] = x
        for z in range(13, -1, -1):
            x = l0.M[z] * l0.Y[z] + l0.A[z + 1] * x
            l0.Y[z] = x

    inner(l0.F)

    def put(k, v):
        red[gz, pl.ds(k * 18, 17), :] = v[0:17]
        red[gz, pl.ds(k * 18 + 17, 1), :] = v[23:24]

    put(0, tail * av[14])
    put(1, l0.D[15] - tail * bv[14])
    put(2, lead * av[0])
    put(3, l0.F[15] + tail * l0.Y[14])
    put(4, lead * l0.Y[0])

    def gather(buf, ss, rs, act):
        loop(ngz - 1, lambda k: act(remote(buf.at[gz], buf.at[gz], ss.at[k + 1], rs.at[gz], gx, gz_at(k + 1))))

    def gathered(buf, ss, rs):
        def get(k):
            p = gz_at(k)
            remote(buf.at[gz], buf.at[p], ss.at[k], rs.at[p], gx, p).wait_recv()

        loop(ngz - 1, lambda k: get(k + 1))

    gather(red, s_red, r_red, lambda c: c.start())

    def es_line_in(k):
        p = gz_at(k + 1)
        remote(es.at[0, gz], es.at[0, p], s_es.at[0, k + 1], r_es.at[0, p], gx, p).wait_recv()

    loop(ngz - 1, es_line_in)
    for copy in es_planes():
        copy.start()

    mask1 = jnp.where(row24 < 8, 1.0, jnp.where(row24 < 16, jnp.where(has_right, 1.0, 0.0), jnp.where(has_left, 1.0, 0.0)))
    mask2 = jnp.where(
        row16 < 4,
        1.0,
        jnp.where(row16 < 8, jnp.where(has_right, 1.0, 0.0), jnp.where(row16 < 12, 0.0, jnp.where(has_left, 1.0, 0.0))),
    )
    l1.mask, l2.mask = mask1, mask2

    def unpack2(v):
        even = jnp.where((lane & 1) == 0, v, roll(v, 1, 2))
        odd = jnp.where((lane & 1) == 1, v, roll(v, -1, 2))
        return jnp.stack([even, odd], axis=1).reshape(2 * v.shape[0], 8, 128)

    here = (None, has_right, has_left)

    def place(buf, start, dst, offset, outside, slots):
        for slot in slots:
            for p in range(ngz):
                v = unpack2(buf[slot, p, start : start + 4])
                if slot:
                    v = jnp.where(here[slot], v, outside)
                dst[p * 8 + offset : p * 8 + offset + 8, slot * 8 : slot * 8 + 8, :] = v

    place(es, 0, l1.E, 1, 0.0, (0,))
    place(es, 4, l1.S, 0, 1.0, (0,))

    def coarsen(src, offset, fine, coarse, dst, dst_offset, split):
        n = fine.n

        def body(i):
            v = halve(src[i * n + offset : (i + 1) * n + offset], fine.index, tmp, i * (n // 2))
            at = slice(i * (n // 2) + dst_offset, (i + 1) * (n // 2) + dst_offset)
            if split:
                dst[at, 0:8, :] = v[:, 0:8]
                dst[at, 12:16, :] = v[:, 8:12]
            else:
                dst[at] = v

        unrolled(fine.Z // n, body)

    def filler(ref, value):
        ref[:, 8:12, :] = jnp.full((ref.shape[0], 4, 128), value, F32)

    filler(l2.E, 0.0)
    filler(l2.S, 1.0)
    filler(l2.F, 0.0)

    lane3 = iota((4, 2, 128), 2)

    def pack4(src, offset, buf, first):
        for i in range(2):
            v = halve(src[i * 16 + offset : i * 16 + offset + 16], 2, tmp, i * 8)[:, 0:2]
            tmp[i * 8 : i * 8 + 8, 32:34, :] = v
        v = tmp[0:16, 32:34, :].reshape(4, 4, 2, 128)
        k = (lane3 >> 1) & 3
        v = jnp.where(k == 0, v[:, 0], jnp.where(k == 1, v[:, 1], jnp.where(k == 2, v[:, 2], v[:, 3])))
        for zz in range(4):
            buf[gx, first + zz * 2 : first + zz * 2 + 2, :] = v[zz]

    def spread(buf, ss, rs, act):
        loop(ngx - 1, lambda k: act(remote(buf.at[gx], buf.at[gx], ss.at[k + 1], rs.at[gx], gx_at(k + 1), gz)))

    def collected(buf, ss, rs):
        def get(k):
            p = gx_at(k)
            remote(buf.at[gx], buf.at[p], ss.at[k], rs.at[p], p, gz).wait_recv()

        loop(ngx - 1, lambda k: get(k + 1))

    gathered(red, s_red, r_red)

    def got(p, k):
        return red[p, pl.ds(k * 18, 18), :]

    m, y = None, None
    for p in range(ngz):
        diag, right = got(p, 1), got(p, 3)
        if p + 1 < ngz:
            diag, right = diag - got(p + 1, 2), right + got(p + 1, 4)
        if p:
            c = got(p, 0)
            a = c * m
            diag, right = diag - c * a, right + a * y
            ra[p] = a
        m, y = 1.0 / diag, right
        rm[p] = m
        ub[p + 1, 0:18, :] = y
    x = m * y
    for p in range(ngz - 1, -1, -1):
        if p + 1 < ngz:
            x = rm[p] * ub[p + 1, 0:18, :] + ra[p + 1] * x
        ub[p + 1, 0:17, :] = x[0:17]
        ub[p + 1, 23:24, :] = x[17:18]
        ub[p + 1, 17:23, :] = jnp.zeros((6, 128), F32)
    ub[0] = jnp.zeros((24, 128), F32)

    before, own = ub[gz], ub[gz + 1]
    for z in range(15):
        l0.U[z] = OMEGA * (l0.Y[z] + av[z] * before + bv[z] * own)
    l0.U[15] = OMEGA * own

    def first_residual(i):
        z0 = i * 4
        l0.R[pl.ds(z0, 4)] = (1.0 - OMEGA) * l0.F[pl.ds(z0, 4)] + lateral(l0, l0.U[pl.ds(z0, 4)], z0, 4)

    unrolled(4, first_residual)
    packed = pack2(halve(l0.R[:, 0:16, :], 0, tmp))
    f1[gz] = packed
    for zz in range(4):
        fh[0, zz * 4 : zz * 4 + 4, :] = packed[zz, 4:8]
        fh[1, zz * 4 : zz * 4 + 4, :] = packed[zz, 0:4]
    f1_copies(lambda c: c.start())

    for copy in es_planes():
        copy.wait_recv()
    place(es, 0, l1.E, 1, 0.0, (1, 2))
    place(es, 4, l1.S, 0, 1.0, (1, 2))
    coarsen(l1.E, 1, l1, l2, l2.E, 1, True)
    coarsen(l1.S, 0, l1, l2, l2.S, 0, True)
    pack4(l2.E, 1, es3, 0)
    pack4(l2.S, 0, es3, 8)
    spread(es3, s_e3, r_e3, lambda c: c.start())
    prepare(l1)
    prepare(l2)

    lane32 = iota((32, 128), 1)

    def swap(v, s):
        return jnp.where((lane32 & s) == 0, roll(v, -s, 1), roll(v, s, 1))

    def place4(buf, rows, first, dst, offset):
        for zz in range(4):
            for xp in range(2):
                v = buf[:, first + zz * 2 + xp, :]
                w = swap(v, 2)
                for k0 in range(2):
                    v1 = jnp.where(((lane32 >> 1) & 1) == k0, v, w)
                    w1 = swap(v1, 4)
                    for k1 in range(2):
                        v2 = jnp.where(((lane32 >> 2) & 1) == k1, v1, w1)
                        dst[offset + zz * 4 + k1 * 2 + k0, pl.ds(xp, ngx, stride=2), :] = v2

    l1.F[:, 8:24, :] = jnp.zeros((l1.Z, 16, 128), F32)
    lane16 = iota((16, 128), 1)
    f1_arrive()
    for p in range(ngz):
        l1.F[p * 8 : p * 8 + 8, 0:8, :] = unpack2(f1[p])
        for side, present, row in ((0, has_left, 20), (1, has_right, 8)):
            v = jnp.where(present, fr[side, p], 0.0)
            both = (jnp.where((lane16 & 1) == 0, v, roll(v, 1, 1)), jnp.where((lane16 & 1) == 1, v, roll(v, -1, 1)))
            for zz in range(4):
                for k in range(2):
                    l1.F[p * 8 + zz * 2 + k, row : row + 4, :] = both[k][zz * 4 : zz * 4 + 4]
    pre(l1)
    coarsen(l1.R, 0, l1, l2, l2.F, 0, True)
    pre(l2)
    pack4(l2.R, 0, f3, 0)
    spread(f3, s_f3, r_f3, lambda c: c.start())

    lane8 = iota((8, 8, 128), 2)
    v = l2.F[:, 0:8, :].reshape(8, 4, 8, 128)
    k = lane8 & 3
    f2[...] = jnp.where(k == 0, v[:, 0], jnp.where(k == 1, v[:, 1], jnp.where(k == 2, v[:, 2], v[:, 3])))

    def f2_copies():
        return [
            remote(f2, f2r.at[0], s_f2.at[0], r_f2.at[0], gx_at(1), gz),
            remote(f2, f2r.at[1], s_f2.at[1], r_f2.at[1], gx_at(-1), gz),
        ]

    for copy in f2_copies():
        copy.start()

    collected(es3, s_e3, r_e3)
    place4(es3, 16, 0, l3.E, 1)
    place4(es3, 16, 8, l3.S, 0)
    deep = [l3, l4, l5, l6]
    for fine, coarse in zip(deep[:-1], deep[1:]):
        coarsen(fine.E, 1, fine, coarse, coarse.E, 1, False)
        coarsen(fine.S, 0, fine, coarse, coarse.S, 0, False)
    for lev in deep:
        prepare(lev)

    for copy in f2_copies():
        copy.wait_recv()

    def swap8(v, s):
        return jnp.where((lane8 & s) == 0, roll(v, -s, 2), roll(v, s, 2))

    for side, present, source, row in ((0, has_left, 2, 14), (1, has_right, 1, 5)):
        v = jnp.where(present, f2r[side], 0.0)
        w = swap8(v, 1)
        for k0 in range(2):
            v1 = jnp.where((lane8 & 1) == k0, v, w)
            w1 = swap8(v1, 2)
            for k1 in range(2):
                v2 = jnp.where(((lane8 >> 1) & 1) == k1, v1, w1)
                for zz in range(8):
                    l2.F[zz * 4 + k1 * 2 + k0, row : row + 1, :] = v2[zz, source : source + 1]
    pre(l2)

    collected(f3, s_f3, r_f3)
    place4(f3, 8, 0, l3.F, 0)
    for fine, coarse in zip(deep[:-1], deep[1:]):
        pre(fine)
        coarsen(fine.R, 0, fine, coarse, coarse.F, 0, False)
    coarsest(l6)
    for fine, coarse in zip(deep[-2::-1], deep[:0:-1]):
        unrolled(coarse.Z, lambda z, fine=fine, coarse=coarse: spread_rows(fine.V, 2 * z + 1, coarse.C[z + 1], ((0, coarse.X, 0),)))
        post(fine)

    tiles = ngx // 4
    first = gx // 4
    shift = lax.rem(24 - 2 * lax.rem(gx, 4), 24)

    def tile_at(z, k):
        return l3.C[z, pl.ds(pl.multiple_of(lax.rem(first + (k + tiles), tiles) * 8, 8), 8), :]

    right_rows, left_rows = (iota((4, 128), 0) < 2) | has_right, has_left

    def down3(z):
        c = jnp.concatenate([tile_at(z + 1, 0), tile_at(z + 1, 1), tile_at(z + 1, -1)], axis=0)
        c = pltpu.roll(c, shift, 0)
        for k in range(2):
            for j in range(2):
                l2.V[2 * z + 1 + k, pl.ds(j, 4, stride=2), :] = jnp.where(right_rows, c[0:4], 0.0)
                l2.V[2 * z + 1 + k, pl.ds(12 + j, 2, stride=2), :] = jnp.where(left_rows, c[22:24], 0.0)

    filler(l2.V, 0.0)
    unrolled(l3.Z, down3)
    post(l2)
    unrolled(l2.Z, lambda z: spread_rows(l1.V, 2 * z + 1, l2.C[z + 1], ((0, 4, 0), (4, 4, 8), (12, 4, 16))))
    post(l1)
    l1.C[0] = jnp.zeros((24, 128), F32)
    l1.C[l1.Z + 1] = jnp.zeros((24, 128), F32)

    for i in range(10):
        c = l1.C[gz * 8 + i]
        for z in (2 * i - 1, 2 * i):
            if 0 <= z < 18:
                for j in range(2):
                    l0.V[z, pl.ds(j, 8, stride=2), :] = c[0:8]
                l0.V[z, 16:17, :] = c[8:9]
                l0.V[z, 17:23, :] = jnp.zeros((6, 128), F32)
                l0.V[z, 23:24, :] = c[23:24]

    def second_residual(i):
        z0 = i * 4
        v = l0.V[pl.ds(z0 + 1, 4)]
        around = lateral(l0, v, z0, 4) + l0.WZ[pl.ds(z0, 4)] * l0.V[pl.ds(z0, 4)] + l0.WZ[pl.ds(z0 + 1, 4)] * l0.V[pl.ds(z0 + 2, 4)]
        l0.F[pl.ds(z0, 4)] = l0.R[pl.ds(z0, 4)] - (l0.D[pl.ds(z0, 4)] * v - around)

    unrolled(4, second_residual)
    inner(l0.F)
    post_red[gz, 0:16, :] = (l0.F[15] + tail * l0.Y[14])[0:16]
    post_red[gz, 16:32, :] = (lead * l0.Y[0])[0:16]
    gather(post_red, s_post, r_post, lambda c: c.start())
    gathered(post_red, s_post, r_post)
    y = None
    for p in range(ngz):
        right = post_red[p, 0:16, :]
        if p + 1 < ngz:
            right = right + post_red[p + 1, 16:32, :]
        if p:
            right = right + ra[p, 0:16, :] * y
        y = right
        ub[p + 1, 0:16, :] = y
    x = rm[ngz - 1, 0:16, :] * y
    for p in range(ngz - 1, -1, -1):
        if p + 1 < ngz:
            x = rm[p, 0:16, :] * ub[p + 1, 0:16, :] + ra[p + 1, 0:16, :] * x
        ub[p + 1, 0:16, :] = x
    before, own = ub[gz, 0:16, :], ub[gz + 1, 0:16, :]
    for z in range(16):
        if z < 15:
            x = l0.Y[z, 0:16, :] + av[z, 0:16, :] * before + bv[z, 0:16, :] * own
        else:
            x = own
        out[pl.ds(z, 16, stride=16), :] = l0.U[z, 0:16, :] + l0.V[z + 1, 0:16, :] + OMEGA * x

    for copy in r1_copies():
        copy.wait_send()
    es_lines(lambda c: c.wait_send())
    for copy in es_planes():
        copy.wait_send()
    f1_copies(lambda c: c.wait_send())
    for copy in f2_copies():
        copy.wait_send()
    gather(red, s_red, r_red, lambda c: c.wait_send())
    gather(post_red, s_post, r_post, lambda c: c.wait_send())
    spread(es3, s_e3, r_e3, lambda c: c.wait_send())
    spread(f3, s_f3, r_f3, lambda c: c.wait_send())


def solution(mesh):
    ngx, ngz = mesh.shape["gx"], mesh.shape["gz"]

    def per_device(charge, codes, eps_table, screen_table):
        nx, nz, ny = charge.shape
        whole_z, whole_x = nz * ngz, nx * ngx
        levels = [
            (nz, 24),
            (whole_z // 2, 24),
            (whole_z // 4, 16),
            (whole_z // 8, whole_x // 8),
            (whole_z // 16, whole_x // 16),
            (whole_z // 32, whole_x // 32),
            (whole_z // 64, whole_x // 64),
        ]
        scratch = []
        for Z, X in levels:
            scratch += Level.scratch(Z, X)
        vm = lambda *shape: pltpu.VMEM(shape, F32)
        scratch += [
            vm(64, 64, 128),
            pltpu.VMEM((nx * nz, ny), jnp.int32),
            vm(nx * nz, ny),
            pltpu.SemaphoreType.DMA((2,)),
            vm(2, 16, 4, 128),
            vm(2, 16, 4, 128),
            vm(2, 16, 128),
            vm(2, 16, 128),
            vm(4, 8, 128),
            vm(4, 8, 128),
            vm(3, ngz, 8, 8, 128),
            vm(ngz, 4, 8, 128),
            vm(ngz, 96, 128),
            vm(ngz, 32, 128),
            vm(ngz + 1, 24, 128),
            vm(ngz, 18, 128),
            vm(ngz, 18, 128),
            vm(16, 24, 128),
            vm(16, 24, 128),
            vm(ngx, 16, 128),
            vm(ngx, 8, 128),
            vm(2, 16, 128),
            vm(2, ngz, 16, 128),
            vm(8, 8, 128),
            vm(2, 8, 8, 128),
        ]
        for shape in ((8,), (3, ngz), (3, ngz), (ngz,), (ngz,), (ngx,), (ngx,), (2,)):
            scratch += [pltpu.SemaphoreType.DMA(shape)] * 2
        result = pl.pallas_call(
            lambda *refs: kernel(ngx, ngz, *refs),
            out_shape=jax.ShapeDtypeStruct((nx * nz, ny), F32),
            in_specs=[
                pl.BlockSpec(memory_space=pl.ANY),
                pl.BlockSpec(memory_space=pl.ANY),
                pl.BlockSpec(memory_space=pltpu.SMEM),
                pl.BlockSpec(memory_space=pltpu.SMEM),
            ],
            out_specs=pl.BlockSpec(memory_space=pltpu.VMEM),
            scratch_shapes=scratch,
            compiler_params=pltpu.CompilerParams(collective_id=0, has_side_effects=True, vmem_limit_bytes=56 << 20),
            name="vcycle",
        )(codes.reshape(nx * nz, ny), charge.reshape(nx * nz, ny), eps_table, screen_table)
        return result.reshape(nx, nz, ny)

    return jax.shard_map(
        per_device,
        mesh=mesh,
        in_specs=(P("gx", "gz", None), P("gx", "gz", None), P(), P()),
        out_specs=P("gx", "gz", None),
        check_vma=False,
    )
```

```python
import jax
import jax.numpy as jnp
from jax import lax
from jax.experimental import pallas as pl
from jax.experimental.pallas import tpu as pltpu
from jax.sharding import PartitionSpec as P

OMEGA = 0.8
SWEEPS = 8
LAST = 6
F32 = jnp.float32
MESH = pl.DeviceIdType.MESH
FAR_FIRST = (4, 3, 5, 2, 6, 1, 7)


def iota(shape, dim):
    return lax.broadcasted_iota(jnp.int32, shape, dim)


def roll(v, shift, axis):
    size = v.shape[axis]
    return pltpu.roll(v, shift % size, axis)


class Level:
    def __init__(self, index, refs, whole, slab):
        (self.E, self.S, self.WXM, self.WXP, self.WYM, self.WYP, self.WZ, self.D, self.A, self.M, self.F, self.U, self.R, self.Y,
         self.V, self.C) = refs
        self.index, self.whole, self.n = index, whole, slab
        self.Z, self.X = self.S.shape[0], self.S.shape[1]
        self.mask = None

    @staticmethod
    def scratch(Z, X):
        sizes = (Z + 2, Z, Z, Z, Z, Z, Z + 1, Z, Z + 1, Z, Z, Z, Z, Z, Z + 2, Z + 2)
        return [pltpu.VMEM((s, X, 128), F32) for s in sizes]


def loop(count, body):
    def step(i, carry):
        body(i)
        return carry

    lax.fori_loop(0, count, step, 0)


def unrolled(count, body):
    for i in range(count):
        body(i)


def couplings(lev, z0, n):
    h = 0.5 ** lev.index * 0.5
    sh = 2 ** lev.index
    X = lev.X
    e = lev.E[pl.ds(z0 + 1, n)]
    lane = iota((n, X, 128), 2)
    first, last = lane < sh, lane >= 128 - sh
    up, down = roll(e, 1, 1), roll(e, -1, 1)
    if lev.whole:
        row = iota((n, X, 128), 1)
        up, down = jnp.where(row == 0, 0.0, up), jnp.where(row == X - 1, 0.0, down)
    left, right = jnp.where(first, 0.0, roll(e, sh, 2)), jnp.where(last, 0.0, roll(e, -sh, 2))
    wxm, wxp, wym, wyp = h * (e + up), h * (e + down), h * (e + left), h * (e + right)
    wzm, wzp = h * (e + lev.E[pl.ds(z0, n)]), h * (e + lev.E[pl.ds(z0 + 2, n)])
    lev.D[pl.ds(z0, n)] = wxm + wxp + wzm + wzp + wym + wyp + lev.S[pl.ds(z0, n)]
    if lev.whole:
        wxm, wxp = jnp.where(row == 0, 0.0, wxm), jnp.where(row == X - 1, 0.0, wxp)
    lev.WXM[pl.ds(z0, n)] = wxm
    lev.WXP[pl.ds(z0, n)] = wxp
    lev.WYM[pl.ds(z0, n)] = jnp.where(first, 0.0, wym)
    lev.WYP[pl.ds(z0, n)] = jnp.where(last, 0.0, wyp)
    lev.WZ[pl.ds(z0, n)] = wzm
    return wzp


def lateral(lev, u, z0, n):
    sh = 2 ** lev.index
    return (
        lev.WXM[pl.ds(z0, n)] * roll(u, 1, 1)
        + lev.WXP[pl.ds(z0, n)] * roll(u, -1, 1)
        + lev.WYM[pl.ds(z0, n)] * roll(u, sh, 2)
        + lev.WYP[pl.ds(z0, n)] * roll(u, -sh, 2)
    )


def steps_of(count):
    for s in (8, 4, 2):
        if count % s == 0:
            return s
    return 1


def prepare(lev):
    Z, X, n = lev.Z, lev.X, lev.n
    zero = jnp.zeros((1, X, 128), F32)
    lev.E[0:1] = zero
    lev.E[Z + 1 : Z + 2] = zero
    (loop if Z // n > 8 else unrolled)(Z // n, lambda i: couplings(lev, i * n, n))
    lev.WZ[0:1] = zero
    lev.WZ[Z : Z + 1] = zero
    lev.A[Z : Z + 1] = zero
    s = steps_of(Z)

    def body(i, m):
        for j in range(s):
            z = i * s + j
            w = lev.WZ[z]
            a = w * m
            m = 1.0 / (lev.D[z] - w * a)
            lev.A[z] = a
            lev.M[z] = m
        return m

    lax.fori_loop(0, Z // s, body, jnp.zeros((X, 128), F32))


def sweep(lev, src, finish):
    Z, X = lev.Z, lev.X
    s = steps_of(Z)

    def forward(i, y):
        for j in range(s):
            z = i * s + j
            y = src[z] + lev.A[z] * y
            lev.Y[z] = y
        return y

    def backward(i, x):
        for j in range(s):
            z = Z - 1 - (i * s + j)
            x = lev.M[z] * lev.Y[z] + lev.A[z + 1] * x
            finish(z, x)
        return x

    lax.fori_loop(0, Z // s, forward, jnp.zeros((X, 128), F32))
    lax.fori_loop(0, Z // s, backward, jnp.zeros((X, 128), F32))


def pair_lanes(v, index):
    sh = 2 ** index
    lane = iota(v.shape, v.ndim - 1)
    other = jnp.where((lane & sh) == 0, roll(v, -sh, v.ndim - 1), roll(v, sh, v.ndim - 1))
    return v + other


def halve(v, index, tmp, at=0):
    n, X = v.shape[0], v.shape[1]
    v = v.reshape(n // 2, 2, X, 128)
    v = pair_lanes(v[:, 0] + v[:, 1], index)
    part = slice(at, at + n // 2)
    tmp[part, 0:X, :] = v
    return 0.125 * (tmp[part, pl.ds(0, X // 2, stride=2), :] + tmp[part, pl.ds(1, X // 2, stride=2), :])


def pre(lev):
    def finish(z, x):
        lev.U[z] = OMEGA * x

    sweep(lev, lev.F, finish)
    n = lev.n

    def body(i):
        z0 = i * n
        r = (1.0 - OMEGA) * lev.F[pl.ds(z0, n)] + lateral(lev, lev.U[pl.ds(z0, n)], z0, n)
        if lev.mask is not None:
            r = jnp.where(lev.mask[None] > 0, r, 0.0)
        lev.R[pl.ds(z0, n)] = r

    unrolled(lev.Z // n, body)


def post(lev):
    n, Z = lev.n, lev.Z
    zero = jnp.zeros((1, lev.X, 128), F32)
    lev.V[0:1] = zero
    lev.V[Z + 1 : Z + 2] = zero

    def body(i):
        z0 = i * n
        v = lev.V[pl.ds(z0 + 1, n)]
        around = lateral(lev, v, z0, n) + lev.WZ[pl.ds(z0, n)] * lev.V[pl.ds(z0, n)] + lev.WZ[pl.ds(z0 + 1, n)] * lev.V[pl.ds(z0 + 2, n)]
        r = lev.R[pl.ds(z0, n)] - (lev.D[pl.ds(z0, n)] * v - around)
        if lev.mask is not None:
            r = jnp.where(lev.mask[None] > 0, r, 0.0)
        lev.F[pl.ds(z0, n)] = r

    unrolled(Z // n, body)

    def finish(z, x):
        lev.C[z + 1] = lev.U[z] + lev.V[z + 1] + OMEGA * x

    sweep(lev, lev.F, finish)


def coarsest(lev):
    Z = lev.Z
    sh = 2 ** lev.index
    f = [lev.F[z] for z in range(Z)]
    a = [lev.A[z] for z in range(Z + 1)]
    m = [lev.M[z] for z in range(Z)]
    w = [(lev.WXM[z], lev.WXP[z], lev.WYM[z], lev.WYP[z]) for z in range(Z)]

    def solved(r):
        y = [r[0]]
        for z in range(1, Z):
            y.append(r[z] + a[z] * y[-1])
        x = [None] * Z
        x[Z - 1] = m[Z - 1] * y[Z - 1]
        for z in range(Z - 2, -1, -1):
            x[z] = m[z] * y[z] + a[z + 1] * x[z + 1]
        return x

    u = [OMEGA * x for x in solved(f)]
    for _ in range(SWEEPS - 1):
        r = []
        for z in range(Z):
            xm, xp, ym, yp = w[z]
            side = xm * roll(u[z], 1, 0) + xp * roll(u[z], -1, 0)
            r.append(f[z] + (side + (ym * roll(u[z], sh, 1) + yp * roll(u[z], -sh, 1))))
        x = solved(r)
        u = [(1.0 - OMEGA) * u[z] + OMEGA * x[z] for z in range(Z)]
    for z in range(Z):
        lev.C[z + 1] = u[z]


def spread_rows(dst, z, c, rows):
    for source, count, target in rows:
        part = c[source : source + count]
        for k in range(2):
            for j in range(2):
                dst[z + k, pl.ds(target + j, count, stride=2), :] = part


def kernel(ngx, ngz, *refs):
    codes_in, charge_in, eps_t, scr_t, out = refs[:5]
    refs = list(refs[5:])

    def take(count):
        got = refs[:count]
        del refs[:count]
        return got

    l0 = Level(0, take(16), False, 4)
    l1 = Level(1, take(16), False, 8)
    l2 = Level(2, take(16), False, 8)
    l3 = Level(3, take(16), True, 4)
    l4 = Level(4, take(16), True, 4)
    l5 = Level(5, take(16), True, 4)
    l6 = Level(6, take(16), True, 2)
    (tmp, codes, charge, s_in, xs, xr, zs, zr, ds, dr, es, f1, red, post_red, ub, rm, ra, av, bv, es3, f3, fh, fr, f2, f2r, ps, rb, pivots, mid) = take(29)
    (s_r1, r_r1, s_es, r_es, s_f1, r_f1, s_red, r_red, s_post, r_post, s_e3, r_e3, s_f3, r_f3, s_f2, r_f2) = take(16)

    gx, gz = lax.axis_index("gx"), lax.axis_index("gz")

    def gx_at(k):
        return lax.rem(gx + (k + ngx), ngx)

    def gz_at(k):
        return lax.rem(gz + (k + ngz), ngz)

    def remote(src, dst, ss, rs, tx, tz):
        return pltpu.make_async_remote_copy(src, dst, ss, rs, device_id=(tx, tz), device_id_type=MESH)

    inputs = (pltpu.make_async_copy(codes_in, codes, s_in.at[0]), pltpu.make_async_copy(charge_in, charge, s_in.at[1]))
    for copy in inputs:
        copy.start()

    barrier = pltpu.get_barrier_semaphore()

    def hello(tx, tz):
        pl.semaphore_signal(barrier, 1, device_id=(tx, tz), device_id_type=MESH)

    loop(ngz - 1, lambda k: hello(gx, gz_at(k + 1)))
    loop(ngz, lambda k: hello(gx_at(1), gz_at(k)))
    loop(ngz, lambda k: hello(gx_at(-1), gz_at(k)))
    loop(ngx - 3, lambda k: hello(gx_at(k + 2), gz))

    row24, row16 = iota((24, 128), 0), iota((16, 128), 0)
    has_right, has_left = gx < ngx - 1, gx > 0
    lane = iota((1, 8, 128), 2)

    table_e = [jnp.full((16, 128), eps_t[k], F32) for k in range(eps_t.shape[0])]
    table_s = [jnp.full((16, 128), scr_t[k], F32) for k in range(eps_t.shape[0])]

    def look(i):
        c = codes[pl.ds(i, 16, stride=16), :]
        e = jnp.zeros((16, 128), F32)
        s = jnp.zeros((16, 128), F32)
        for k in range(eps_t.shape[0]):
            e = jnp.where(c == k, table_e[k], e)
            s = jnp.where(c == k, table_s[k], s)
        l0.E[i + 1, 0:16, :] = e
        l0.S[i, 0:16, :] = s
        l0.F[i, 0:16, :] = charge[pl.ds(i, 16, stride=16), :]

    for copy in inputs:
        copy.wait()
    unrolled(16, look)

    xs[0, :, 0:2, :] = l0.E[1:17, 14:16, :]
    xs[0, :, 2:3, :] = l0.S[:, 15:16, :]
    xs[0, :, 3:4, :] = l0.F[:, 15:16, :]
    xs[1, :, 0:2, :] = l0.E[1:17, 0:2, :]
    xs[1, :, 2:3, :] = l0.S[:, 0:1, :]
    xs[1, :, 3:4, :] = l0.F[:, 0:1, :]
    zs[0] = l0.E[16, 0:16, :]
    zs[1] = l0.E[1, 0:16, :]
    ds[0] = l0.E[16, 8:16, :]
    ds[1] = l0.E[16, 0:8, :]
    ds[2] = l0.E[1, 8:16, :]
    ds[3] = l0.E[1, 0:8, :]

    def pack2(v):
        v = v.reshape(4, 2, 8, 128)
        return jnp.where((lane & 1) == 0, v[:, 0], v[:, 1])

    es[0, gz, 0:4] = pack2(halve(l0.E[1:17, 0:16, :], 0, tmp))
    es[0, gz, 4:8] = pack2(halve(l0.S[:, 0:16, :], 0, tmp, 8))

    def r1_copies():
        return [
            remote(xs.at[0], xr.at[0], s_r1.at[0], r_r1.at[0], gx_at(1), gz),
            remote(xs.at[1], xr.at[1], s_r1.at[1], r_r1.at[1], gx_at(-1), gz),
            remote(zs.at[0], zr.at[0], s_r1.at[2], r_r1.at[2], gx, gz_at(1)),
            remote(zs.at[1], zr.at[1], s_r1.at[3], r_r1.at[3], gx, gz_at(-1)),
            remote(ds.at[0], dr.at[0], s_r1.at[4], r_r1.at[4], gx_at(1), gz_at(1)),
            remote(ds.at[1], dr.at[1], s_r1.at[5], r_r1.at[5], gx_at(-1), gz_at(1)),
            remote(ds.at[2], dr.at[2], s_r1.at[6], r_r1.at[6], gx_at(1), gz_at(-1)),
            remote(ds.at[3], dr.at[3], s_r1.at[7], r_r1.at[7], gx_at(-1), gz_at(-1)),
        ]

    pl.semaphore_wait(barrier, 3 * ngz - 1 + ngx - 3)
    for copy in r1_copies():
        copy.start()

    def f1_copies(act):
        def go(slot, k, src, dst, tx):
            act(remote(src, dst, s_f1.at[slot, k], r_f1.at[slot, gz], tx, gz_at(k)))

        for k in (4, 3, 5, 2, 6, 1, 7, 0):
            if k:
                go(0, k, f1.at[gz], f1.at[gz], gx)
            go(1, k, fh.at[0], fr.at[0, gz], gx_at(1))
            go(2, k, fh.at[1], fr.at[1, gz], gx_at(-1))

    def f1_arrive():
        def get(slot, dst, k):
            p = gz_at(k)
            remote(dst, dst, s_f1.at[slot, k], r_f1.at[slot, p], gx, gz_at(1)).wait_recv()

        loop(ngz - 1, lambda k: get(0, f1.at[gz], k + 1))
        loop(ngz, lambda k: get(1, fr.at[0, gz], k))
        loop(ngz, lambda k: get(2, fr.at[1, gz], k))

    def es_lines(act):
        for k in FAR_FIRST:
            act(remote(es.at[0, gz], es.at[0, gz], s_es.at[0, k], r_es.at[0, gz], gx, gz_at(k)))

    def es_planes():
        return [
            remote(es.at[0], es.at[2], s_es.at[2, 0], r_es.at[2, 0], gx_at(1), gz),
            remote(es.at[0], es.at[1], s_es.at[1, 0], r_es.at[1, 0], gx_at(-1), gz),
        ]

    es_lines(lambda c: c.start())

    for copy in r1_copies():
        copy.wait_recv()

    above, below = gz > 0, gz < ngz - 1
    zero16 = jnp.zeros((16, 24, 128), F32)
    l0.E[0:1] = zero16[0:1]
    l0.E[17:18] = zero16[0:1]
    l0.E[1:17, 16:24, :] = zero16[:, 0:8]
    l0.S[:, 16:24, :] = jnp.ones((16, 8, 128), F32)
    l0.F[:, 16:24, :] = zero16[:, 0:8]
    l0.E[1:17, 22:24, :] = jnp.where(has_left, xr[0, :, 0:2, :], 0.0)
    l0.S[:, 23:24, :] = jnp.where(has_left, xr[0, :, 2:3, :], 1.0)
    l0.F[:, 23:24, :] = jnp.where(has_left, xr[0, :, 3:4, :], 0.0)
    l0.E[1:17, 16:18, :] = jnp.where(has_right, xr[1, :, 0:2, :], 0.0)
    l0.S[:, 16:17, :] = jnp.where(has_right, xr[1, :, 2:3, :], 1.0)
    l0.F[:, 16:17, :] = jnp.where(has_right, xr[1, :, 3:4, :], 0.0)
    l0.E[0, 0:16, :] = jnp.where(above, zr[0], 0.0)
    l0.E[17, 0:16, :] = jnp.where(below, zr[1], 0.0)
    l0.E[0, 23:24, :] = jnp.where(above & has_left, dr[0, 7:8, :], 0.0)
    l0.E[0, 16:17, :] = jnp.where(above & has_right, dr[1, 0:1, :], 0.0)
    l0.E[17, 23:24, :] = jnp.where(below & has_left, dr[2, 7:8, :], 0.0)
    l0.E[17, 16:17, :] = jnp.where(below & has_right, dr[3, 0:1, :], 0.0)

    for i in range(4):
        wzp = couplings(l0, i * 4, 4)
    l0.WZ[16:17] = wzp[3:4]

    m = 1.0 / l0.D[0]
    l0.M[0] = m
    for z in range(1, 15):
        w = l0.WZ[z]
        a = w * m
        m = 1.0 / (l0.D[z] - w * a)
        l0.A[z] = a
        l0.M[z] = m
    lead = jnp.where(above, l0.WZ[0], 0.0)
    tail = l0.WZ[15]

    y = lead
    av[0] = y
    for z in range(1, 15):
        y = l0.A[z] * y
        av[z] = y
    x = l0.M[14] * y
    b = l0.M[14] * tail
    av[14] = x
    bv[14] = b
    for z in range(13, -1, -1):
        x = l0.M[z] * av[z] + l0.A[z + 1] * x
        b = l0.A[z + 1] * b
        av[z] = x
        bv[z] = b

    def inner(src):
        y = src[0]
        l0.Y[0] = y
        for z in range(1, 15):
            y = src[z] + l0.A[z] * y
            l0.Y[z] = y
        x = l0.M[14] * y
        l0.Y[14] = x
        for z in range(13, -1, -1):
            x = l0.M[z] * l0.Y[z] + l0.A[z + 1] * x
            l0.Y[z] = x

    inner(l0.F)

    def put(k, v):
        red[gz, pl.ds(k * 18, 17), :] = v[0:17]
        red[gz, pl.ds(k * 18 + 17, 1), :] = v[23:24]

    put(0, tail * av[14])
    put(1, l0.D[15] - tail * bv[14])
    put(2, lead * av[0])
    put(3, l0.F[15] + tail * l0.Y[14])
    put(4, lead * l0.Y[0])

    def gather(buf, ss, rs, act):
        for k in FAR_FIRST:
            act(remote(buf.at[gz], buf.at[gz], ss.at[k], rs.at[gz], gx, gz_at(k)))

    def post_copies(act):
        for k in FAR_FIRST:
            side = lax.div(gz + k, ngz)
            act(remote(ps.at[side], post_red.at[gz], s_post.at[k], r_post.at[gz], gx, gz_at(k)))

    def gathered(buf, ss, rs):
        def get(k):
            p = gz_at(k)
            remote(buf.at[gz], buf.at[p], ss.at[k], rs.at[p], gx, p).wait_recv()

        loop(ngz - 1, lambda k: get(k + 1))

    gather(red, s_red, r_red, lambda c: c.start())

    def es_line_in(k):
        p = gz_at(k + 1)
        remote(es.at[0, gz], es.at[0, p], s_es.at[0, k + 1], r_es.at[0, p], gx, p).wait_recv()

    loop(ngz - 1, es_line_in)
    for copy in es_planes():
        copy.start()

    mask1 = jnp.where(row24 < 8, 1.0, jnp.where(row24 < 16, jnp.where(has_right, 1.0, 0.0), jnp.where(has_left, 1.0, 0.0)))
    mask2 = jnp.where(
        row16 < 4,
        1.0,
        jnp.where(row16 < 8, jnp.where(has_right, 1.0, 0.0), jnp.where(row16 < 12, 0.0, jnp.where(has_left, 1.0, 0.0))),
    )
    l1.mask, l2.mask = mask1, mask2

    def unpack2(v):
        even = jnp.where((lane & 1) == 0, v, roll(v, 1, 2))
        odd = jnp.where((lane & 1) == 1, v, roll(v, -1, 2))
        return jnp.stack([even, odd], axis=1).reshape(2 * v.shape[0], 8, 128)

    here = (None, has_right, has_left)

    def place(buf, start, dst, offset, outside, slots):
        for slot in slots:
            for p in range(ngz):
                v = unpack2(buf[slot, p, start : start + 4])
                if slot:
                    v = jnp.where(here[slot], v, outside)
                dst[p * 8 + offset : p * 8 + offset + 8, slot * 8 : slot * 8 + 8, :] = v

    place(es, 0, l1.E, 1, 0.0, (0,))
    place(es, 4, l1.S, 0, 1.0, (0,))

    def coarsen(src, offset, fine, coarse, dst, dst_offset, split):
        n = fine.n

        def body(i):
            v = halve(src[i * n + offset : (i + 1) * n + offset], fine.index, tmp, i * (n // 2))
            at = slice(i * (n // 2) + dst_offset, (i + 1) * (n // 2) + dst_offset)
            if split:
                dst[at, 0:8, :] = v[:, 0:8]
                dst[at, 12:16, :] = v[:, 8:12]
            else:
                dst[at] = v

        unrolled(fine.Z // n, body)

    def filler(ref, value):
        ref[:, 8:12, :] = jnp.full((ref.shape[0], 4, 128), value, F32)

    filler(l2.E, 0.0)
    filler(l2.S, 1.0)
    filler(l2.F, 0.0)

    lane3 = iota((4, 2, 128), 2)

    def pack4(src, offset, buf, first):
        for i in range(2):
            v = halve(src[i * 16 + offset : i * 16 + offset + 16], 2, tmp, i * 8)[:, 0:2]
            tmp[i * 8 : i * 8 + 8, 32:34, :] = v
        v = tmp[0:16, 32:34, :].reshape(4, 4, 2, 128)
        k = (lane3 >> 1) & 3
        v = jnp.where(k == 0, v[:, 0], jnp.where(k == 1, v[:, 1], jnp.where(k == 2, v[:, 2], v[:, 3])))
        for zz in range(4):
            buf[gx, first + zz * 2 : first + zz * 2 + 2, :] = v[zz]

    def spread(buf, ss, rs, act):
        loop(ngx - 1, lambda k: act(remote(buf.at[gx], buf.at[gx], ss.at[k + 1], rs.at[gx], gx_at(k + 1), gz)))

    def collected(buf, ss, rs):
        def get(k):
            p = gx_at(k)
            remote(buf.at[gx], buf.at[p], ss.at[k], rs.at[p], p, gz).wait_recv()

        loop(ngx - 1, lambda k: get(k + 1))

    gathered(red, s_red, r_red)

    def got(p, k):
        return red[p, pl.ds(k * 18, 18), :]

    m, y = None, None
    for p in range(ngz):
        diag, right = got(p, 1), got(p, 3)
        if p + 1 < ngz:
            diag, right = diag - got(p + 1, 2), right + got(p + 1, 4)
        if p:
            c = got(p, 0)
            a = c * m
            diag, right = diag - c * a, right + a * y
            ra[p] = a
        m, y = 1.0 / diag, right
        rm[p] = m
        ub[p + 1, 0:18, :] = y
    x = m * y
    for p in range(ngz - 1, -1, -1):
        if p + 1 < ngz:
            x = rm[p] * ub[p + 1, 0:18, :] + ra[p + 1] * x
        ub[p + 1, 0:17, :] = x[0:17]
        ub[p + 1, 23:24, :] = x[17:18]
        ub[p + 1, 17:23, :] = jnp.zeros((6, 128), F32)
    ub[0] = jnp.zeros((24, 128), F32)

    before, own = ub[gz], ub[gz + 1]
    for z in range(15):
        l0.U[z] = OMEGA * (l0.Y[z] + av[z] * before + bv[z] * own)
    l0.U[15] = OMEGA * own

    def first_residual(i):
        z0 = i * 4
        l0.R[pl.ds(z0, 4)] = (1.0 - OMEGA) * l0.F[pl.ds(z0, 4)] + lateral(l0, l0.U[pl.ds(z0, 4)], z0, 4)

    unrolled(4, first_residual)
    packed = pack2(halve(l0.R[:, 0:16, :], 0, tmp))
    f1[gz] = packed
    for zz in range(4):
        fh[0, zz * 4 : zz * 4 + 4, :] = packed[zz, 4:8]
        fh[1, zz * 4 : zz * 4 + 4, :] = packed[zz, 0:4]
    f1_copies(lambda c: c.start())

    q = got(ngz - 1, 1)[0:16]
    pivots[ngz - 1] = q
    for p in range(ngz - 1, 0, -1):
        c = got(p, 0)[0:16]
        b = c * (1.0 / q)
        rb[p] = b
        q = got(p - 1, 1)[0:16] - got(p, 2)[0:16] - c * b
        pivots[p - 1] = q
    rb[0] = jnp.zeros((16, 128), F32)
    c = jnp.where(above, red[gz, 0:16, :], 0.0)
    left = rm[jnp.maximum(gz - 1, 0), 0:16, :]
    mid[0] = left
    mid[1] = c * left
    mid[2] = 1.0 / (pivots[gz] - c * c * left)
    mid[3] = c

    for copy in es_planes():
        copy.wait_recv()
    place(es, 0, l1.E, 1, 0.0, (1, 2))
    place(es, 4, l1.S, 0, 1.0, (1, 2))
    coarsen(l1.E, 1, l1, l2, l2.E, 1, True)
    coarsen(l1.S, 0, l1, l2, l2.S, 0, True)
    pack4(l2.E, 1, es3, 0)
    pack4(l2.S, 0, es3, 8)
    spread(es3, s_e3, r_e3, lambda c: c.start())
    prepare(l1)
    prepare(l2)

    lane32 = iota((32, 128), 1)

    def swap(v, s):
        return jnp.where((lane32 & s) == 0, roll(v, -s, 1), roll(v, s, 1))

    def place4(buf, rows, first, dst, offset):
        for zz in range(4):
            for xp in range(2):
                v = buf[:, first + zz * 2 + xp, :]
                w = swap(v, 2)
                for k0 in range(2):
                    v1 = jnp.where(((lane32 >> 1) & 1) == k0, v, w)
                    w1 = swap(v1, 4)
                    for k1 in range(2):
                        v2 = jnp.where(((lane32 >> 2) & 1) == k1, v1, w1)
                        dst[offset + zz * 4 + k1 * 2 + k0, pl.ds(xp, ngx, stride=2), :] = v2

    l1.F[:, 8:24, :] = jnp.zeros((l1.Z, 16, 128), F32)
    lane16 = iota((16, 128), 1)
    f1_arrive()
    for p in range(ngz):
        l1.F[p * 8 : p * 8 + 8, 0:8, :] = unpack2(f1[p])
        for side, present, row in ((0, has_left, 20), (1, has_right, 8)):
            v = jnp.where(present, fr[side, p], 0.0)
            both = (jnp.where((lane16 & 1) == 0, v, roll(v, 1, 1)), jnp.where((lane16 & 1) == 1, v, roll(v, -1, 1)))
            for zz in range(4):
                for k in range(2):
                    l1.F[p * 8 + zz * 2 + k, row : row + 4, :] = both[k][zz * 4 : zz * 4 + 4]
    pre(l1)
    coarsen(l1.R, 0, l1, l2, l2.F, 0, True)
    pre(l2)
    pack4(l2.R, 0, f3, 0)
    spread(f3, s_f3, r_f3, lambda c: c.start())

    lane8 = iota((8, 8, 128), 2)
    v = l2.F[:, 0:8, :].reshape(8, 4, 8, 128)
    k = lane8 & 3
    f2[...] = jnp.where(k == 0, v[:, 0], jnp.where(k == 1, v[:, 1], jnp.where(k == 2, v[:, 2], v[:, 3])))

    def f2_copies():
        return [
            remote(f2, f2r.at[0], s_f2.at[0], r_f2.at[0], gx_at(1), gz),
            remote(f2, f2r.at[1], s_f2.at[1], r_f2.at[1], gx_at(-1), gz),
        ]

    for copy in f2_copies():
        copy.start()

    collected(es3, s_e3, r_e3)
    place4(es3, 16, 0, l3.E, 1)
    place4(es3, 16, 8, l3.S, 0)
    deep = [l3, l4, l5, l6]
    for fine, coarse in zip(deep[:-1], deep[1:]):
        coarsen(fine.E, 1, fine, coarse, coarse.E, 1, False)
        coarsen(fine.S, 0, fine, coarse, coarse.S, 0, False)
    for lev in deep:
        prepare(lev)

    for copy in f2_copies():
        copy.wait_recv()

    def swap8(v, s):
        return jnp.where((lane8 & s) == 0, roll(v, -s, 2), roll(v, s, 2))

    for side, present, source, row in ((0, has_left, 2, 14), (1, has_right, 1, 5)):
        v = jnp.where(present, f2r[side], 0.0)
        w = swap8(v, 1)
        for k0 in range(2):
            v1 = jnp.where((lane8 & 1) == k0, v, w)
            w1 = swap8(v1, 2)
            for k1 in range(2):
                v2 = jnp.where(((lane8 >> 1) & 1) == k1, v1, w1)
                for zz in range(8):
                    l2.F[zz * 4 + k1 * 2 + k0, row : row + 1, :] = v2[zz, source : source + 1]
    pre(l2)

    collected(f3, s_f3, r_f3)
    place4(f3, 8, 0, l3.F, 0)
    for fine, coarse in zip(deep[:-1], deep[1:]):
        pre(fine)
        coarsen(fine.R, 0, fine, coarse, coarse.F, 0, False)
    coarsest(l6)
    for fine, coarse in zip(deep[-2::-1], deep[:0:-1]):
        unrolled(coarse.Z, lambda z, fine=fine, coarse=coarse: spread_rows(fine.V, 2 * z + 1, coarse.C[z + 1], ((0, coarse.X, 0),)))
        post(fine)

    tiles = ngx // 4
    first = gx // 4
    shift = lax.rem(24 - 2 * lax.rem(gx, 4), 24)

    def tile_at(z, k):
        return l3.C[z, pl.ds(pl.multiple_of(lax.rem(first + (k + tiles), tiles) * 8, 8), 8), :]

    right_rows, left_rows = (iota((4, 128), 0) < 2) | has_right, has_left

    def down3(z):
        c = jnp.concatenate([tile_at(z + 1, 0), tile_at(z + 1, 1), tile_at(z + 1, -1)], axis=0)
        c = pltpu.roll(c, shift, 0)
        for k in range(2):
            for j in range(2):
                l2.V[2 * z + 1 + k, pl.ds(j, 4, stride=2), :] = jnp.where(right_rows, c[0:4], 0.0)
                l2.V[2 * z + 1 + k, pl.ds(12 + j, 2, stride=2), :] = jnp.where(left_rows, c[22:24], 0.0)

    filler(l2.V, 0.0)
    unrolled(l3.Z, down3)
    post(l2)
    unrolled(l2.Z, lambda z: spread_rows(l1.V, 2 * z + 1, l2.C[z + 1], ((0, 4, 0), (4, 4, 8), (12, 4, 16))))
    post(l1)
    l1.C[0] = jnp.zeros((24, 128), F32)
    l1.C[l1.Z + 1] = jnp.zeros((24, 128), F32)

    for i in range(10):
        c = l1.C[gz * 8 + i]
        for z in (2 * i - 1, 2 * i):
            if 0 <= z < 18:
                for j in range(2):
                    l0.V[z, pl.ds(j, 8, stride=2), :] = c[0:8]
                l0.V[z, 16:17, :] = c[8:9]
                l0.V[z, 17:23, :] = jnp.zeros((6, 128), F32)
                l0.V[z, 23:24, :] = c[23:24]

    def second_residual(i):
        z0 = i * 4
        v = l0.V[pl.ds(z0 + 1, 4)]
        around = lateral(l0, v, z0, 4) + l0.WZ[pl.ds(z0, 4)] * l0.V[pl.ds(z0, 4)] + l0.WZ[pl.ds(z0 + 1, 4)] * l0.V[pl.ds(z0 + 2, 4)]
        l0.F[pl.ds(z0, 4)] = l0.R[pl.ds(z0, 4)] - (l0.D[pl.ds(z0, 4)] * v - around)

    unrolled(4, second_residual)
    inner(l0.F)
    end_row, first_row = (l0.F[15] + tail * l0.Y[14])[0:16], (lead * l0.Y[0])[0:16]
    ps[0] = end_row + jnp.where(above, ra[gz, 0:16, :], 0.0) * first_row
    ps[1] = first_row + rb[gz] * end_row
    post_red[gz] = jnp.zeros((16, 128), F32)
    post_copies(lambda c: c.start())
    for z in range(16):
        l0.U[z, 0:16, :] = l0.U[z, 0:16, :] + l0.V[z + 1, 0:16, :]
    gathered(post_red, s_post, r_post)
    tau = jnp.zeros((16, 128), F32)
    for p in range(ngz - 1):
        took = post_red[p] if p == 0 else post_red[p] + ra[p, 0:16, :] * tau
        tau = jnp.where(p < gz, took, tau)
    sigma = jnp.zeros((16, 128), F32)
    for p in range(ngz - 1, 0, -1):
        sigma = jnp.where(p > gz, post_red[p] + rb[p] * sigma, sigma)
    b1 = first_row + tau
    own = mid[2] * (end_row + sigma + mid[1] * b1)
    before = mid[0] * (b1 + mid[3] * own)
    for z in range(16):
        if z < 15:
            x = l0.Y[z, 0:16, :] + av[z, 0:16, :] * before + bv[z, 0:16, :] * own
        else:
            x = own
        out[pl.ds(z, 16, stride=16), :] = l0.U[z, 0:16, :] + OMEGA * x

    for copy in r1_copies():
        copy.wait_send()
    es_lines(lambda c: c.wait_send())
    for copy in es_planes():
        copy.wait_send()
    f1_copies(lambda c: c.wait_send())
    for copy in f2_copies():
        copy.wait_send()
    gather(red, s_red, r_red, lambda c: c.wait_send())
    post_copies(lambda c: c.wait_send())
    spread(es3, s_e3, r_e3, lambda c: c.wait_send())
    spread(f3, s_f3, r_f3, lambda c: c.wait_send())


def solution(mesh):
    ngx, ngz = mesh.shape["gx"], mesh.shape["gz"]

    def per_device(charge, codes, eps_table, screen_table):
        nx, nz, ny = charge.shape
        whole_z, whole_x = nz * ngz, nx * ngx
        levels = [
            (nz, 24),
            (whole_z // 2, 24),
            (whole_z // 4, 16),
            (whole_z // 8, whole_x // 8),
            (whole_z // 16, whole_x // 16),
            (whole_z // 32, whole_x // 32),
            (whole_z // 64, whole_x // 64),
        ]
        scratch = []
        for Z, X in levels:
            scratch += Level.scratch(Z, X)
        vm = lambda *shape: pltpu.VMEM(shape, F32)
        scratch += [
            vm(64, 64, 128),
            pltpu.VMEM((nx * nz, ny), jnp.int32),
            vm(nx * nz, ny),
            pltpu.SemaphoreType.DMA((2,)),
            vm(2, 16, 4, 128),
            vm(2, 16, 4, 128),
            vm(2, 16, 128),
            vm(2, 16, 128),
            vm(4, 8, 128),
            vm(4, 8, 128),
            vm(3, ngz, 8, 8, 128),
            vm(ngz, 4, 8, 128),
            vm(ngz, 96, 128),
            vm(ngz, 16, 128),
            vm(ngz + 1, 24, 128),
            vm(ngz, 18, 128),
            vm(ngz, 18, 128),
            vm(16, 24, 128),
            vm(16, 24, 128),
            vm(ngx, 16, 128),
            vm(ngx, 8, 128),
            vm(2, 16, 128),
            vm(2, ngz, 16, 128),
            vm(8, 8, 128),
            vm(2, 8, 8, 128),
            vm(2, 16, 128),
            vm(ngz, 16, 128),
            vm(ngz, 16, 128),
            vm(4, 16, 128),
        ]
        for shape in ((8,), (3, ngz), (3, ngz), (ngz,), (ngz,), (ngx,), (ngx,), (2,)):
            scratch += [pltpu.SemaphoreType.DMA(shape)] * 2
        result = pl.pallas_call(
            lambda *refs: kernel(ngx, ngz, *refs),
            out_shape=jax.ShapeDtypeStruct((nx * nz, ny), F32),
            in_specs=[
                pl.BlockSpec(memory_space=pl.ANY),
                pl.BlockSpec(memory_space=pl.ANY),
                pl.BlockSpec(memory_space=pltpu.SMEM),
                pl.BlockSpec(memory_space=pltpu.SMEM),
            ],
            out_specs=pl.BlockSpec(memory_space=pltpu.VMEM),
            scratch_shapes=scratch,
            compiler_params=pltpu.CompilerParams(collective_id=0, has_side_effects=True, vmem_limit_bytes=55040 << 10),
            name="vcycle",
        )(codes.reshape(nx * nz, ny), charge.reshape(nx * nz, ny), eps_table, screen_table)
        return result.reshape(nx, nz, ny)

    return jax.shard_map(
        per_device,
        mesh=mesh,
        in_specs=(P("gx", "gz", None), P("gx", "gz", None), P(), P()),
        out_specs=P("gx", "gz", None),
        check_vma=False,
    )
```

```python
import jax
import jax.numpy as jnp
from jax import lax
from jax.experimental import pallas as pl
from jax.experimental.pallas import tpu as pltpu
from jax.sharding import PartitionSpec as P

OMEGA = 0.8
SWEEPS = 8
LAST = 6
F32 = jnp.float32
MESH = pl.DeviceIdType.MESH
FAR_FIRST = (4, 3, 5, 2, 6, 1, 7)


def iota(shape, dim):
    return lax.broadcasted_iota(jnp.int32, shape, dim)


def roll(v, shift, axis):
    size = v.shape[axis]
    return pltpu.roll(v, shift % size, axis)


class Level:
    def __init__(self, index, refs, whole, slab):
        (self.E, self.S, self.WXM, self.WXP, self.WYM, self.WYP, self.WZ, self.D, self.A, self.M, self.F, self.U, self.R, self.Y,
         self.V, self.C) = refs
        self.index, self.whole, self.n = index, whole, slab
        self.Z, self.X = self.S.shape[0], self.S.shape[1]
        self.mask = None

    @staticmethod
    def scratch(Z, X):
        sizes = (Z + 2, Z, Z, Z, Z, Z, Z + 1, Z, Z + 1, Z, Z, Z, Z, Z, Z + 2, Z + 2)
        return [pltpu.VMEM((s, X, 128), F32) for s in sizes]


def loop(count, body):
    def step(i, carry):
        body(i)
        return carry

    lax.fori_loop(0, count, step, 0)


def unrolled(count, body):
    for i in range(count):
        body(i)


def couplings(lev, z0, n):
    h = 0.5 ** lev.index * 0.5
    sh = 2 ** lev.index
    X = lev.X
    e = lev.E[pl.ds(z0 + 1, n)]
    lane = iota((n, X, 128), 2)
    first, last = lane < sh, lane >= 128 - sh
    up, down = roll(e, 1, 1), roll(e, -1, 1)
    if lev.whole:
        row = iota((n, X, 128), 1)
        up, down = jnp.where(row == 0, 0.0, up), jnp.where(row == X - 1, 0.0, down)
    left, right = jnp.where(first, 0.0, roll(e, sh, 2)), jnp.where(last, 0.0, roll(e, -sh, 2))
    wxm, wxp, wym, wyp = h * (e + up), h * (e + down), h * (e + left), h * (e + right)
    wzm, wzp = h * (e + lev.E[pl.ds(z0, n)]), h * (e + lev.E[pl.ds(z0 + 2, n)])
    lev.D[pl.ds(z0, n)] = wxm + wxp + wzm + wzp + wym + wyp + lev.S[pl.ds(z0, n)]
    if lev.whole:
        wxm, wxp = jnp.where(row == 0, 0.0, wxm), jnp.where(row == X - 1, 0.0, wxp)
    lev.WXM[pl.ds(z0, n)] = wxm
    lev.WXP[pl.ds(z0, n)] = wxp
    lev.WYM[pl.ds(z0, n)] = jnp.where(first, 0.0, wym)
    lev.WYP[pl.ds(z0, n)] = jnp.where(last, 0.0, wyp)
    lev.WZ[pl.ds(z0, n)] = wzm
    return wzp


def lateral(lev, u, z0, n):
    sh = 2 ** lev.index
    return (
        lev.WXM[pl.ds(z0, n)] * roll(u, 1, 1)
        + lev.WXP[pl.ds(z0, n)] * roll(u, -1, 1)
        + lev.WYM[pl.ds(z0, n)] * roll(u, sh, 2)
        + lev.WYP[pl.ds(z0, n)] * roll(u, -sh, 2)
    )


def steps_of(count):
    for s in (8, 4, 2):
        if count % s == 0:
            return s
    return 1


def prepare(lev):
    Z, X, n = lev.Z, lev.X, lev.n
    zero = jnp.zeros((1, X, 128), F32)
    lev.E[0:1] = zero
    lev.E[Z + 1 : Z + 2] = zero
    (loop if Z // n > 8 else unrolled)(Z // n, lambda i: couplings(lev, i * n, n))
    lev.WZ[0:1] = zero
    lev.WZ[Z : Z + 1] = zero
    lev.A[Z : Z + 1] = zero
    s = steps_of(Z)

    def body(i, m):
        for j in range(s):
            z = i * s + j
            w = lev.WZ[z]
            a = w * m
            m = 1.0 / (lev.D[z] - w * a)
            lev.A[z] = a
            lev.M[z] = m
        return m

    lax.fori_loop(0, Z // s, body, jnp.zeros((X, 128), F32))


def sweep(lev, src, finish):
    Z, X = lev.Z, lev.X
    s = steps_of(Z)

    def forward(i, y):
        for j in range(s):
            z = i * s + j
            y = src[z] + lev.A[z] * y
            lev.Y[z] = y
        return y

    def backward(i, x):
        for j in range(s):
            z = Z - 1 - (i * s + j)
            x = lev.M[z] * lev.Y[z] + lev.A[z + 1] * x
            finish(z, x)
        return x

    lax.fori_loop(0, Z // s, forward, jnp.zeros((X, 128), F32))
    lax.fori_loop(0, Z // s, backward, jnp.zeros((X, 128), F32))


def pair_lanes(v, index):
    sh = 2 ** index
    lane = iota(v.shape, v.ndim - 1)
    other = jnp.where((lane & sh) == 0, roll(v, -sh, v.ndim - 1), roll(v, sh, v.ndim - 1))
    return v + other


def halve(v, index, tmp, at=0):
    n, X = v.shape[0], v.shape[1]
    v = v.reshape(n // 2, 2, X, 128)
    v = pair_lanes(v[:, 0] + v[:, 1], index)
    part = slice(at, at + n // 2)
    tmp[part, 0:X, :] = v
    return 0.125 * (tmp[part, pl.ds(0, X // 2, stride=2), :] + tmp[part, pl.ds(1, X // 2, stride=2), :])


def pre(lev):
    def finish(z, x):
        lev.U[z] = OMEGA * x

    sweep(lev, lev.F, finish)
    n = lev.n

    def body(i):
        z0 = i * n
        r = (1.0 - OMEGA) * lev.F[pl.ds(z0, n)] + lateral(lev, lev.U[pl.ds(z0, n)], z0, n)
        if lev.mask is not None:
            r = jnp.where(lev.mask[None] > 0, r, 0.0)
        lev.R[pl.ds(z0, n)] = r

    unrolled(lev.Z // n, body)


def post(lev):
    n, Z = lev.n, lev.Z
    zero = jnp.zeros((1, lev.X, 128), F32)
    lev.V[0:1] = zero
    lev.V[Z + 1 : Z + 2] = zero

    def body(i):
        z0 = i * n
        v = lev.V[pl.ds(z0 + 1, n)]
        around = lateral(lev, v, z0, n) + lev.WZ[pl.ds(z0, n)] * lev.V[pl.ds(z0, n)] + lev.WZ[pl.ds(z0 + 1, n)] * lev.V[pl.ds(z0 + 2, n)]
        r = lev.R[pl.ds(z0, n)] - (lev.D[pl.ds(z0, n)] * v - around)
        if lev.mask is not None:
            r = jnp.where(lev.mask[None] > 0, r, 0.0)
        lev.F[pl.ds(z0, n)] = r

    unrolled(Z // n, body)

    def finish(z, x):
        lev.C[z + 1] = lev.U[z] + lev.V[z + 1] + OMEGA * x

    sweep(lev, lev.F, finish)


def coarsest(lev):
    Z = lev.Z
    sh = 2 ** lev.index
    f = [lev.F[z] for z in range(Z)]
    a = [lev.A[z] for z in range(Z + 1)]
    m = [lev.M[z] for z in range(Z)]
    w = [(lev.WXM[z], lev.WXP[z], lev.WYM[z], lev.WYP[z]) for z in range(Z)]

    def solved(r):
        y = [r[0]]
        for z in range(1, Z):
            y.append(r[z] + a[z] * y[-1])
        x = [None] * Z
        x[Z - 1] = m[Z - 1] * y[Z - 1]
        for z in range(Z - 2, -1, -1):
            x[z] = m[z] * y[z] + a[z + 1] * x[z + 1]
        return x

    u = [OMEGA * x for x in solved(f)]
    for _ in range(SWEEPS - 1):
        r = []
        for z in range(Z):
            xm, xp, ym, yp = w[z]
            side = xm * roll(u[z], 1, 0) + xp * roll(u[z], -1, 0)
            r.append(f[z] + (side + (ym * roll(u[z], sh, 1) + yp * roll(u[z], -sh, 1))))
        x = solved(r)
        u = [(1.0 - OMEGA) * u[z] + OMEGA * x[z] for z in range(Z)]
    for z in range(Z):
        lev.C[z + 1] = u[z]


def spread_rows(dst, z, c, rows):
    for source, count, target in rows:
        part = c[source : source + count]
        for k in range(2):
            for j in range(2):
                dst[z + k, pl.ds(target + j, count, stride=2), :] = part


def kernel(ngx, ngz, *refs):
    codes_in, charge_in, eps_t, scr_t, out = refs[:5]
    refs = list(refs[5:])

    def take(count):
        got = refs[:count]
        del refs[:count]
        return got

    l0 = Level(0, take(16), False, 4)
    l1 = Level(1, take(16), False, 8)
    l2 = Level(2, take(16), False, 8)
    l3 = Level(3, take(16), True, 4)
    l4 = Level(4, take(16), True, 4)
    l5 = Level(5, take(16), True, 4)
    l6 = Level(6, take(16), True, 2)
    (tmp, codes, charge, s_in, xs, xr, zs, zr, ds, dr, es, f1, red, post_red, ub, rm, ra, av, bv, es3, f3, fh, fr, f2, f2r, ps, rb, pivots, mid) = take(29)
    (s_r1, r_r1, s_es, r_es, s_f1, r_f1, s_red, r_red, s_post, r_post, s_e3, r_e3, s_f3, r_f3, s_f2, r_f2) = take(16)

    gx, gz = lax.axis_index("gx"), lax.axis_index("gz")

    def gx_at(k):
        return lax.rem(gx + (k + ngx), ngx)

    def gz_at(k):
        return lax.rem(gz + (k + ngz), ngz)

    def remote(src, dst, ss, rs, tx, tz):
        return pltpu.make_async_remote_copy(src, dst, ss, rs, device_id=(tx, tz), device_id_type=MESH)

    inputs = (pltpu.make_async_copy(codes_in, codes, s_in.at[0]), pltpu.make_async_copy(charge_in, charge, s_in.at[1]))
    for copy in inputs:
        copy.start()

    barrier = pltpu.get_barrier_semaphore()

    def hello(tx, tz):
        pl.semaphore_signal(barrier, 1, device_id=(tx, tz), device_id_type=MESH)

    loop(ngz - 1, lambda k: hello(gx, gz_at(k + 1)))
    loop(ngz, lambda k: hello(gx_at(1), gz_at(k)))
    loop(ngz, lambda k: hello(gx_at(-1), gz_at(k)))
    loop(ngx - 3, lambda k: hello(gx_at(k + 2), gz))

    row24, row16 = iota((24, 128), 0), iota((16, 128), 0)
    has_right, has_left = gx < ngx - 1, gx > 0
    lane = iota((1, 8, 128), 2)

    table_e = [jnp.full((16, 128), eps_t[k], F32) for k in range(eps_t.shape[0])]
    table_s = [jnp.full((16, 128), scr_t[k], F32) for k in range(eps_t.shape[0])]

    def look(i):
        c = codes[pl.ds(i, 16, stride=16), :]
        e = jnp.zeros((16, 128), F32)
        s = jnp.zeros((16, 128), F32)
        for k in range(eps_t.shape[0]):
            e = jnp.where(c == k, table_e[k], e)
            s = jnp.where(c == k, table_s[k], s)
        l0.E[i + 1, 0:16, :] = e
        l0.S[i, 0:16, :] = s
        l0.F[i, 0:16, :] = charge[pl.ds(i, 16, stride=16), :]

    for copy in inputs:
        copy.wait()
    unrolled(16, look)

    xs[0, :, 0:2, :] = l0.E[1:17, 14:16, :]
    xs[0, :, 2:3, :] = l0.S[:, 15:16, :]
    xs[0, :, 3:4, :] = l0.F[:, 15:16, :]
    xs[1, :, 0:2, :] = l0.E[1:17, 0:2, :]
    xs[1, :, 2:3, :] = l0.S[:, 0:1, :]
    xs[1, :, 3:4, :] = l0.F[:, 0:1, :]
    zs[0] = l0.E[16, 0:16, :]
    zs[1] = l0.E[1, 0:16, :]
    ds[0] = l0.E[16, 8:16, :]
    ds[1] = l0.E[16, 0:8, :]
    ds[2] = l0.E[1, 8:16, :]
    ds[3] = l0.E[1, 0:8, :]

    def pack2(v):
        v = v.reshape(4, 2, 8, 128)
        return jnp.where((lane & 1) == 0, v[:, 0], v[:, 1])

    es[0, gz, 0:4] = pack2(halve(l0.E[1:17, 0:16, :], 0, tmp))
    es[0, gz, 4:8] = pack2(halve(l0.S[:, 0:16, :], 0, tmp, 8))

    def r1_copies():
        return [
            remote(xs.at[0], xr.at[0], s_r1.at[0], r_r1.at[0], gx_at(1), gz),
            remote(xs.at[1], xr.at[1], s_r1.at[1], r_r1.at[1], gx_at(-1), gz),
            remote(zs.at[0], zr.at[0], s_r1.at[2], r_r1.at[2], gx, gz_at(1)),
            remote(zs.at[1], zr.at[1], s_r1.at[3], r_r1.at[3], gx, gz_at(-1)),
            remote(ds.at[0], dr.at[0], s_r1.at[4], r_r1.at[4], gx_at(1), gz_at(1)),
            remote(ds.at[1], dr.at[1], s_r1.at[5], r_r1.at[5], gx_at(-1), gz_at(1)),
            remote(ds.at[2], dr.at[2], s_r1.at[6], r_r1.at[6], gx_at(1), gz_at(-1)),
            remote(ds.at[3], dr.at[3], s_r1.at[7], r_r1.at[7], gx_at(-1), gz_at(-1)),
        ]

    pl.semaphore_wait(barrier, 3 * ngz - 1 + ngx - 3)
    for copy in r1_copies():
        copy.start()

    def f1_copies(act):
        def go(slot, k, src, dst, tx):
            act(remote(src, dst, s_f1.at[slot, k], r_f1.at[slot, gz], tx, gz_at(k)))

        for k in (4, 3, 5, 2, 6, 1, 7, 0):
            if k:
                go(0, k, f1.at[gz], f1.at[gz], gx)
            go(1, k, fh.at[0], fr.at[0, gz], gx_at(1))
            go(2, k, fh.at[1], fr.at[1, gz], gx_at(-1))

    def f1_arrive():
        def get(slot, dst, k):
            p = gz_at(k)
            remote(dst, dst, s_f1.at[slot, k], r_f1.at[slot, p], gx, gz_at(1)).wait_recv()

        loop(ngz - 1, lambda k: get(0, f1.at[gz], k + 1))
        loop(ngz, lambda k: get(1, fr.at[0, gz], k))
        loop(ngz, lambda k: get(2, fr.at[1, gz], k))

    def es_lines(act):
        for k in FAR_FIRST:
            act(remote(es.at[0, gz], es.at[0, gz], s_es.at[0, k], r_es.at[0, gz], gx, gz_at(k)))

    def es_planes():
        return [
            remote(es.at[0], es.at[2], s_es.at[2, 0], r_es.at[2, 0], gx_at(1), gz),
            remote(es.at[0], es.at[1], s_es.at[1, 0], r_es.at[1, 0], gx_at(-1), gz),
        ]

    es_lines(lambda c: c.start())

    for copy in r1_copies():
        copy.wait_recv()

    above, below = gz > 0, gz < ngz - 1
    zero16 = jnp.zeros((16, 24, 128), F32)
    l0.E[0:1] = zero16[0:1]
    l0.E[17:18] = zero16[0:1]
    l0.E[1:17, 16:24, :] = zero16[:, 0:8]
    l0.S[:, 16:24, :] = jnp.ones((16, 8, 128), F32)
    l0.F[:, 16:24, :] = zero16[:, 0:8]
    l0.E[1:17, 22:24, :] = jnp.where(has_left, xr[0, :, 0:2, :], 0.0)
    l0.S[:, 23:24, :] = jnp.where(has_left, xr[0, :, 2:3, :], 1.0)
    l0.F[:, 23:24, :] = jnp.where(has_left, xr[0, :, 3:4, :], 0.0)
    l0.E[1:17, 16:18, :] = jnp.where(has_right, xr[1, :, 0:2, :], 0.0)
    l0.S[:, 16:17, :] = jnp.where(has_right, xr[1, :, 2:3, :], 1.0)
    l0.F[:, 16:17, :] = jnp.where(has_right, xr[1, :, 3:4, :], 0.0)
    l0.E[0, 0:16, :] = jnp.where(above, zr[0], 0.0)
    l0.E[17, 0:16, :] = jnp.where(below, zr[1], 0.0)
    l0.E[0, 23:24, :] = jnp.where(above & has_left, dr[0, 7:8, :], 0.0)
    l0.E[0, 16:17, :] = jnp.where(above & has_right, dr[1, 0:1, :], 0.0)
    l0.E[17, 23:24, :] = jnp.where(below & has_left, dr[2, 7:8, :], 0.0)
    l0.E[17, 16:17, :] = jnp.where(below & has_right, dr[3, 0:1, :], 0.0)

    for i in range(4):
        wzp = couplings(l0, i * 4, 4)
    l0.WZ[16:17] = wzp[3:4]

    m = 1.0 / l0.D[0]
    l0.M[0] = m
    for z in range(1, 15):
        w = l0.WZ[z]
        a = w * m
        m = 1.0 / (l0.D[z] - w * a)
        l0.A[z] = a
        l0.M[z] = m
    lead = jnp.where(above, l0.WZ[0], 0.0)
    tail = l0.WZ[15]

    y = lead
    av[0] = y
    for z in range(1, 15):
        y = l0.A[z] * y
        av[z] = y
    x = l0.M[14] * y
    b = l0.M[14] * tail
    av[14] = x
    bv[14] = b
    for z in range(13, -1, -1):
        x = l0.M[z] * av[z] + l0.A[z + 1] * x
        b = l0.A[z + 1] * b
        av[z] = x
        bv[z] = b

    def inner(src):
        y = src[0]
        l0.Y[0] = y
        for z in range(1, 15):
            y = src[z] + l0.A[z] * y
            l0.Y[z] = y
        x = l0.M[14] * y
        l0.Y[14] = x
        for z in range(13, -1, -1):
            x = l0.M[z] * l0.Y[z] + l0.A[z + 1] * x
            l0.Y[z] = x

    inner(l0.F)

    def put(k, v):
        red[gz, pl.ds(k * 18, 17), :] = v[0:17]
        red[gz, pl.ds(k * 18 + 17, 1), :] = v[23:24]

    put(0, tail * av[14])
    put(1, l0.D[15] - tail * bv[14])
    put(2, lead * av[0])
    put(3, l0.F[15] + tail * l0.Y[14])
    put(4, lead * l0.Y[0])

    def gather(buf, ss, rs, act):
        for k in FAR_FIRST:
            act(remote(buf.at[gz], buf.at[gz], ss.at[k], rs.at[gz], gx, gz_at(k)))

    def post_copies(act):
        for k in FAR_FIRST:
            side = lax.div(gz + k, ngz)
            act(remote(ps.at[side], post_red.at[gz], s_post.at[k], r_post.at[gz], gx, gz_at(k)))

    def gathered(buf, ss, rs):
        def get(k):
            p = gz_at(k)
            remote(buf.at[gz], buf.at[p], ss.at[k], rs.at[p], gx, p).wait_recv()

        loop(ngz - 1, lambda k: get(k + 1))

    gather(red, s_red, r_red, lambda c: c.start())

    def es_line_in(k):
        p = gz_at(k + 1)
        remote(es.at[0, gz], es.at[0, p], s_es.at[0, k + 1], r_es.at[0, p], gx, p).wait_recv()

    loop(ngz - 1, es_line_in)
    for copy in es_planes():
        copy.start()

    mask1 = jnp.where(row24 < 8, 1.0, jnp.where(row24 < 16, jnp.where(has_right, 1.0, 0.0), jnp.where(has_left, 1.0, 0.0)))
    mask2 = jnp.where(
        row16 < 4,
        1.0,
        jnp.where(row16 < 8, jnp.where(has_right, 1.0, 0.0), jnp.where(row16 < 12, 0.0, jnp.where(has_left, 1.0, 0.0))),
    )
    l1.mask, l2.mask = mask1, mask2

    def unpack2(v):
        even = jnp.where((lane & 1) == 0, v, roll(v, 1, 2))
        odd = jnp.where((lane & 1) == 1, v, roll(v, -1, 2))
        return jnp.stack([even, odd], axis=1).reshape(2 * v.shape[0], 8, 128)

    here = (None, has_right, has_left)

    def place(buf, start, dst, offset, outside, slots):
        for slot in slots:
            for p in range(ngz):
                v = unpack2(buf[slot, p, start : start + 4])
                if slot:
                    v = jnp.where(here[slot], v, outside)
                dst[p * 8 + offset : p * 8 + offset + 8, slot * 8 : slot * 8 + 8, :] = v

    place(es, 0, l1.E, 1, 0.0, (0,))
    place(es, 4, l1.S, 0, 1.0, (0,))

    def coarsen(src, offset, fine, coarse, dst, dst_offset, split):
        n = fine.n

        def body(i):
            v = halve(src[i * n + offset : (i + 1) * n + offset], fine.index, tmp, i * (n // 2))
            at = slice(i * (n // 2) + dst_offset, (i + 1) * (n // 2) + dst_offset)
            if split:
                dst[at, 0:8, :] = v[:, 0:8]
                dst[at, 12:16, :] = v[:, 8:12]
            else:
                dst[at] = v

        unrolled(fine.Z // n, body)

    def filler(ref, value):
        ref[:, 8:12, :] = jnp.full((ref.shape[0], 4, 128), value, F32)

    filler(l2.E, 0.0)
    filler(l2.S, 1.0)
    filler(l2.F, 0.0)

    lane3 = iota((2, 2, 128), 2)

    def pack8(src, offset, buf, first):
        for i in range(2):
            v = halve(src[i * 16 + offset : i * 16 + offset + 16], 2, tmp, i * 8)[:, 0:2]
            tmp[i * 8 : i * 8 + 8, 32:34, :] = v
        v = tmp[0:16, 32:34, :].reshape(2, 8, 2, 128)
        picked = v[:, 7]
        for k in range(7):
            picked = jnp.where((lane3 & 7) == k, v[:, k], picked)
        for zz in range(2):
            buf[gx, first + zz * 2 : first + zz * 2 + 2, :] = picked[zz]

    core, x4, y4 = lax.rem(gx, 2), lax.rem(lax.div(gx, 2), 4), lax.div(gx, 8)
    hops = sorted(((dy, dx, dc) for dy in range(4) for dx in range(4) for dc in range(2)), key=lambda t: -(min(t[0], 4 - t[0]) + min(t[1], 4 - t[1]) + 0.5 * t[2]))
    far_gx = [lax.rem(y4 + dy, 4) * 8 + lax.rem(x4 + dx, 4) * 2 + lax.rem(core + dc, 2) for dy, dx, dc in hops[:-1]]

    def spread(buf, ss, rs, act):
        for i, tx in enumerate(far_gx):
            act(remote(buf.at[gx], buf.at[gx], ss.at[i], rs.at[gx], tx, gz))

    def collected(buf, ss, rs):
        def get(k):
            p = gx_at(k)
            remote(buf.at[gx], buf.at[p], ss.at[k], rs.at[p], p, gz).wait_recv()

        loop(ngx - 1, lambda k: get(k + 1))

    gathered(red, s_red, r_red)

    def got(p, k):
        return red[p, pl.ds(k * 18, 18), :]

    m, y = None, None
    for p in range(ngz):
        diag, right = got(p, 1), got(p, 3)
        if p + 1 < ngz:
            diag, right = diag - got(p + 1, 2), right + got(p + 1, 4)
        if p:
            c = got(p, 0)
            a = c * m
            diag, right = diag - c * a, right + a * y
            ra[p] = a
        m, y = 1.0 / diag, right
        rm[p] = m
        ub[p + 1, 0:18, :] = y
    x = m * y
    for p in range(ngz - 1, -1, -1):
        if p + 1 < ngz:
            x = rm[p] * ub[p + 1, 0:18, :] + ra[p + 1] * x
        ub[p + 1, 0:17, :] = x[0:17]
        ub[p + 1, 23:24, :] = x[17:18]
        ub[p + 1, 17:23, :] = jnp.zeros((6, 128), F32)
    ub[0] = jnp.zeros((24, 128), F32)

    before, own = ub[gz], ub[gz + 1]
    for z in range(15):
        l0.U[z] = OMEGA * (l0.Y[z] + av[z] * before + bv[z] * own)
    l0.U[15] = OMEGA * own

    def first_residual(i):
        z0 = i * 4
        l0.R[pl.ds(z0, 4)] = (1.0 - OMEGA) * l0.F[pl.ds(z0, 4)] + lateral(l0, l0.U[pl.ds(z0, 4)], z0, 4)

    unrolled(4, first_residual)
    packed = pack2(halve(l0.R[:, 0:16, :], 0, tmp))
    f1[gz] = packed
    for zz in range(4):
        fh[0, zz * 4 : zz * 4 + 4, :] = packed[zz, 4:8]
        fh[1, zz * 4 : zz * 4 + 4, :] = packed[zz, 0:4]
    f1_copies(lambda c: c.start())

    q = got(ngz - 1, 1)[0:16]
    pivots[ngz - 1] = q
    for p in range(ngz - 1, 0, -1):
        c = got(p, 0)[0:16]
        b = c * (1.0 / q)
        rb[p] = b
        q = got(p - 1, 1)[0:16] - got(p, 2)[0:16] - c * b
        pivots[p - 1] = q
    rb[0] = jnp.zeros((16, 128), F32)
    c = jnp.where(above, red[gz, 0:16, :], 0.0)
    left = rm[jnp.maximum(gz - 1, 0), 0:16, :]
    mid[0] = left
    mid[1] = c * left
    mid[2] = 1.0 / (pivots[gz] - c * c * left)
    mid[3] = c

    for copy in es_planes():
        copy.wait_recv()
    place(es, 0, l1.E, 1, 0.0, (1, 2))
    place(es, 4, l1.S, 0, 1.0, (1, 2))
    coarsen(l1.E, 1, l1, l2, l2.E, 1, True)
    coarsen(l1.S, 0, l1, l2, l2.S, 0, True)
    pack8(l2.E, 1, es3, 0)
    pack8(l2.S, 0, es3, 4)
    spread(es3, s_e3, r_e3, lambda c: c.start())
    prepare(l1)
    prepare(l2)

    lane32 = iota((32, 128), 1)

    def swap(v, s):
        return jnp.where((lane32 & s) == 0, roll(v, -s, 1), roll(v, s, 1))

    def place8(buf, first, dst, offset):
        for zz in range(2):
            for xp in range(2):
                found = [(buf[:, first + zz * 2 + xp, :], 0)]
                for bit in (1, 2, 4):
                    split = []
                    for v, z in found:
                        w = swap(v, bit)
                        low = (lane32 & bit) == 0
                        split += [(jnp.where(low, v, w), z), (jnp.where(low, w, v), z + bit)]
                    found = split
                for v, z in found:
                    dst[offset + zz * 8 + z, pl.ds(xp, ngx, stride=2), :] = v

    l1.F[:, 8:24, :] = jnp.zeros((l1.Z, 16, 128), F32)
    lane16 = iota((16, 128), 1)
    f1_arrive()
    for p in range(ngz):
        l1.F[p * 8 : p * 8 + 8, 0:8, :] = unpack2(f1[p])
        for side, present, row in ((0, has_left, 20), (1, has_right, 8)):
            v = jnp.where(present, fr[side, p], 0.0)
            both = (jnp.where((lane16 & 1) == 0, v, roll(v, 1, 1)), jnp.where((lane16 & 1) == 1, v, roll(v, -1, 1)))
            for zz in range(4):
                for k in range(2):
                    l1.F[p * 8 + zz * 2 + k, row : row + 4, :] = both[k][zz * 4 : zz * 4 + 4]
    pre(l1)
    coarsen(l1.R, 0, l1, l2, l2.F, 0, True)
    lane8 = iota((8, 8, 128), 2)
    v = l2.F[:, 0:8, :].reshape(8, 4, 8, 128)
    k = lane8 & 3
    f2[...] = jnp.where(k == 0, v[:, 0], jnp.where(k == 1, v[:, 1], jnp.where(k == 2, v[:, 2], v[:, 3])))

    def f2_copies():
        return [
            remote(f2, f2r.at[0], s_f2.at[0], r_f2.at[0], gx_at(1), gz),
            remote(f2, f2r.at[1], s_f2.at[1], r_f2.at[1], gx_at(-1), gz),
        ]

    for copy in f2_copies():
        copy.start()

    pre(l2)
    pack8(l2.R, 0, f3, 0)
    spread(f3, s_f3, r_f3, lambda c: c.start())

    collected(es3, s_e3, r_e3)
    place8(es3, 0, l3.E, 1)
    place8(es3, 4, l3.S, 0)
    deep = [l3, l4, l5, l6]
    for fine, coarse in zip(deep[:-1], deep[1:]):
        coarsen(fine.E, 1, fine, coarse, coarse.E, 1, False)
        coarsen(fine.S, 0, fine, coarse, coarse.S, 0, False)
    for lev in deep:
        prepare(lev)

    for copy in f2_copies():
        copy.wait_recv()

    def swap8(v, s):
        return jnp.where((lane8 & s) == 0, roll(v, -s, 2), roll(v, s, 2))

    for side, present, source, row in ((0, has_left, 2, 14), (1, has_right, 1, 5)):
        v = jnp.where(present, f2r[side], 0.0)
        w = swap8(v, 1)
        for k0 in range(2):
            v1 = jnp.where((lane8 & 1) == k0, v, w)
            w1 = swap8(v1, 2)
            for k1 in range(2):
                v2 = jnp.where(((lane8 >> 1) & 1) == k1, v1, w1)
                for zz in range(8):
                    l2.F[zz * 4 + k1 * 2 + k0, row : row + 1, :] = v2[zz, source : source + 1]
    pre(l2)

    collected(f3, s_f3, r_f3)
    place8(f3, 0, l3.F, 0)
    for fine, coarse in zip(deep[:-1], deep[1:]):
        pre(fine)
        coarsen(fine.R, 0, fine, coarse, coarse.F, 0, False)
    coarsest(l6)
    for fine, coarse in zip(deep[-2::-1], deep[:0:-1]):
        unrolled(coarse.Z, lambda z, fine=fine, coarse=coarse: spread_rows(fine.V, 2 * z + 1, coarse.C[z + 1], ((0, coarse.X, 0),)))
        post(fine)

    tiles = ngx // 4
    first = gx // 4
    shift = lax.rem(24 - 2 * lax.rem(gx, 4), 24)

    def tile_at(z, k):
        return l3.C[z, pl.ds(pl.multiple_of(lax.rem(first + (k + tiles), tiles) * 8, 8), 8), :]

    right_rows, left_rows = (iota((4, 128), 0) < 2) | has_right, has_left

    def down3(z):
        c = jnp.concatenate([tile_at(z + 1, 0), tile_at(z + 1, 1), tile_at(z + 1, -1)], axis=0)
        c = pltpu.roll(c, shift, 0)
        for k in range(2):
            for j in range(2):
                l2.V[2 * z + 1 + k, pl.ds(j, 4, stride=2), :] = jnp.where(right_rows, c[0:4], 0.0)
                l2.V[2 * z + 1 + k, pl.ds(12 + j, 2, stride=2), :] = jnp.where(left_rows, c[22:24], 0.0)

    filler(l2.V, 0.0)
    unrolled(l3.Z, down3)
    post(l2)
    unrolled(l2.Z, lambda z: spread_rows(l1.V, 2 * z + 1, l2.C[z + 1], ((0, 4, 0), (4, 4, 8), (12, 4, 16))))
    post(l1)
    l1.C[0] = jnp.zeros((24, 128), F32)
    l1.C[l1.Z + 1] = jnp.zeros((24, 128), F32)

    for i in range(10):
        c = l1.C[gz * 8 + i]
        for z in (2 * i - 1, 2 * i):
            if 0 <= z < 18:
                for j in range(2):
                    l0.V[z, pl.ds(j, 8, stride=2), :] = c[0:8]
                l0.V[z, 16:17, :] = c[8:9]
                l0.V[z, 17:23, :] = jnp.zeros((6, 128), F32)
                l0.V[z, 23:24, :] = c[23:24]

    def second_residual(i):
        z0 = i * 4
        v = l0.V[pl.ds(z0 + 1, 4)]
        around = lateral(l0, v, z0, 4) + l0.WZ[pl.ds(z0, 4)] * l0.V[pl.ds(z0, 4)] + l0.WZ[pl.ds(z0 + 1, 4)] * l0.V[pl.ds(z0 + 2, 4)]
        l0.F[pl.ds(z0, 4)] = l0.R[pl.ds(z0, 4)] - (l0.D[pl.ds(z0, 4)] * v - around)

    unrolled(4, second_residual)
    inner(l0.F)
    end_row, first_row = (l0.F[15] + tail * l0.Y[14])[0:16], (lead * l0.Y[0])[0:16]
    ps[0] = end_row + jnp.where(above, ra[gz, 0:16, :], 0.0) * first_row
    ps[1] = first_row + rb[gz] * end_row
    post_red[gz] = jnp.zeros((16, 128), F32)
    post_copies(lambda c: c.start())
    for z in range(16):
        l0.U[z, 0:16, :] = l0.U[z, 0:16, :] + l0.V[z + 1, 0:16, :]
    gathered(post_red, s_post, r_post)
    tau = jnp.zeros((16, 128), F32)
    for p in range(ngz - 1):
        took = post_red[p] if p == 0 else post_red[p] + ra[p, 0:16, :] * tau
        tau = jnp.where(p < gz, took, tau)
    sigma = jnp.zeros((16, 128), F32)
    for p in range(ngz - 1, 0, -1):
        sigma = jnp.where(p > gz, post_red[p] + rb[p] * sigma, sigma)
    b1 = first_row + tau
    own = mid[2] * (end_row + sigma + mid[1] * b1)
    before = mid[0] * (b1 + mid[3] * own)
    for z in range(16):
        if z < 15:
            x = l0.Y[z, 0:16, :] + av[z, 0:16, :] * before + bv[z, 0:16, :] * own
        else:
            x = own
        out[pl.ds(z, 16, stride=16), :] = l0.U[z, 0:16, :] + OMEGA * x

    for copy in r1_copies():
        copy.wait_send()
    es_lines(lambda c: c.wait_send())
    for copy in es_planes():
        copy.wait_send()
    f1_copies(lambda c: c.wait_send())
    for copy in f2_copies():
        copy.wait_send()
    gather(red, s_red, r_red, lambda c: c.wait_send())
    post_copies(lambda c: c.wait_send())
    spread(es3, s_e3, r_e3, lambda c: c.wait_send())
    spread(f3, s_f3, r_f3, lambda c: c.wait_send())


def solution(mesh):
    ngx, ngz = mesh.shape["gx"], mesh.shape["gz"]

    def per_device(charge, codes, eps_table, screen_table):
        nx, nz, ny = charge.shape
        whole_z, whole_x = nz * ngz, nx * ngx
        levels = [
            (nz, 24),
            (whole_z // 2, 24),
            (whole_z // 4, 16),
            (whole_z // 8, whole_x // 8),
            (whole_z // 16, whole_x // 16),
            (whole_z // 32, whole_x // 32),
            (whole_z // 64, whole_x // 64),
        ]
        scratch = []
        for Z, X in levels:
            scratch += Level.scratch(Z, X)
        vm = lambda *shape: pltpu.VMEM(shape, F32)
        scratch += [
            vm(64, 64, 128),
            pltpu.VMEM((nx * nz, ny), jnp.int32),
            vm(nx * nz, ny),
            pltpu.SemaphoreType.DMA((2,)),
            vm(2, 16, 4, 128),
            vm(2, 16, 4, 128),
            vm(2, 16, 128),
            vm(2, 16, 128),
            vm(4, 8, 128),
            vm(4, 8, 128),
            vm(3, ngz, 8, 8, 128),
            vm(ngz, 4, 8, 128),
            vm(ngz, 90, 128),
            vm(ngz, 16, 128),
            vm(ngz + 1, 24, 128),
            vm(ngz, 18, 128),
            vm(ngz, 18, 128),
            vm(16, 24, 128),
            vm(16, 24, 128),
            vm(ngx, 8, 128),
            vm(ngx, 4, 128),
            vm(2, 16, 128),
            vm(2, ngz, 16, 128),
            vm(8, 8, 128),
            vm(2, 8, 8, 128),
            vm(2, 16, 128),
            vm(ngz, 16, 128),
            vm(ngz, 16, 128),
            vm(4, 16, 128),
        ]
        for shape in ((8,), (3, ngz), (3, ngz), (ngz,), (ngz,), (ngx,), (ngx,), (2,)):
            scratch += [pltpu.SemaphoreType.DMA(shape)] * 2
        result = pl.pallas_call(
            lambda *refs: kernel(ngx, ngz, *refs),
            out_shape=jax.ShapeDtypeStruct((nx * nz, ny), F32),
            in_specs=[
                pl.BlockSpec(memory_space=pl.ANY),
                pl.BlockSpec(memory_space=pl.ANY),
                pl.BlockSpec(memory_space=pltpu.SMEM),
                pl.BlockSpec(memory_space=pltpu.SMEM),
            ],
            out_specs=pl.BlockSpec(memory_space=pltpu.VMEM),
            scratch_shapes=scratch,
            compiler_params=pltpu.CompilerParams(collective_id=0, has_side_effects=True, vmem_limit_bytes=55040 << 10),
            name="vcycle",
        )(codes.reshape(nx * nz, ny), charge.reshape(nx * nz, ny), eps_table, screen_table)
        return result.reshape(nx, nz, ny)

    return jax.shard_map(
        per_device,
        mesh=mesh,
        in_specs=(P("gx", "gz", None), P("gx", "gz", None), P(), P()),
        out_specs=P("gx", "gz", None),
        check_vma=False,
    )
```

```python
import jax
import jax.numpy as jnp
from jax import lax
from jax.experimental import pallas as pl
from jax.experimental.pallas import tpu as pltpu
from jax.sharding import PartitionSpec as P

OMEGA = 0.8
SWEEPS = 8
LAST = 6
F32 = jnp.float32
MESH = pl.DeviceIdType.MESH
FAR_FIRST = (4, 3, 5, 2, 6, 1, 7)


def iota(shape, dim):
    return lax.broadcasted_iota(jnp.int32, shape, dim)


def roll(v, shift, axis):
    size = v.shape[axis]
    return pltpu.roll(v, shift % size, axis)


class Level:
    def __init__(self, index, refs, whole, slab):
        (self.E, self.S, self.WXM, self.WXP, self.WYM, self.WYP, self.WZ, self.D, self.A, self.M, self.F, self.U, self.R, self.Y,
         self.V, self.C) = refs
        self.index, self.whole, self.n = index, whole, slab
        self.Z, self.X = self.S.shape[0], self.S.shape[1]
        self.mask = None

    @staticmethod
    def scratch(Z, X):
        sizes = (Z + 2, Z, Z, Z, Z, Z, Z + 1, Z, Z + 1, Z, Z, Z, Z, Z, Z + 2, Z + 2)
        return [pltpu.VMEM((s, X, 128), F32) for s in sizes]


def loop(count, body):
    def step(i, carry):
        body(i)
        return carry

    lax.fori_loop(0, count, step, 0)


def unrolled(count, body):
    for i in range(count):
        body(i)


def couplings(lev, z0, n):
    h = 0.5 ** lev.index * 0.5
    sh = 2 ** lev.index
    X = lev.X
    e = lev.E[pl.ds(z0 + 1, n)]
    lane = iota((n, X, 128), 2)
    first, last = lane < sh, lane >= 128 - sh
    up, down = roll(e, 1, 1), roll(e, -1, 1)
    if lev.whole:
        row = iota((n, X, 128), 1)
        up, down = jnp.where(row == 0, 0.0, up), jnp.where(row == X - 1, 0.0, down)
    left, right = jnp.where(first, 0.0, roll(e, sh, 2)), jnp.where(last, 0.0, roll(e, -sh, 2))
    wxm, wxp, wym, wyp = h * (e + up), h * (e + down), h * (e + left), h * (e + right)
    wzm, wzp = h * (e + lev.E[pl.ds(z0, n)]), h * (e + lev.E[pl.ds(z0 + 2, n)])
    lev.D[pl.ds(z0, n)] = wxm + wxp + wzm + wzp + wym + wyp + lev.S[pl.ds(z0, n)]
    if lev.whole:
        wxm, wxp = jnp.where(row == 0, 0.0, wxm), jnp.where(row == X - 1, 0.0, wxp)
    lev.WXM[pl.ds(z0, n)] = wxm
    lev.WXP[pl.ds(z0, n)] = wxp
    lev.WYM[pl.ds(z0, n)] = jnp.where(first, 0.0, wym)
    lev.WYP[pl.ds(z0, n)] = jnp.where(last, 0.0, wyp)
    lev.WZ[pl.ds(z0, n)] = wzm
    return wzp


def lateral(lev, u, z0, n):
    sh = 2 ** lev.index
    return (
        lev.WXM[pl.ds(z0, n)] * roll(u, 1, 1)
        + lev.WXP[pl.ds(z0, n)] * roll(u, -1, 1)
        + lev.WYM[pl.ds(z0, n)] * roll(u, sh, 2)
        + lev.WYP[pl.ds(z0, n)] * roll(u, -sh, 2)
    )


def steps_of(count):
    if count <= 32:
        return count
    return 8 if count % 8 == 0 else 1


def prepare(lev):
    Z, X, n = lev.Z, lev.X, lev.n
    zero = jnp.zeros((1, X, 128), F32)
    lev.E[0:1] = zero
    lev.E[Z + 1 : Z + 2] = zero
    (loop if Z // n > 8 else unrolled)(Z // n, lambda i: couplings(lev, i * n, n))
    lev.WZ[0:1] = zero
    lev.WZ[Z : Z + 1] = zero
    lev.A[Z : Z + 1] = zero
    s = steps_of(Z)

    def body(i, m):
        for j in range(s):
            z = i * s + j
            w = lev.WZ[z]
            a = w * m
            m = 1.0 / (lev.D[z] - w * a)
            lev.A[z] = a
            lev.M[z] = m
        return m

    lax.fori_loop(0, Z // s, body, jnp.zeros((X, 128), F32))


def sweep(lev, src, finish):
    Z, X = lev.Z, lev.X
    s = steps_of(Z)

    def forward(i, y):
        for j in range(s):
            z = i * s + j
            y = src[z] + lev.A[z] * y
            lev.Y[z] = y
        return y

    def backward(i, x):
        for j in range(s):
            z = Z - 1 - (i * s + j)
            x = lev.M[z] * lev.Y[z] + lev.A[z + 1] * x
            finish(z, x)
        return x

    lax.fori_loop(0, Z // s, forward, jnp.zeros((X, 128), F32))
    lax.fori_loop(0, Z // s, backward, jnp.zeros((X, 128), F32))


def pair_lanes(v, index):
    sh = 2 ** index
    lane = iota(v.shape, v.ndim - 1)
    other = jnp.where((lane & sh) == 0, roll(v, -sh, v.ndim - 1), roll(v, sh, v.ndim - 1))
    return v + other


def halve(v, index, tmp, at=0):
    n, X = v.shape[0], v.shape[1]
    v = v.reshape(n // 2, 2, X, 128)
    v = pair_lanes(v[:, 0] + v[:, 1], index)
    part = slice(at, at + n // 2)
    tmp[part, 0:X, :] = v
    return 0.125 * (tmp[part, pl.ds(0, X // 2, stride=2), :] + tmp[part, pl.ds(1, X // 2, stride=2), :])


def pre(lev):
    def finish(z, x):
        lev.U[z] = OMEGA * x

    sweep(lev, lev.F, finish)
    n = lev.n

    def body(i):
        z0 = i * n
        r = (1.0 - OMEGA) * lev.F[pl.ds(z0, n)] + lateral(lev, lev.U[pl.ds(z0, n)], z0, n)
        if lev.mask is not None:
            r = jnp.where(lev.mask[None] > 0, r, 0.0)
        lev.R[pl.ds(z0, n)] = r

    unrolled(lev.Z // n, body)


def post(lev):
    n, Z = lev.n, lev.Z
    zero = jnp.zeros((1, lev.X, 128), F32)
    lev.V[0:1] = zero
    lev.V[Z + 1 : Z + 2] = zero

    def body(i):
        z0 = i * n
        v = lev.V[pl.ds(z0 + 1, n)]
        around = lateral(lev, v, z0, n) + lev.WZ[pl.ds(z0, n)] * lev.V[pl.ds(z0, n)] + lev.WZ[pl.ds(z0 + 1, n)] * lev.V[pl.ds(z0 + 2, n)]
        r = lev.R[pl.ds(z0, n)] - (lev.D[pl.ds(z0, n)] * v - around)
        if lev.mask is not None:
            r = jnp.where(lev.mask[None] > 0, r, 0.0)
        lev.F[pl.ds(z0, n)] = r

    unrolled(Z // n, body)

    def finish(z, x):
        lev.C[z + 1] = lev.U[z] + lev.V[z + 1] + OMEGA * x

    sweep(lev, lev.F, finish)


def coarsest(lev):
    Z = lev.Z
    sh = 2 ** lev.index
    f = [lev.F[z] for z in range(Z)]
    a = [lev.A[z] for z in range(Z + 1)]
    m = [lev.M[z] for z in range(Z)]
    w = [(lev.WXM[z], lev.WXP[z], lev.WYM[z], lev.WYP[z]) for z in range(Z)]

    def solved(r):
        y = [r[0]]
        for z in range(1, Z):
            y.append(r[z] + a[z] * y[-1])
        x = [None] * Z
        x[Z - 1] = m[Z - 1] * y[Z - 1]
        for z in range(Z - 2, -1, -1):
            x[z] = m[z] * y[z] + a[z + 1] * x[z + 1]
        return x

    u = [OMEGA * x for x in solved(f)]
    for _ in range(SWEEPS - 1):
        r = []
        for z in range(Z):
            xm, xp, ym, yp = w[z]
            side = xm * roll(u[z], 1, 0) + xp * roll(u[z], -1, 0)
            r.append(f[z] + (side + (ym * roll(u[z], sh, 1) + yp * roll(u[z], -sh, 1))))
        x = solved(r)
        u = [(1.0 - OMEGA) * u[z] + OMEGA * x[z] for z in range(Z)]
    for z in range(Z):
        lev.C[z + 1] = u[z]


def spread_rows(dst, z, c, rows):
    for source, count, target in rows:
        part = c[source : source + count]
        for k in range(2):
            for j in range(2):
                dst[z + k, pl.ds(target + j, count, stride=2), :] = part


def kernel(ngx, ngz, *refs):
    codes_in, charge_in, eps_t, scr_t, out = refs[:5]
    refs = list(refs[5:])

    def take(count):
        got = refs[:count]
        del refs[:count]
        return got

    l0 = Level(0, take(16), False, 4)
    l1 = Level(1, take(16), False, 8)
    l2 = Level(2, take(16), False, 8)
    l3 = Level(3, take(16), True, 4)
    l4 = Level(4, take(16), True, 4)
    l5 = Level(5, take(16), True, 4)
    l6 = Level(6, take(16), True, 2)
    (tmp, codes, charge, s_in, xs, xr, zs, zr, ds, dr, es, f1, red, post_red, ub, rm, ra, av, bv, es3, f3, fh, fr, f2, f2r, ps, rb, pivots, mid) = take(29)
    (s_r1, r_r1, s_es, r_es, s_f1, r_f1, s_red, r_red, s_post, r_post, s_e3, r_e3, s_f3, r_f3, s_f2, r_f2) = take(16)

    gx, gz = lax.axis_index("gx"), lax.axis_index("gz")

    def gx_at(k):
        return lax.rem(gx + (k + ngx), ngx)

    def gz_at(k):
        return lax.rem(gz + (k + ngz), ngz)

    def remote(src, dst, ss, rs, tx, tz):
        return pltpu.make_async_remote_copy(src, dst, ss, rs, device_id=(tx, tz), device_id_type=MESH)

    inputs = (pltpu.make_async_copy(codes_in, codes, s_in.at[0]), pltpu.make_async_copy(charge_in, charge, s_in.at[1]))
    for copy in inputs:
        copy.start()

    barrier = pltpu.get_barrier_semaphore()

    def hello(tx, tz):
        pl.semaphore_signal(barrier, 1, device_id=(tx, tz), device_id_type=MESH)

    loop(ngz - 1, lambda k: hello(gx, gz_at(k + 1)))
    loop(ngz, lambda k: hello(gx_at(1), gz_at(k)))
    loop(ngz, lambda k: hello(gx_at(-1), gz_at(k)))
    loop(ngx - 3, lambda k: hello(gx_at(k + 2), gz))

    row24, row16 = iota((24, 128), 0), iota((16, 128), 0)
    has_right, has_left = gx < ngx - 1, gx > 0
    lane = iota((1, 8, 128), 2)

    table_e = [jnp.full((16, 128), eps_t[k], F32) for k in range(eps_t.shape[0])]
    table_s = [jnp.full((16, 128), scr_t[k], F32) for k in range(eps_t.shape[0])]

    def look(i):
        c = codes[pl.ds(i, 16, stride=16), :]
        e = jnp.zeros((16, 128), F32)
        s = jnp.zeros((16, 128), F32)
        for k in range(eps_t.shape[0]):
            e = jnp.where(c == k, table_e[k], e)
            s = jnp.where(c == k, table_s[k], s)
        l0.E[i + 1, 0:16, :] = e
        l0.S[i, 0:16, :] = s
        l0.F[i, 0:16, :] = charge[pl.ds(i, 16, stride=16), :]

    for copy in inputs:
        copy.wait()
    unrolled(16, look)

    xs[0, :, 0:2, :] = l0.E[1:17, 14:16, :]
    xs[0, :, 2:3, :] = l0.S[:, 15:16, :]
    xs[0, :, 3:4, :] = l0.F[:, 15:16, :]
    xs[1, :, 0:2, :] = l0.E[1:17, 0:2, :]
    xs[1, :, 2:3, :] = l0.S[:, 0:1, :]
    xs[1, :, 3:4, :] = l0.F[:, 0:1, :]
    zs[0] = l0.E[16, 0:16, :]
    zs[1] = l0.E[1, 0:16, :]
    ds[0] = l0.E[16, 8:16, :]
    ds[1] = l0.E[16, 0:8, :]
    ds[2] = l0.E[1, 8:16, :]
    ds[3] = l0.E[1, 0:8, :]

    def pack2(v):
        v = v.reshape(4, 2, 8, 128)
        return jnp.where((lane & 1) == 0, v[:, 0], v[:, 1])

    es[0, gz, 0:4] = pack2(halve(l0.E[1:17, 0:16, :], 0, tmp))
    es[0, gz, 4:8] = pack2(halve(l0.S[:, 0:16, :], 0, tmp, 8))

    def r1_copies():
        return [
            remote(xs.at[0], xr.at[0], s_r1.at[0], r_r1.at[0], gx_at(1), gz),
            remote(xs.at[1], xr.at[1], s_r1.at[1], r_r1.at[1], gx_at(-1), gz),
            remote(zs.at[0], zr.at[0], s_r1.at[2], r_r1.at[2], gx, gz_at(1)),
            remote(zs.at[1], zr.at[1], s_r1.at[3], r_r1.at[3], gx, gz_at(-1)),
            remote(ds.at[0], dr.at[0], s_r1.at[4], r_r1.at[4], gx_at(1), gz_at(1)),
            remote(ds.at[1], dr.at[1], s_r1.at[5], r_r1.at[5], gx_at(-1), gz_at(1)),
            remote(ds.at[2], dr.at[2], s_r1.at[6], r_r1.at[6], gx_at(1), gz_at(-1)),
            remote(ds.at[3], dr.at[3], s_r1.at[7], r_r1.at[7], gx_at(-1), gz_at(-1)),
        ]

    pl.semaphore_wait(barrier, 3 * ngz - 1 + ngx - 3)
    for copy in r1_copies():
        copy.start()

    def f1_copies(act):
        def go(slot, k, src, dst, tx):
            act(remote(src, dst, s_f1.at[slot, k], r_f1.at[slot, gz], tx, gz_at(k)))

        for k in (4, 3, 5, 2, 6, 1, 7, 0):
            if k:
                go(0, k, f1.at[gz], f1.at[gz], gx)
            go(1, k, fh.at[0], fr.at[0, gz], gx_at(1))
            go(2, k, fh.at[1], fr.at[1, gz], gx_at(-1))

    def f1_arrive():
        def get(slot, dst, k):
            p = gz_at(k)
            remote(dst, dst, s_f1.at[slot, k], r_f1.at[slot, p], gx, gz_at(1)).wait_recv()

        loop(ngz - 1, lambda k: get(0, f1.at[gz], k + 1))
        loop(ngz, lambda k: get(1, fr.at[0, gz], k))
        loop(ngz, lambda k: get(2, fr.at[1, gz], k))

    def es_lines(act):
        for k in FAR_FIRST:
            act(remote(es.at[0, gz], es.at[0, gz], s_es.at[0, k], r_es.at[0, gz], gx, gz_at(k)))

    def es_planes():
        return [
            remote(es.at[0], es.at[2], s_es.at[2, 0], r_es.at[2, 0], gx_at(1), gz),
            remote(es.at[0], es.at[1], s_es.at[1, 0], r_es.at[1, 0], gx_at(-1), gz),
        ]

    es_lines(lambda c: c.start())

    for copy in r1_copies():
        copy.wait_recv()

    above, below = gz > 0, gz < ngz - 1
    zero16 = jnp.zeros((16, 24, 128), F32)
    l0.E[0:1] = zero16[0:1]
    l0.E[17:18] = zero16[0:1]
    l0.E[1:17, 16:24, :] = zero16[:, 0:8]
    l0.S[:, 16:24, :] = jnp.ones((16, 8, 128), F32)
    l0.F[:, 16:24, :] = zero16[:, 0:8]
    l0.E[1:17, 22:24, :] = jnp.where(has_left, xr[0, :, 0:2, :], 0.0)
    l0.S[:, 23:24, :] = jnp.where(has_left, xr[0, :, 2:3, :], 1.0)
    l0.F[:, 23:24, :] = jnp.where(has_left, xr[0, :, 3:4, :], 0.0)
    l0.E[1:17, 16:18, :] = jnp.where(has_right, xr[1, :, 0:2, :], 0.0)
    l0.S[:, 16:17, :] = jnp.where(has_right, xr[1, :, 2:3, :], 1.0)
    l0.F[:, 16:17, :] = jnp.where(has_right, xr[1, :, 3:4, :], 0.0)
    l0.E[0, 0:16, :] = jnp.where(above, zr[0], 0.0)
    l0.E[17, 0:16, :] = jnp.where(below, zr[1], 0.0)
    l0.E[0, 23:24, :] = jnp.where(above & has_left, dr[0, 7:8, :], 0.0)
    l0.E[0, 16:17, :] = jnp.where(above & has_right, dr[1, 0:1, :], 0.0)
    l0.E[17, 23:24, :] = jnp.where(below & has_left, dr[2, 7:8, :], 0.0)
    l0.E[17, 16:17, :] = jnp.where(below & has_right, dr[3, 0:1, :], 0.0)

    for i in range(4):
        wzp = couplings(l0, i * 4, 4)
    l0.WZ[16:17] = wzp[3:4]

    m = 1.0 / l0.D[0]
    l0.M[0] = m
    for z in range(1, 15):
        w = l0.WZ[z]
        a = w * m
        m = 1.0 / (l0.D[z] - w * a)
        l0.A[z] = a
        l0.M[z] = m
    lead = jnp.where(above, l0.WZ[0], 0.0)
    tail = l0.WZ[15]

    y = lead
    av[0] = y
    for z in range(1, 15):
        y = l0.A[z] * y
        av[z] = y
    x = l0.M[14] * y
    b = l0.M[14] * tail
    av[14] = x
    bv[14] = b
    for z in range(13, -1, -1):
        x = l0.M[z] * av[z] + l0.A[z + 1] * x
        b = l0.A[z + 1] * b
        av[z] = x
        bv[z] = b

    def inner(src):
        y = src[0]
        l0.Y[0] = y
        for z in range(1, 15):
            y = src[z] + l0.A[z] * y
            l0.Y[z] = y
        x = l0.M[14] * y
        l0.Y[14] = x
        for z in range(13, -1, -1):
            x = l0.M[z] * l0.Y[z] + l0.A[z + 1] * x
            l0.Y[z] = x

    inner(l0.F)

    def put(k, v):
        red[gz, pl.ds(k * 18, 17), :] = v[0:17]
        red[gz, pl.ds(k * 18 + 17, 1), :] = v[23:24]

    put(0, tail * av[14])
    put(1, l0.D[15] - tail * bv[14])
    put(2, lead * av[0])
    put(3, l0.F[15] + tail * l0.Y[14])
    put(4, lead * l0.Y[0])

    def gather(buf, ss, rs, act):
        for k in FAR_FIRST:
            act(remote(buf.at[gz], buf.at[gz], ss.at[k], rs.at[gz], gx, gz_at(k)))

    def post_copies(act):
        for k in FAR_FIRST:
            side = lax.div(gz + k, ngz)
            act(remote(ps.at[side], post_red.at[gz], s_post.at[k], r_post.at[gz], gx, gz_at(k)))

    def gathered(buf, ss, rs):
        def get(k):
            p = gz_at(k)
            remote(buf.at[gz], buf.at[p], ss.at[k], rs.at[p], gx, p).wait_recv()

        loop(ngz - 1, lambda k: get(k + 1))

    gather(red, s_red, r_red, lambda c: c.start())

    def es_line_in(k):
        p = gz_at(k + 1)
        remote(es.at[0, gz], es.at[0, p], s_es.at[0, k + 1], r_es.at[0, p], gx, p).wait_recv()

    loop(ngz - 1, es_line_in)
    for copy in es_planes():
        copy.start()

    mask1 = jnp.where(row24 < 8, 1.0, jnp.where(row24 < 16, jnp.where(has_right, 1.0, 0.0), jnp.where(has_left, 1.0, 0.0)))
    mask2 = jnp.where(
        row16 < 4,
        1.0,
        jnp.where(row16 < 8, jnp.where(has_right, 1.0, 0.0), jnp.where(row16 < 12, 0.0, jnp.where(has_left, 1.0, 0.0))),
    )
    l1.mask, l2.mask = mask1, mask2

    def unpack2(v):
        even = jnp.where((lane & 1) == 0, v, roll(v, 1, 2))
        odd = jnp.where((lane & 1) == 1, v, roll(v, -1, 2))
        return jnp.stack([even, odd], axis=1).reshape(2 * v.shape[0], 8, 128)

    here = (None, has_right, has_left)

    def place(buf, start, dst, offset, outside, slots):
        for slot in slots:
            for p in range(ngz):
                v = unpack2(buf[slot, p, start : start + 4])
                if slot:
                    v = jnp.where(here[slot], v, outside)
                dst[p * 8 + offset : p * 8 + offset + 8, slot * 8 : slot * 8 + 8, :] = v

    place(es, 0, l1.E, 1, 0.0, (0,))
    place(es, 4, l1.S, 0, 1.0, (0,))

    def coarsen(src, offset, fine, coarse, dst, dst_offset, split):
        n = fine.n

        def body(i):
            v = halve(src[i * n + offset : (i + 1) * n + offset], fine.index, tmp, i * (n // 2))
            at = slice(i * (n // 2) + dst_offset, (i + 1) * (n // 2) + dst_offset)
            if split:
                dst[at, 0:8, :] = v[:, 0:8]
                dst[at, 12:16, :] = v[:, 8:12]
            else:
                dst[at] = v

        unrolled(fine.Z // n, body)

    def filler(ref, value):
        ref[:, 8:12, :] = jnp.full((ref.shape[0], 4, 128), value, F32)

    filler(l2.E, 0.0)
    filler(l2.S, 1.0)
    filler(l2.F, 0.0)

    lane3 = iota((2, 2, 128), 2)

    def pack8(src, offset, buf, first):
        for i in range(2):
            v = halve(src[i * 16 + offset : i * 16 + offset + 16], 2, tmp, i * 8)[:, 0:2]
            tmp[i * 8 : i * 8 + 8, 32:34, :] = v
        v = tmp[0:16, 32:34, :].reshape(2, 8, 2, 128)
        picked = v[:, 7]
        for k in range(7):
            picked = jnp.where((lane3 & 7) == k, v[:, k], picked)
        for zz in range(2):
            buf[gx, first + zz * 2 : first + zz * 2 + 2, :] = picked[zz]

    core, x4, y4 = lax.rem(gx, 2), lax.rem(lax.div(gx, 2), 4), lax.div(gx, 8)
    hops = sorted(((dy, dx, dc) for dy in range(4) for dx in range(4) for dc in range(2)), key=lambda t: -(min(t[0], 4 - t[0]) + min(t[1], 4 - t[1]) + 0.5 * t[2]))
    far_gx = [lax.rem(y4 + dy, 4) * 8 + lax.rem(x4 + dx, 4) * 2 + lax.rem(core + dc, 2) for dy, dx, dc in hops[:-1]]

    def spread(buf, ss, rs, act):
        for i, tx in enumerate(far_gx):
            act(remote(buf.at[gx], buf.at[gx], ss.at[i], rs.at[gx], tx, gz))

    def collected(buf, ss, rs):
        def get(k):
            p = gx_at(k)
            remote(buf.at[gx], buf.at[p], ss.at[k], rs.at[p], p, gz).wait_recv()

        loop(ngx - 1, lambda k: get(k + 1))

    gathered(red, s_red, r_red)

    def got(p, k):
        return red[p, pl.ds(k * 18, 18), :]

    m, y = None, None
    for p in range(ngz):
        diag, right = got(p, 1), got(p, 3)
        if p + 1 < ngz:
            diag, right = diag - got(p + 1, 2), right + got(p + 1, 4)
        if p:
            c = got(p, 0)
            a = c * m
            diag, right = diag - c * a, right + a * y
            ra[p] = a
        m, y = 1.0 / diag, right
        rm[p] = m
        ub[p + 1, 0:18, :] = y
    x = m * y
    for p in range(ngz - 1, -1, -1):
        if p + 1 < ngz:
            x = rm[p] * ub[p + 1, 0:18, :] + ra[p + 1] * x
        ub[p + 1, 0:17, :] = x[0:17]
        ub[p + 1, 23:24, :] = x[17:18]
        ub[p + 1, 17:23, :] = jnp.zeros((6, 128), F32)
    ub[0] = jnp.zeros((24, 128), F32)

    before, own = ub[gz], ub[gz + 1]
    for z in range(15):
        l0.U[z] = OMEGA * (l0.Y[z] + av[z] * before + bv[z] * own)
    l0.U[15] = OMEGA * own

    def first_residual(i):
        z0 = i * 4
        l0.R[pl.ds(z0, 4)] = (1.0 - OMEGA) * l0.F[pl.ds(z0, 4)] + lateral(l0, l0.U[pl.ds(z0, 4)], z0, 4)

    unrolled(4, first_residual)
    packed = pack2(halve(l0.R[:, 0:16, :], 0, tmp))
    f1[gz] = packed
    for zz in range(4):
        fh[0, zz * 4 : zz * 4 + 4, :] = packed[zz, 4:8]
        fh[1, zz * 4 : zz * 4 + 4, :] = packed[zz, 0:4]
    f1_copies(lambda c: c.start())

    q = got(ngz - 1, 1)[0:16]
    pivots[ngz - 1] = q
    for p in range(ngz - 1, 0, -1):
        c = got(p, 0)[0:16]
        b = c * (1.0 / q)
        rb[p] = b
        q = got(p - 1, 1)[0:16] - got(p, 2)[0:16] - c * b
        pivots[p - 1] = q
    rb[0] = jnp.zeros((16, 128), F32)
    c = jnp.where(above, red[gz, 0:16, :], 0.0)
    left = rm[jnp.maximum(gz - 1, 0), 0:16, :]
    mid[0] = left
    mid[1] = c * left
    mid[2] = 1.0 / (pivots[gz] - c * c * left)
    mid[3] = c

    for copy in es_planes():
        copy.wait_recv()
    place(es, 0, l1.E, 1, 0.0, (1, 2))
    place(es, 4, l1.S, 0, 1.0, (1, 2))
    coarsen(l1.E, 1, l1, l2, l2.E, 1, True)
    coarsen(l1.S, 0, l1, l2, l2.S, 0, True)
    pack8(l2.E, 1, es3, 0)
    pack8(l2.S, 0, es3, 4)
    spread(es3, s_e3, r_e3, lambda c: c.start())
    prepare(l1)
    prepare(l2)

    lane32 = iota((32, 128), 1)

    def swap(v, s):
        return jnp.where((lane32 & s) == 0, roll(v, -s, 1), roll(v, s, 1))

    def place8(buf, first, dst, offset):
        for zz in range(2):
            for xp in range(2):
                found = [(buf[:, first + zz * 2 + xp, :], 0)]
                for bit in (1, 2, 4):
                    split = []
                    for v, z in found:
                        w = swap(v, bit)
                        low = (lane32 & bit) == 0
                        split += [(jnp.where(low, v, w), z), (jnp.where(low, w, v), z + bit)]
                    found = split
                for v, z in found:
                    dst[offset + zz * 8 + z, pl.ds(xp, ngx, stride=2), :] = v

    l1.F[:, 8:24, :] = jnp.zeros((l1.Z, 16, 128), F32)
    lane16 = iota((16, 128), 1)
    f1_arrive()
    for p in range(ngz):
        l1.F[p * 8 : p * 8 + 8, 0:8, :] = unpack2(f1[p])
        for side, present, row in ((0, has_left, 20), (1, has_right, 8)):
            v = jnp.where(present, fr[side, p], 0.0)
            both = (jnp.where((lane16 & 1) == 0, v, roll(v, 1, 1)), jnp.where((lane16 & 1) == 1, v, roll(v, -1, 1)))
            for zz in range(4):
                for k in range(2):
                    l1.F[p * 8 + zz * 2 + k, row : row + 4, :] = both[k][zz * 4 : zz * 4 + 4]
    pre(l1)
    coarsen(l1.R, 0, l1, l2, l2.F, 0, True)
    lane8 = iota((8, 8, 128), 2)
    v = l2.F[:, 0:8, :].reshape(8, 4, 8, 128)
    k = lane8 & 3
    f2[...] = jnp.where(k == 0, v[:, 0], jnp.where(k == 1, v[:, 1], jnp.where(k == 2, v[:, 2], v[:, 3])))

    def f2_copies():
        return [
            remote(f2, f2r.at[0], s_f2.at[0], r_f2.at[0], gx_at(1), gz),
            remote(f2, f2r.at[1], s_f2.at[1], r_f2.at[1], gx_at(-1), gz),
        ]

    for copy in f2_copies():
        copy.start()

    pre(l2)
    pack8(l2.R, 0, f3, 0)
    spread(f3, s_f3, r_f3, lambda c: c.start())

    collected(es3, s_e3, r_e3)
    place8(es3, 0, l3.E, 1)
    place8(es3, 4, l3.S, 0)
    deep = [l3, l4, l5, l6]
    for fine, coarse in zip(deep[:-1], deep[1:]):
        coarsen(fine.E, 1, fine, coarse, coarse.E, 1, False)
        coarsen(fine.S, 0, fine, coarse, coarse.S, 0, False)
    for lev in deep:
        prepare(lev)

    for copy in f2_copies():
        copy.wait_recv()

    def swap8(v, s):
        return jnp.where((lane8 & s) == 0, roll(v, -s, 2), roll(v, s, 2))

    for side, present, source, row in ((0, has_left, 2, 14), (1, has_right, 1, 5)):
        v = jnp.where(present, f2r[side], 0.0)
        w = swap8(v, 1)
        for k0 in range(2):
            v1 = jnp.where((lane8 & 1) == k0, v, w)
            w1 = swap8(v1, 2)
            for k1 in range(2):
                v2 = jnp.where(((lane8 >> 1) & 1) == k1, v1, w1)
                for zz in range(8):
                    l2.F[zz * 4 + k1 * 2 + k0, row : row + 1, :] = v2[zz, source : source + 1]
    pre(l2)

    collected(f3, s_f3, r_f3)
    place8(f3, 0, l3.F, 0)
    for fine, coarse in zip(deep[:-1], deep[1:]):
        pre(fine)
        coarsen(fine.R, 0, fine, coarse, coarse.F, 0, False)
    coarsest(l6)
    for fine, coarse in zip(deep[-2::-1], deep[:0:-1]):
        unrolled(coarse.Z, lambda z, fine=fine, coarse=coarse: spread_rows(fine.V, 2 * z + 1, coarse.C[z + 1], ((0, coarse.X, 0),)))
        post(fine)

    tiles = ngx // 4
    first = gx // 4
    shift = lax.rem(24 - 2 * lax.rem(gx, 4), 24)

    def tile_at(z, k):
        return l3.C[z, pl.ds(pl.multiple_of(lax.rem(first + (k + tiles), tiles) * 8, 8), 8), :]

    right_rows, left_rows = (iota((4, 128), 0) < 2) | has_right, has_left

    def down3(z):
        c = jnp.concatenate([tile_at(z + 1, 0), tile_at(z + 1, 1), tile_at(z + 1, -1)], axis=0)
        c = pltpu.roll(c, shift, 0)
        for k in range(2):
            for j in range(2):
                l2.V[2 * z + 1 + k, pl.ds(j, 4, stride=2), :] = jnp.where(right_rows, c[0:4], 0.0)
                l2.V[2 * z + 1 + k, pl.ds(12 + j, 2, stride=2), :] = jnp.where(left_rows, c[22:24], 0.0)

    filler(l2.V, 0.0)
    unrolled(l3.Z, down3)
    post(l2)
    unrolled(l2.Z, lambda z: spread_rows(l1.V, 2 * z + 1, l2.C[z + 1], ((0, 4, 0), (4, 4, 8), (12, 4, 16))))
    post(l1)
    l1.C[0] = jnp.zeros((24, 128), F32)
    l1.C[l1.Z + 1] = jnp.zeros((24, 128), F32)

    for i in range(10):
        c = l1.C[gz * 8 + i]
        for z in (2 * i - 1, 2 * i):
            if 0 <= z < 18:
                for j in range(2):
                    l0.V[z, pl.ds(j, 8, stride=2), :] = c[0:8]
                l0.V[z, 16:17, :] = c[8:9]
                l0.V[z, 17:23, :] = jnp.zeros((6, 128), F32)
                l0.V[z, 23:24, :] = c[23:24]

    def second_residual(i):
        z0 = i * 4
        v = l0.V[pl.ds(z0 + 1, 4)]
        around = lateral(l0, v, z0, 4) + l0.WZ[pl.ds(z0, 4)] * l0.V[pl.ds(z0, 4)] + l0.WZ[pl.ds(z0 + 1, 4)] * l0.V[pl.ds(z0 + 2, 4)]
        l0.F[pl.ds(z0, 4)] = l0.R[pl.ds(z0, 4)] - (l0.D[pl.ds(z0, 4)] * v - around)

    unrolled(4, second_residual)
    inner(l0.F)
    end_row, first_row = (l0.F[15] + tail * l0.Y[14])[0:16], (lead * l0.Y[0])[0:16]
    ps[0] = end_row + jnp.where(above, ra[gz, 0:16, :], 0.0) * first_row
    ps[1] = first_row + rb[gz] * end_row
    post_red[gz] = jnp.zeros((16, 128), F32)
    post_copies(lambda c: c.start())
    for z in range(16):
        l0.U[z, 0:16, :] = l0.U[z, 0:16, :] + l0.V[z + 1, 0:16, :]
    for copy in r1_copies():
        copy.wait_send()
    es_lines(lambda c: c.wait_send())
    for copy in es_planes():
        copy.wait_send()
    f1_copies(lambda c: c.wait_send())
    for copy in f2_copies():
        copy.wait_send()
    gather(red, s_red, r_red, lambda c: c.wait_send())
    spread(es3, s_e3, r_e3, lambda c: c.wait_send())
    spread(f3, s_f3, r_f3, lambda c: c.wait_send())
    gathered(post_red, s_post, r_post)
    tau = jnp.zeros((16, 128), F32)
    for p in range(ngz - 1):
        took = post_red[p] if p == 0 else post_red[p] + ra[p, 0:16, :] * tau
        tau = jnp.where(p < gz, took, tau)
    sigma = jnp.zeros((16, 128), F32)
    for p in range(ngz - 1, 0, -1):
        sigma = jnp.where(p > gz, post_red[p] + rb[p] * sigma, sigma)
    b1 = first_row + tau
    own = mid[2] * (end_row + sigma + mid[1] * b1)
    before = mid[0] * (b1 + mid[3] * own)
    for z in range(16):
        if z < 15:
            x = l0.Y[z, 0:16, :] + av[z, 0:16, :] * before + bv[z, 0:16, :] * own
        else:
            x = own
        out[pl.ds(z, 16, stride=16), :] = l0.U[z, 0:16, :] + OMEGA * x

    post_copies(lambda c: c.wait_send())


def solution(mesh):
    ngx, ngz = mesh.shape["gx"], mesh.shape["gz"]

    def per_device(charge, codes, eps_table, screen_table):
        nx, nz, ny = charge.shape
        whole_z, whole_x = nz * ngz, nx * ngx
        levels = [
            (nz, 24),
            (whole_z // 2, 24),
            (whole_z // 4, 16),
            (whole_z // 8, whole_x // 8),
            (whole_z // 16, whole_x // 16),
            (whole_z // 32, whole_x // 32),
            (whole_z // 64, whole_x // 64),
        ]
        scratch = []
        for Z, X in levels:
            scratch += Level.scratch(Z, X)
        vm = lambda *shape: pltpu.VMEM(shape, F32)
        scratch += [
            vm(64, 64, 128),
            pltpu.VMEM((nx * nz, ny), jnp.int32),
            vm(nx * nz, ny),
            pltpu.SemaphoreType.DMA((2,)),
            vm(2, 16, 4, 128),
            vm(2, 16, 4, 128),
            vm(2, 16, 128),
            vm(2, 16, 128),
            vm(4, 8, 128),
            vm(4, 8, 128),
            vm(3, ngz, 8, 8, 128),
            vm(ngz, 4, 8, 128),
            vm(ngz, 90, 128),
            vm(ngz, 16, 128),
            vm(ngz + 1, 24, 128),
            vm(ngz, 18, 128),
            vm(ngz, 18, 128),
            vm(16, 24, 128),
            vm(16, 24, 128),
            vm(ngx, 8, 128),
            vm(ngx, 4, 128),
            vm(2, 16, 128),
            vm(2, ngz, 16, 128),
            vm(8, 8, 128),
            vm(2, 8, 8, 128),
            vm(2, 16, 128),
            vm(ngz, 16, 128),
            vm(ngz, 16, 128),
            vm(4, 16, 128),
        ]
        for shape in ((8,), (3, ngz), (3, ngz), (ngz,), (ngz,), (ngx,), (ngx,), (2,)):
            scratch += [pltpu.SemaphoreType.DMA(shape)] * 2
        result = pl.pallas_call(
            lambda *refs: kernel(ngx, ngz, *refs),
            out_shape=jax.ShapeDtypeStruct((nx * nz, ny), F32),
            in_specs=[
                pl.BlockSpec(memory_space=pl.ANY),
                pl.BlockSpec(memory_space=pl.ANY),
                pl.BlockSpec(memory_space=pltpu.SMEM),
                pl.BlockSpec(memory_space=pltpu.SMEM),
            ],
            out_specs=pl.BlockSpec(memory_space=pltpu.VMEM),
            scratch_shapes=scratch,
            compiler_params=pltpu.CompilerParams(collective_id=0, has_side_effects=True, vmem_limit_bytes=55040 << 10),
            name="vcycle",
        )(codes.reshape(nx * nz, ny), charge.reshape(nx * nz, ny), eps_table, screen_table)
        return result.reshape(nx, nz, ny)

    return jax.shard_map(
        per_device,
        mesh=mesh,
        in_specs=(P("gx", "gz", None), P("gx", "gz", None), P(), P()),
        out_specs=P("gx", "gz", None),
        check_vma=False,
    )
```

```python
import jax
import jax.numpy as jnp
from jax import lax
from jax.experimental import pallas as pl
from jax.experimental.pallas import tpu as pltpu
from jax.sharding import PartitionSpec as P

OMEGA = 0.8
SWEEPS = 8
LAST = 6
F32 = jnp.float32
MESH = pl.DeviceIdType.MESH
FAR_FIRST = (4, 3, 5, 2, 6, 1, 7)


def iota(shape, dim):
    return lax.broadcasted_iota(jnp.int32, shape, dim)


def roll(v, shift, axis):
    size = v.shape[axis]
    return pltpu.roll(v, shift % size, axis)


class Level:
    def __init__(self, index, refs, whole, slab):
        (self.E, self.S, self.WXM, self.WXP, self.WYM, self.WYP, self.WZ, self.D, self.A, self.M, self.F, self.U, self.R, self.Y,
         self.V, self.C) = refs
        self.index, self.whole, self.n = index, whole, slab
        self.Z, self.X = self.S.shape[0], self.S.shape[1]
        self.mask = None

    @staticmethod
    def scratch(Z, X):
        sizes = (Z + 2, Z, Z, Z, Z, Z, Z + 1, Z, Z + 1, Z, Z, Z, Z, Z, Z + 2, Z + 2)
        return [pltpu.VMEM((s, X, 128), F32) for s in sizes]


def loop(count, body):
    def step(i, carry):
        body(i)
        return carry

    lax.fori_loop(0, count, step, 0)


def unrolled(count, body):
    for i in range(count):
        body(i)


def couplings(lev, z0, n):
    h = 0.5 ** lev.index * 0.5
    sh = 2 ** lev.index
    X = lev.X
    e = lev.E[pl.ds(z0 + 1, n)]
    lane = iota((n, X, 128), 2)
    first, last = lane < sh, lane >= 128 - sh
    up, down = roll(e, 1, 1), roll(e, -1, 1)
    if lev.whole:
        row = iota((n, X, 128), 1)
        up, down = jnp.where(row == 0, 0.0, up), jnp.where(row == X - 1, 0.0, down)
    left, right = jnp.where(first, 0.0, roll(e, sh, 2)), jnp.where(last, 0.0, roll(e, -sh, 2))
    wxm, wxp, wym, wyp = h * (e + up), h * (e + down), h * (e + left), h * (e + right)
    wzm, wzp = h * (e + lev.E[pl.ds(z0, n)]), h * (e + lev.E[pl.ds(z0 + 2, n)])
    lev.D[pl.ds(z0, n)] = wxm + wxp + wzm + wzp + wym + wyp + lev.S[pl.ds(z0, n)]
    if lev.whole:
        wxm, wxp = jnp.where(row == 0, 0.0, wxm), jnp.where(row == X - 1, 0.0, wxp)
    lev.WXM[pl.ds(z0, n)] = wxm
    lev.WXP[pl.ds(z0, n)] = wxp
    lev.WYM[pl.ds(z0, n)] = jnp.where(first, 0.0, wym)
    lev.WYP[pl.ds(z0, n)] = jnp.where(last, 0.0, wyp)
    lev.WZ[pl.ds(z0, n)] = wzm
    return wzp


def lateral(lev, u, z0, n):
    sh = 2 ** lev.index
    return (
        lev.WXM[pl.ds(z0, n)] * roll(u, 1, 1)
        + lev.WXP[pl.ds(z0, n)] * roll(u, -1, 1)
        + lev.WYM[pl.ds(z0, n)] * roll(u, sh, 2)
        + lev.WYP[pl.ds(z0, n)] * roll(u, -sh, 2)
    )


def steps_of(count):
    if count <= 64:
        return count
    return 8 if count % 8 == 0 else 1


def prepare(lev):
    Z, X, n = lev.Z, lev.X, lev.n
    zero = jnp.zeros((1, X, 128), F32)
    lev.E[0:1] = zero
    lev.E[Z + 1 : Z + 2] = zero
    unrolled(Z // n, lambda i: couplings(lev, i * n, n))
    lev.WZ[0:1] = zero
    lev.WZ[Z : Z + 1] = zero
    lev.A[Z : Z + 1] = zero
    s = steps_of(Z)

    def body(i, m):
        for j in range(s):
            z = i * s + j
            w = lev.WZ[z]
            a = w * m
            m = 1.0 / (lev.D[z] - w * a)
            lev.A[z] = a
            lev.M[z] = m
        return m

    lax.fori_loop(0, Z // s, body, jnp.zeros((X, 128), F32))


def sweep(lev, src, finish):
    Z, X = lev.Z, lev.X
    s = steps_of(Z)

    def forward(i, y):
        for j in range(s):
            z = i * s + j
            y = src[z] + lev.A[z] * y
            lev.Y[z] = y
        return y

    def backward(i, x):
        for j in range(s):
            z = Z - 1 - (i * s + j)
            x = lev.M[z] * lev.Y[z] + lev.A[z + 1] * x
            finish(z, x)
        return x

    lax.fori_loop(0, Z // s, forward, jnp.zeros((X, 128), F32))
    lax.fori_loop(0, Z // s, backward, jnp.zeros((X, 128), F32))


def pair_lanes(v, index):
    sh = 2 ** index
    lane = iota(v.shape, v.ndim - 1)
    other = jnp.where((lane & sh) == 0, roll(v, -sh, v.ndim - 1), roll(v, sh, v.ndim - 1))
    return v + other


def halve(v, index, tmp, at=0):
    n, X = v.shape[0], v.shape[1]
    v = v.reshape(n // 2, 2, X, 128)
    v = pair_lanes(v[:, 0] + v[:, 1], index)
    part = slice(at, at + n // 2)
    tmp[part, 0:X, :] = v
    return 0.125 * (tmp[part, pl.ds(0, X // 2, stride=2), :] + tmp[part, pl.ds(1, X // 2, stride=2), :])


def pre(lev):
    def finish(z, x):
        lev.U[z] = OMEGA * x

    sweep(lev, lev.F, finish)
    n = lev.n

    def body(i):
        z0 = i * n
        r = (1.0 - OMEGA) * lev.F[pl.ds(z0, n)] + lateral(lev, lev.U[pl.ds(z0, n)], z0, n)
        if lev.mask is not None:
            r = jnp.where(lev.mask[None] > 0, r, 0.0)
        lev.R[pl.ds(z0, n)] = r

    unrolled(lev.Z // n, body)


def post(lev):
    n, Z = lev.n, lev.Z
    zero = jnp.zeros((1, lev.X, 128), F32)
    lev.V[0:1] = zero
    lev.V[Z + 1 : Z + 2] = zero

    def body(i):
        z0 = i * n
        v = lev.V[pl.ds(z0 + 1, n)]
        around = lateral(lev, v, z0, n) + lev.WZ[pl.ds(z0, n)] * lev.V[pl.ds(z0, n)] + lev.WZ[pl.ds(z0 + 1, n)] * lev.V[pl.ds(z0 + 2, n)]
        r = lev.R[pl.ds(z0, n)] - (lev.D[pl.ds(z0, n)] * v - around)
        if lev.mask is not None:
            r = jnp.where(lev.mask[None] > 0, r, 0.0)
        lev.F[pl.ds(z0, n)] = r

    unrolled(Z // n, body)

    def finish(z, x):
        lev.C[z + 1] = lev.U[z] + lev.V[z + 1] + OMEGA * x

    sweep(lev, lev.F, finish)


def coarsest(lev):
    Z = lev.Z
    sh = 2 ** lev.index
    f = [lev.F[z] for z in range(Z)]
    a = [lev.A[z] for z in range(Z + 1)]
    m = [lev.M[z] for z in range(Z)]
    w = [(lev.WXM[z], lev.WXP[z], lev.WYM[z], lev.WYP[z]) for z in range(Z)]

    def solved(r):
        y = [r[0]]
        for z in range(1, Z):
            y.append(r[z] + a[z] * y[-1])
        x = [None] * Z
        x[Z - 1] = m[Z - 1] * y[Z - 1]
        for z in range(Z - 2, -1, -1):
            x[z] = m[z] * y[z] + a[z + 1] * x[z + 1]
        return x

    u = [OMEGA * x for x in solved(f)]
    for _ in range(SWEEPS - 1):
        r = []
        for z in range(Z):
            xm, xp, ym, yp = w[z]
            side = xm * roll(u[z], 1, 0) + xp * roll(u[z], -1, 0)
            r.append(f[z] + (side + (ym * roll(u[z], sh, 1) + yp * roll(u[z], -sh, 1))))
        x = solved(r)
        u = [(1.0 - OMEGA) * u[z] + OMEGA * x[z] for z in range(Z)]
    for z in range(Z):
        lev.C[z + 1] = u[z]


def spread_rows(dst, z, c, rows):
    for source, count, target in rows:
        part = c[source : source + count]
        for k in range(2):
            for j in range(2):
                dst[z + k, pl.ds(target + j, count, stride=2), :] = part


def kernel(ngx, ngz, *refs):
    codes_in, charge_in, eps_t, scr_t, out = refs[:5]
    refs = list(refs[5:])

    def take(count):
        got = refs[:count]
        del refs[:count]
        return got

    l0 = Level(0, take(16), False, 4)
    l1 = Level(1, take(16), False, 8)
    l2 = Level(2, take(16), False, 8)
    l3 = Level(3, take(16), True, 4)
    l4 = Level(4, take(16), True, 4)
    l5 = Level(5, take(16), True, 4)
    l6 = Level(6, take(16), True, 2)
    (tmp, codes, charge, s_in, xs, xr, zs, zr, ds, dr, es, f1, red, post_red, ub, rm, ra, av, bv, es3, f3, fh, fr, f2, f2r, ps, rb, pivots, mid) = take(29)
    (s_r1, r_r1, s_es, r_es, s_f1, r_f1, s_red, r_red, s_post, r_post, s_e3, r_e3, s_f3, r_f3, s_f2, r_f2) = take(16)

    gx, gz = lax.axis_index("gx"), lax.axis_index("gz")

    def gx_at(k):
        return lax.rem(gx + (k + ngx), ngx)

    def gz_at(k):
        return lax.rem(gz + (k + ngz), ngz)

    def remote(src, dst, ss, rs, tx, tz):
        return pltpu.make_async_remote_copy(src, dst, ss, rs, device_id=(tx, tz), device_id_type=MESH)

    inputs = (pltpu.make_async_copy(codes_in, codes, s_in.at[0]), pltpu.make_async_copy(charge_in, charge, s_in.at[1]))
    for copy in inputs:
        copy.start()

    barrier = pltpu.get_barrier_semaphore()

    def hello(tx, tz):
        pl.semaphore_signal(barrier, 1, device_id=(tx, tz), device_id_type=MESH)

    loop(ngz - 1, lambda k: hello(gx, gz_at(k + 1)))
    loop(ngz, lambda k: hello(gx_at(1), gz_at(k)))
    loop(ngz, lambda k: hello(gx_at(-1), gz_at(k)))
    loop(ngx - 3, lambda k: hello(gx_at(k + 2), gz))

    row24, row16 = iota((24, 128), 0), iota((16, 128), 0)
    has_right, has_left = gx < ngx - 1, gx > 0
    lane = iota((1, 8, 128), 2)

    table_e = [jnp.full((16, 128), eps_t[k], F32) for k in range(eps_t.shape[0])]
    table_s = [jnp.full((16, 128), scr_t[k], F32) for k in range(eps_t.shape[0])]

    def look(i):
        c = codes[pl.ds(i, 16, stride=16), :]
        e = jnp.zeros((16, 128), F32)
        s = jnp.zeros((16, 128), F32)
        for k in range(eps_t.shape[0]):
            e = jnp.where(c == k, table_e[k], e)
            s = jnp.where(c == k, table_s[k], s)
        l0.E[i + 1, 0:16, :] = e
        l0.S[i, 0:16, :] = s
        l0.F[i, 0:16, :] = charge[pl.ds(i, 16, stride=16), :]

    for copy in inputs:
        copy.wait()
    unrolled(16, look)

    xs[0, :, 0:2, :] = l0.E[1:17, 14:16, :]
    xs[0, :, 2:3, :] = l0.S[:, 15:16, :]
    xs[0, :, 3:4, :] = l0.F[:, 15:16, :]
    xs[1, :, 0:2, :] = l0.E[1:17, 0:2, :]
    xs[1, :, 2:3, :] = l0.S[:, 0:1, :]
    xs[1, :, 3:4, :] = l0.F[:, 0:1, :]
    zs[0] = l0.E[16, 0:16, :]
    zs[1] = l0.E[1, 0:16, :]
    ds[0] = l0.E[16, 8:16, :]
    ds[1] = l0.E[16, 0:8, :]
    ds[2] = l0.E[1, 8:16, :]
    ds[3] = l0.E[1, 0:8, :]

    def pack2(v):
        v = v.reshape(4, 2, 8, 128)
        return jnp.where((lane & 1) == 0, v[:, 0], v[:, 1])

    es[0, gz, 0:4] = pack2(halve(l0.E[1:17, 0:16, :], 0, tmp))
    es[0, gz, 4:8] = pack2(halve(l0.S[:, 0:16, :], 0, tmp, 8))

    def r1_copies():
        return [
            remote(xs.at[0], xr.at[0], s_r1.at[0], r_r1.at[0], gx_at(1), gz),
            remote(xs.at[1], xr.at[1], s_r1.at[1], r_r1.at[1], gx_at(-1), gz),
            remote(zs.at[0], zr.at[0], s_r1.at[2], r_r1.at[2], gx, gz_at(1)),
            remote(zs.at[1], zr.at[1], s_r1.at[3], r_r1.at[3], gx, gz_at(-1)),
            remote(ds.at[0], dr.at[0], s_r1.at[4], r_r1.at[4], gx_at(1), gz_at(1)),
            remote(ds.at[1], dr.at[1], s_r1.at[5], r_r1.at[5], gx_at(-1), gz_at(1)),
            remote(ds.at[2], dr.at[2], s_r1.at[6], r_r1.at[6], gx_at(1), gz_at(-1)),
            remote(ds.at[3], dr.at[3], s_r1.at[7], r_r1.at[7], gx_at(-1), gz_at(-1)),
        ]

    pl.semaphore_wait(barrier, 3 * ngz - 1 + ngx - 3)
    for copy in r1_copies():
        copy.start()

    def f1_copies(act):
        def go(slot, k, src, dst, tx):
            act(remote(src, dst, s_f1.at[slot, k], r_f1.at[slot, gz], tx, gz_at(k)))

        for k in (4, 3, 5, 2, 6, 1, 7, 0):
            if k:
                go(0, k, f1.at[gz], f1.at[gz], gx)
            go(1, k, fh.at[0], fr.at[0, gz], gx_at(1))
            go(2, k, fh.at[1], fr.at[1, gz], gx_at(-1))

    def f1_arrive():
        def get(slot, dst, k):
            p = gz_at(k)
            remote(dst, dst, s_f1.at[slot, k], r_f1.at[slot, p], gx, gz_at(1)).wait_recv()

        loop(ngz - 1, lambda k: get(0, f1.at[gz], k + 1))
        loop(ngz, lambda k: get(1, fr.at[0, gz], k))
        loop(ngz, lambda k: get(2, fr.at[1, gz], k))

    def es_lines(act):
        for k in FAR_FIRST:
            act(remote(es.at[0, gz], es.at[0, gz], s_es.at[0, k], r_es.at[0, gz], gx, gz_at(k)))

    def es_planes():
        return [
            remote(es.at[0], es.at[2], s_es.at[2, 0], r_es.at[2, 0], gx_at(1), gz),
            remote(es.at[0], es.at[1], s_es.at[1, 0], r_es.at[1, 0], gx_at(-1), gz),
        ]

    es_lines(lambda c: c.start())

    for copy in r1_copies():
        copy.wait_recv()

    above, below = gz > 0, gz < ngz - 1
    zero16 = jnp.zeros((16, 24, 128), F32)
    l0.E[0:1] = zero16[0:1]
    l0.E[17:18] = zero16[0:1]
    l0.E[1:17, 16:24, :] = zero16[:, 0:8]
    l0.S[:, 16:24, :] = jnp.ones((16, 8, 128), F32)
    l0.F[:, 16:24, :] = zero16[:, 0:8]
    l0.E[1:17, 22:24, :] = jnp.where(has_left, xr[0, :, 0:2, :], 0.0)
    l0.S[:, 23:24, :] = jnp.where(has_left, xr[0, :, 2:3, :], 1.0)
    l0.F[:, 23:24, :] = jnp.where(has_left, xr[0, :, 3:4, :], 0.0)
    l0.E[1:17, 16:18, :] = jnp.where(has_right, xr[1, :, 0:2, :], 0.0)
    l0.S[:, 16:17, :] = jnp.where(has_right, xr[1, :, 2:3, :], 1.0)
    l0.F[:, 16:17, :] = jnp.where(has_right, xr[1, :, 3:4, :], 0.0)
    l0.E[0, 0:16, :] = jnp.where(above, zr[0], 0.0)
    l0.E[17, 0:16, :] = jnp.where(below, zr[1], 0.0)
    l0.E[0, 23:24, :] = jnp.where(above & has_left, dr[0, 7:8, :], 0.0)
    l0.E[0, 16:17, :] = jnp.where(above & has_right, dr[1, 0:1, :], 0.0)
    l0.E[17, 23:24, :] = jnp.where(below & has_left, dr[2, 7:8, :], 0.0)
    l0.E[17, 16:17, :] = jnp.where(below & has_right, dr[3, 0:1, :], 0.0)

    for i in range(4):
        wzp = couplings(l0, i * 4, 4)
    l0.WZ[16:17] = wzp[3:4]

    m = 1.0 / l0.D[0]
    l0.M[0] = m
    for z in range(1, 15):
        w = l0.WZ[z]
        a = w * m
        m = 1.0 / (l0.D[z] - w * a)
        l0.A[z] = a
        l0.M[z] = m
    lead = jnp.where(above, l0.WZ[0], 0.0)
    tail = l0.WZ[15]

    y = lead
    av[0] = y
    for z in range(1, 15):
        y = l0.A[z] * y
        av[z] = y
    x = l0.M[14] * y
    b = l0.M[14] * tail
    av[14] = x
    bv[14] = b
    for z in range(13, -1, -1):
        x = l0.M[z] * av[z] + l0.A[z + 1] * x
        b = l0.A[z + 1] * b
        av[z] = x
        bv[z] = b

    def inner(src):
        y = src[0]
        l0.Y[0] = y
        for z in range(1, 15):
            y = src[z] + l0.A[z] * y
            l0.Y[z] = y
        x = l0.M[14] * y
        l0.Y[14] = x
        for z in range(13, -1, -1):
            x = l0.M[z] * l0.Y[z] + l0.A[z + 1] * x
            l0.Y[z] = x

    inner(l0.F)

    def put(k, v):
        red[gz, pl.ds(k * 18, 17), :] = v[0:17]
        red[gz, pl.ds(k * 18 + 17, 1), :] = v[23:24]

    put(0, tail * av[14])
    put(1, l0.D[15] - tail * bv[14])
    put(2, lead * av[0])
    put(3, l0.F[15] + tail * l0.Y[14])
    put(4, lead * l0.Y[0])

    def gather(buf, ss, rs, act):
        for k in FAR_FIRST:
            act(remote(buf.at[gz], buf.at[gz], ss.at[k], rs.at[gz], gx, gz_at(k)))

    def post_copies(act):
        for k in FAR_FIRST:
            side = lax.div(gz + k, ngz)
            act(remote(ps.at[side], post_red.at[gz], s_post.at[k], r_post.at[gz], gx, gz_at(k)))

    def gathered(buf, ss, rs):
        def get(k):
            p = gz_at(k)
            remote(buf.at[gz], buf.at[p], ss.at[k], rs.at[p], gx, p).wait_recv()

        loop(ngz - 1, lambda k: get(k + 1))

    gather(red, s_red, r_red, lambda c: c.start())

    def es_line_in(k):
        p = gz_at(k + 1)
        remote(es.at[0, gz], es.at[0, p], s_es.at[0, k + 1], r_es.at[0, p], gx, p).wait_recv()

    loop(ngz - 1, es_line_in)
    for copy in es_planes():
        copy.start()

    mask1 = jnp.where(row24 < 8, 1.0, jnp.where(row24 < 16, jnp.where(has_right, 1.0, 0.0), jnp.where(has_left, 1.0, 0.0)))
    mask2 = jnp.where(
        row16 < 4,
        1.0,
        jnp.where(row16 < 8, jnp.where(has_right, 1.0, 0.0), jnp.where(row16 < 12, 0.0, jnp.where(has_left, 1.0, 0.0))),
    )
    l1.mask, l2.mask = mask1, mask2

    def unpack2(v):
        even = jnp.where((lane & 1) == 0, v, roll(v, 1, 2))
        odd = jnp.where((lane & 1) == 1, v, roll(v, -1, 2))
        return jnp.stack([even, odd], axis=1).reshape(2 * v.shape[0], 8, 128)

    here = (None, has_right, has_left)

    def place(buf, start, dst, offset, outside, slots):
        for slot in slots:
            for p in range(ngz):
                v = unpack2(buf[slot, p, start : start + 4])
                if slot:
                    v = jnp.where(here[slot], v, outside)
                dst[p * 8 + offset : p * 8 + offset + 8, slot * 8 : slot * 8 + 8, :] = v

    place(es, 0, l1.E, 1, 0.0, (0,))
    place(es, 4, l1.S, 0, 1.0, (0,))

    def coarsen(src, offset, fine, coarse, dst, dst_offset, split):
        n = fine.n

        def body(i):
            v = halve(src[i * n + offset : (i + 1) * n + offset], fine.index, tmp, i * (n // 2))
            at = slice(i * (n // 2) + dst_offset, (i + 1) * (n // 2) + dst_offset)
            if split:
                dst[at, 0:8, :] = v[:, 0:8]
                dst[at, 12:16, :] = v[:, 8:12]
            else:
                dst[at] = v

        unrolled(fine.Z // n, body)

    def filler(ref, value):
        ref[:, 8:12, :] = jnp.full((ref.shape[0], 4, 128), value, F32)

    filler(l2.E, 0.0)
    filler(l2.S, 1.0)
    filler(l2.F, 0.0)

    lane3 = iota((2, 2, 128), 2)

    def pack8(src, offset, buf, first):
        for i in range(2):
            v = halve(src[i * 16 + offset : i * 16 + offset + 16], 2, tmp, i * 8)[:, 0:2]
            tmp[i * 8 : i * 8 + 8, 32:34, :] = v
        v = tmp[0:16, 32:34, :].reshape(2, 8, 2, 128)
        picked = v[:, 7]
        for k in range(7):
            picked = jnp.where((lane3 & 7) == k, v[:, k], picked)
        for zz in range(2):
            buf[gx, first + zz * 2 : first + zz * 2 + 2, :] = picked[zz]

    core, x4, y4 = lax.rem(gx, 2), lax.rem(lax.div(gx, 2), 4), lax.div(gx, 8)
    hops = sorted(((dy, dx, dc) for dy in range(4) for dx in range(4) for dc in range(2)), key=lambda t: -(min(t[0], 4 - t[0]) + min(t[1], 4 - t[1]) + 0.5 * t[2]))
    far_gx = [lax.rem(y4 + dy, 4) * 8 + lax.rem(x4 + dx, 4) * 2 + lax.rem(core + dc, 2) for dy, dx, dc in hops[:-1]]

    def spread(buf, ss, rs, act):
        for i, tx in enumerate(far_gx):
            act(remote(buf.at[gx], buf.at[gx], ss.at[i], rs.at[gx], tx, gz))

    def collected(buf, ss, rs):
        def get(k):
            p = gx_at(k)
            remote(buf.at[gx], buf.at[p], ss.at[k], rs.at[p], p, gz).wait_recv()

        loop(ngx - 1, lambda k: get(k + 1))

    gathered(red, s_red, r_red)

    def got(p, k):
        return red[p, pl.ds(k * 18, 18), :]

    m, y = None, None
    for p in range(ngz):
        diag, right = got(p, 1), got(p, 3)
        if p + 1 < ngz:
            diag, right = diag - got(p + 1, 2), right + got(p + 1, 4)
        if p:
            c = got(p, 0)
            a = c * m
            diag, right = diag - c * a, right + a * y
            ra[p] = a
        m, y = 1.0 / diag, right
        rm[p] = m
        ub[p + 1, 0:18, :] = y
    x = m * y
    for p in range(ngz - 1, -1, -1):
        if p + 1 < ngz:
            x = rm[p] * ub[p + 1, 0:18, :] + ra[p + 1] * x
        ub[p + 1, 0:17, :] = x[0:17]
        ub[p + 1, 23:24, :] = x[17:18]
        ub[p + 1, 17:23, :] = jnp.zeros((6, 128), F32)
    ub[0] = jnp.zeros((24, 128), F32)

    before, own = ub[gz], ub[gz + 1]
    for z in range(15):
        l0.U[z] = OMEGA * (l0.Y[z] + av[z] * before + bv[z] * own)
    l0.U[15] = OMEGA * own

    def first_residual(i):
        z0 = i * 4
        l0.R[pl.ds(z0, 4)] = (1.0 - OMEGA) * l0.F[pl.ds(z0, 4)] + lateral(l0, l0.U[pl.ds(z0, 4)], z0, 4)

    unrolled(4, first_residual)
    packed = pack2(halve(l0.R[:, 0:16, :], 0, tmp))
    f1[gz] = packed
    for zz in range(4):
        fh[0, zz * 4 : zz * 4 + 4, :] = packed[zz, 4:8]
        fh[1, zz * 4 : zz * 4 + 4, :] = packed[zz, 0:4]
    f1_copies(lambda c: c.start())

    q = got(ngz - 1, 1)[0:16]
    pivots[ngz - 1] = q
    for p in range(ngz - 1, 0, -1):
        c = got(p, 0)[0:16]
        b = c * (1.0 / q)
        rb[p] = b
        q = got(p - 1, 1)[0:16] - got(p, 2)[0:16] - c * b
        pivots[p - 1] = q
    rb[0] = jnp.zeros((16, 128), F32)
    c = jnp.where(above, red[gz, 0:16, :], 0.0)
    left = rm[jnp.maximum(gz - 1, 0), 0:16, :]
    mid[0] = left
    mid[1] = c * left
    mid[2] = 1.0 / (pivots[gz] - c * c * left)
    mid[3] = c

    for copy in es_planes():
        copy.wait_recv()
    place(es, 0, l1.E, 1, 0.0, (1, 2))
    place(es, 4, l1.S, 0, 1.0, (1, 2))
    coarsen(l1.E, 1, l1, l2, l2.E, 1, True)
    coarsen(l1.S, 0, l1, l2, l2.S, 0, True)
    pack8(l2.E, 1, es3, 0)
    pack8(l2.S, 0, es3, 4)
    spread(es3, s_e3, r_e3, lambda c: c.start())
    prepare(l1)
    prepare(l2)

    lane32 = iota((32, 128), 1)

    def swap(v, s):
        return jnp.where((lane32 & s) == 0, roll(v, -s, 1), roll(v, s, 1))

    def place8(buf, first, dst, offset):
        for zz in range(2):
            for xp in range(2):
                found = [(buf[:, first + zz * 2 + xp, :], 0)]
                for bit in (1, 2, 4):
                    split = []
                    for v, z in found:
                        w = swap(v, bit)
                        low = (lane32 & bit) == 0
                        split += [(jnp.where(low, v, w), z), (jnp.where(low, w, v), z + bit)]
                    found = split
                for v, z in found:
                    dst[offset + zz * 8 + z, pl.ds(xp, ngx, stride=2), :] = v

    l1.F[:, 8:24, :] = jnp.zeros((l1.Z, 16, 128), F32)
    lane16 = iota((16, 128), 1)
    f1_arrive()
    for p in range(ngz):
        l1.F[p * 8 : p * 8 + 8, 0:8, :] = unpack2(f1[p])
        for side, present, row in ((0, has_left, 20), (1, has_right, 8)):
            v = jnp.where(present, fr[side, p], 0.0)
            both = (jnp.where((lane16 & 1) == 0, v, roll(v, 1, 1)), jnp.where((lane16 & 1) == 1, v, roll(v, -1, 1)))
            for zz in range(4):
                for k in range(2):
                    l1.F[p * 8 + zz * 2 + k, row : row + 4, :] = both[k][zz * 4 : zz * 4 + 4]
    pre(l1)
    coarsen(l1.R, 0, l1, l2, l2.F, 0, True)
    lane8 = iota((8, 8, 128), 2)
    v = l2.F[:, 0:8, :].reshape(8, 4, 8, 128)
    k = lane8 & 3
    f2[...] = jnp.where(k == 0, v[:, 0], jnp.where(k == 1, v[:, 1], jnp.where(k == 2, v[:, 2], v[:, 3])))

    def f2_copies():
        return [
            remote(f2, f2r.at[0], s_f2.at[0], r_f2.at[0], gx_at(1), gz),
            remote(f2, f2r.at[1], s_f2.at[1], r_f2.at[1], gx_at(-1), gz),
        ]

    for copy in f2_copies():
        copy.start()

    pre(l2)
    pack8(l2.R, 0, f3, 0)
    spread(f3, s_f3, r_f3, lambda c: c.start())

    collected(es3, s_e3, r_e3)
    place8(es3, 0, l3.E, 1)
    place8(es3, 4, l3.S, 0)
    deep = [l3, l4, l5, l6]
    for fine, coarse in zip(deep[:-1], deep[1:]):
        coarsen(fine.E, 1, fine, coarse, coarse.E, 1, False)
        coarsen(fine.S, 0, fine, coarse, coarse.S, 0, False)
    for lev in deep:
        prepare(lev)

    for copy in f2_copies():
        copy.wait_recv()

    def swap8(v, s):
        return jnp.where((lane8 & s) == 0, roll(v, -s, 2), roll(v, s, 2))

    for side, present, source, row in ((0, has_left, 2, 14), (1, has_right, 1, 5)):
        v = jnp.where(present, f2r[side], 0.0)
        w = swap8(v, 1)
        for k0 in range(2):
            v1 = jnp.where((lane8 & 1) == k0, v, w)
            w1 = swap8(v1, 2)
            for k1 in range(2):
                v2 = jnp.where(((lane8 >> 1) & 1) == k1, v1, w1)
                for zz in range(8):
                    l2.F[zz * 4 + k1 * 2 + k0, row : row + 1, :] = v2[zz, source : source + 1]
    pre(l2)

    collected(f3, s_f3, r_f3)
    place8(f3, 0, l3.F, 0)
    for fine, coarse in zip(deep[:-1], deep[1:]):
        pre(fine)
        coarsen(fine.R, 0, fine, coarse, coarse.F, 0, False)
    coarsest(l6)
    for fine, coarse in zip(deep[-2::-1], deep[:0:-1]):
        unrolled(coarse.Z, lambda z, fine=fine, coarse=coarse: spread_rows(fine.V, 2 * z + 1, coarse.C[z + 1], ((0, coarse.X, 0),)))
        post(fine)

    tiles = ngx // 4
    first = gx // 4
    shift = lax.rem(24 - 2 * lax.rem(gx, 4), 24)

    def tile_at(z, k):
        return l3.C[z, pl.ds(pl.multiple_of(lax.rem(first + (k + tiles), tiles) * 8, 8), 8), :]

    right_rows, left_rows = (iota((4, 128), 0) < 2) | has_right, has_left

    def down3(z):
        c = jnp.concatenate([tile_at(z + 1, 0), tile_at(z + 1, 1), tile_at(z + 1, -1)], axis=0)
        c = pltpu.roll(c, shift, 0)
        for k in range(2):
            for j in range(2):
                l2.V[2 * z + 1 + k, pl.ds(j, 4, stride=2), :] = jnp.where(right_rows, c[0:4], 0.0)
                l2.V[2 * z + 1 + k, pl.ds(12 + j, 2, stride=2), :] = jnp.where(left_rows, c[22:24], 0.0)

    filler(l2.V, 0.0)
    unrolled(l3.Z, down3)
    post(l2)
    unrolled(l2.Z, lambda z: spread_rows(l1.V, 2 * z + 1, l2.C[z + 1], ((0, 4, 0), (4, 4, 8), (12, 4, 16))))
    post(l1)
    l1.C[0] = jnp.zeros((24, 128), F32)
    l1.C[l1.Z + 1] = jnp.zeros((24, 128), F32)

    for i in range(10):
        c = l1.C[gz * 8 + i]
        for z in (2 * i - 1, 2 * i):
            if 0 <= z < 18:
                for j in range(2):
                    l0.V[z, pl.ds(j, 8, stride=2), :] = c[0:8]
                l0.V[z, 16:17, :] = c[8:9]
                l0.V[z, 17:23, :] = jnp.zeros((6, 128), F32)
                l0.V[z, 23:24, :] = c[23:24]

    def second_residual(i):
        z0 = i * 4
        v = l0.V[pl.ds(z0 + 1, 4)]
        around = lateral(l0, v, z0, 4) + l0.WZ[pl.ds(z0, 4)] * l0.V[pl.ds(z0, 4)] + l0.WZ[pl.ds(z0 + 1, 4)] * l0.V[pl.ds(z0 + 2, 4)]
        l0.F[pl.ds(z0, 4)] = l0.R[pl.ds(z0, 4)] - (l0.D[pl.ds(z0, 4)] * v - around)

    unrolled(4, second_residual)
    inner(l0.F)
    end_row, first_row = (l0.F[15] + tail * l0.Y[14])[0:16], (lead * l0.Y[0])[0:16]
    ps[0] = end_row + jnp.where(above, ra[gz, 0:16, :], 0.0) * first_row
    ps[1] = first_row + rb[gz] * end_row
    post_red[gz] = jnp.zeros((16, 128), F32)
    post_copies(lambda c: c.start())
    for z in range(16):
        l0.U[z, 0:16, :] = l0.U[z, 0:16, :] + l0.V[z + 1, 0:16, :]
    for copy in r1_copies():
        copy.wait_send()
    es_lines(lambda c: c.wait_send())
    for copy in es_planes():
        copy.wait_send()
    f1_copies(lambda c: c.wait_send())
    for copy in f2_copies():
        copy.wait_send()
    gather(red, s_red, r_red, lambda c: c.wait_send())
    spread(es3, s_e3, r_e3, lambda c: c.wait_send())
    spread(f3, s_f3, r_f3, lambda c: c.wait_send())
    gathered(post_red, s_post, r_post)
    tau = jnp.zeros((16, 128), F32)
    for p in range(ngz - 1):
        took = post_red[p] if p == 0 else post_red[p] + ra[p, 0:16, :] * tau
        tau = jnp.where(p < gz, took, tau)
    sigma = jnp.zeros((16, 128), F32)
    for p in range(ngz - 1, 0, -1):
        sigma = jnp.where(p > gz, post_red[p] + rb[p] * sigma, sigma)
    b1 = first_row + tau
    own = mid[2] * (end_row + sigma + mid[1] * b1)
    before = mid[0] * (b1 + mid[3] * own)
    for z in range(16):
        if z < 15:
            x = l0.Y[z, 0:16, :] + av[z, 0:16, :] * before + bv[z, 0:16, :] * own
        else:
            x = own
        out[pl.ds(z, 16, stride=16), :] = l0.U[z, 0:16, :] + OMEGA * x

    post_copies(lambda c: c.wait_send())


def solution(mesh):
    ngx, ngz = mesh.shape["gx"], mesh.shape["gz"]

    def per_device(charge, codes, eps_table, screen_table):
        nx, nz, ny = charge.shape
        whole_z, whole_x = nz * ngz, nx * ngx
        levels = [
            (nz, 24),
            (whole_z // 2, 24),
            (whole_z // 4, 16),
            (whole_z // 8, whole_x // 8),
            (whole_z // 16, whole_x // 16),
            (whole_z // 32, whole_x // 32),
            (whole_z // 64, whole_x // 64),
        ]
        scratch = []
        for Z, X in levels:
            scratch += Level.scratch(Z, X)
        vm = lambda *shape: pltpu.VMEM(shape, F32)
        scratch += [
            vm(64, 64, 128),
            pltpu.VMEM((nx * nz, ny), jnp.int32),
            vm(nx * nz, ny),
            pltpu.SemaphoreType.DMA((2,)),
            vm(2, 16, 4, 128),
            vm(2, 16, 4, 128),
            vm(2, 16, 128),
            vm(2, 16, 128),
            vm(4, 8, 128),
            vm(4, 8, 128),
            vm(3, ngz, 8, 8, 128),
            vm(ngz, 4, 8, 128),
            vm(ngz, 90, 128),
            vm(ngz, 16, 128),
            vm(ngz + 1, 24, 128),
            vm(ngz, 18, 128),
            vm(ngz, 18, 128),
            vm(16, 24, 128),
            vm(16, 24, 128),
            vm(ngx, 8, 128),
            vm(ngx, 4, 128),
            vm(2, 16, 128),
            vm(2, ngz, 16, 128),
            vm(8, 8, 128),
            vm(2, 8, 8, 128),
            vm(2, 16, 128),
            vm(ngz, 16, 128),
            vm(ngz, 16, 128),
            vm(4, 16, 128),
        ]
        for shape in ((8,), (3, ngz), (3, ngz), (ngz,), (ngz,), (ngx,), (ngx,), (2,)):
            scratch += [pltpu.SemaphoreType.DMA(shape)] * 2
        result = pl.pallas_call(
            lambda *refs: kernel(ngx, ngz, *refs),
            out_shape=jax.ShapeDtypeStruct((nx * nz, ny), F32),
            in_specs=[
                pl.BlockSpec(memory_space=pl.ANY),
                pl.BlockSpec(memory_space=pl.ANY),
                pl.BlockSpec(memory_space=pltpu.SMEM),
                pl.BlockSpec(memory_space=pltpu.SMEM),
            ],
            out_specs=pl.BlockSpec(memory_space=pltpu.VMEM),
            scratch_shapes=scratch,
            compiler_params=pltpu.CompilerParams(collective_id=0, has_side_effects=True, vmem_limit_bytes=55040 << 10),
            name="vcycle",
        )(codes.reshape(nx * nz, ny), charge.reshape(nx * nz, ny), eps_table, screen_table)
        return result.reshape(nx, nz, ny)

    return jax.shard_map(
        per_device,
        mesh=mesh,
        in_specs=(P("gx", "gz", None), P("gx", "gz", None), P(), P()),
        out_specs=P("gx", "gz", None),
        check_vma=False,
    )
```

```python
import jax
import jax.numpy as jnp
from jax import lax
from jax.experimental import pallas as pl
from jax.experimental.pallas import tpu as pltpu
from jax.sharding import PartitionSpec as P

OMEGA = 0.8
SWEEPS = 8
LAST = 6
F32 = jnp.float32
MESH = pl.DeviceIdType.MESH
FAR_FIRST = (4, 3, 5, 2, 6, 1, 7)


def iota(shape, dim):
    return lax.broadcasted_iota(jnp.int32, shape, dim)


def roll(v, shift, axis):
    size = v.shape[axis]
    return pltpu.roll(v, shift % size, axis)


class Level:
    def __init__(self, index, refs, whole, slab):
        (self.E, self.S, self.WXM, self.WXP, self.WYM, self.WYP, self.WZ, self.D, self.A, self.M, self.F, self.U, self.R, self.Y,
         self.V, self.C) = refs
        self.index, self.whole, self.n = index, whole, slab
        self.Z, self.X = self.S.shape[0], self.S.shape[1]
        self.mask = None

    @staticmethod
    def scratch(Z, X):
        sizes = (Z + 2, Z, Z, Z, Z, Z, Z + 1, Z, Z + 1, Z, Z, Z, Z, Z, Z + 2, Z + 2)
        return [pltpu.VMEM((s, X, 128), F32) for s in sizes]


def loop(count, body):
    def step(i, carry):
        body(i)
        return carry

    lax.fori_loop(0, count, step, 0)


def unrolled(count, body):
    for i in range(count):
        body(i)


def couplings(lev, z0, n):
    h = 0.5 ** lev.index * 0.5
    sh = 2 ** lev.index
    X = lev.X
    e = lev.E[pl.ds(z0 + 1, n)]
    lane = iota((n, X, 128), 2)
    first, last = lane < sh, lane >= 128 - sh
    up, down = roll(e, 1, 1), roll(e, -1, 1)
    if lev.whole:
        row = iota((n, X, 128), 1)
        up, down = jnp.where(row == 0, 0.0, up), jnp.where(row == X - 1, 0.0, down)
    left, right = jnp.where(first, 0.0, roll(e, sh, 2)), jnp.where(last, 0.0, roll(e, -sh, 2))
    wxm, wxp, wym, wyp = h * (e + up), h * (e + down), h * (e + left), h * (e + right)
    wzm, wzp = h * (e + lev.E[pl.ds(z0, n)]), h * (e + lev.E[pl.ds(z0 + 2, n)])
    lev.D[pl.ds(z0, n)] = wxm + wxp + wzm + wzp + wym + wyp + lev.S[pl.ds(z0, n)]
    if lev.whole:
        wxm, wxp = jnp.where(row == 0, 0.0, wxm), jnp.where(row == X - 1, 0.0, wxp)
    lev.WXM[pl.ds(z0, n)] = wxm
    lev.WXP[pl.ds(z0, n)] = wxp
    lev.WYM[pl.ds(z0, n)] = jnp.where(first, 0.0, wym)
    lev.WYP[pl.ds(z0, n)] = jnp.where(last, 0.0, wyp)
    lev.WZ[pl.ds(z0, n)] = wzm
    return wzp


def lateral(lev, u, z0, n):
    sh = 2 ** lev.index
    return (
        lev.WXM[pl.ds(z0, n)] * roll(u, 1, 1)
        + lev.WXP[pl.ds(z0, n)] * roll(u, -1, 1)
        + lev.WYM[pl.ds(z0, n)] * roll(u, sh, 2)
        + lev.WYP[pl.ds(z0, n)] * roll(u, -sh, 2)
    )


def steps_of(count):
    if count <= 64:
        return count
    return 8 if count % 8 == 0 else 1


def prepare(lev):
    Z, X, n = lev.Z, lev.X, lev.n
    zero = jnp.zeros((1, X, 128), F32)
    lev.E[0:1] = zero
    lev.E[Z + 1 : Z + 2] = zero
    unrolled(Z // n, lambda i: couplings(lev, i * n, n))
    lev.WZ[0:1] = zero
    lev.WZ[Z : Z + 1] = zero
    lev.A[Z : Z + 1] = zero
    s = steps_of(Z)

    def body(i, m):
        for j in range(s):
            z = i * s + j
            w = lev.WZ[z]
            a = w * m
            m = 1.0 / (lev.D[z] - w * a)
            lev.A[z] = a
            lev.M[z] = m
        return m

    lax.fori_loop(0, Z // s, body, jnp.zeros((X, 128), F32))


def sweep(lev, src, finish):
    Z, X = lev.Z, lev.X
    s = steps_of(Z)

    def forward(i, y):
        for j in range(s):
            z = i * s + j
            y = src[z] + lev.A[z] * y
            lev.Y[z] = y
        return y

    def backward(i, x):
        for j in range(s):
            z = Z - 1 - (i * s + j)
            x = lev.M[z] * lev.Y[z] + lev.A[z + 1] * x
            finish(z, x)
        return x

    lax.fori_loop(0, Z // s, forward, jnp.zeros((X, 128), F32))
    lax.fori_loop(0, Z // s, backward, jnp.zeros((X, 128), F32))


def pair_lanes(v, index):
    sh = 2 ** index
    lane = iota(v.shape, v.ndim - 1)
    other = jnp.where((lane & sh) == 0, roll(v, -sh, v.ndim - 1), roll(v, sh, v.ndim - 1))
    return v + other


def halve(v, index, tmp, at=0):
    n, X = v.shape[0], v.shape[1]
    v = v.reshape(n // 2, 2, X, 128)
    v = pair_lanes(v[:, 0] + v[:, 1], index)
    part = slice(at, at + n // 2)
    tmp[part, 0:X, :] = v
    return 0.125 * (tmp[part, pl.ds(0, X // 2, stride=2), :] + tmp[part, pl.ds(1, X // 2, stride=2), :])


def pre(lev):
    def finish(z, x):
        lev.U[z] = OMEGA * x

    sweep(lev, lev.F, finish)
    n = lev.n

    def body(i):
        z0 = i * n
        r = (1.0 - OMEGA) * lev.F[pl.ds(z0, n)] + lateral(lev, lev.U[pl.ds(z0, n)], z0, n)
        if lev.mask is not None:
            r = jnp.where(lev.mask[None] > 0, r, 0.0)
        lev.R[pl.ds(z0, n)] = r

    unrolled(lev.Z // n, body)


def post(lev):
    n, Z = lev.n, lev.Z
    zero = jnp.zeros((1, lev.X, 128), F32)
    lev.V[0:1] = zero
    lev.V[Z + 1 : Z + 2] = zero

    def body(i):
        z0 = i * n
        v = lev.V[pl.ds(z0 + 1, n)]
        around = lateral(lev, v, z0, n) + lev.WZ[pl.ds(z0, n)] * lev.V[pl.ds(z0, n)] + lev.WZ[pl.ds(z0 + 1, n)] * lev.V[pl.ds(z0 + 2, n)]
        r = lev.R[pl.ds(z0, n)] - (lev.D[pl.ds(z0, n)] * v - around)
        if lev.mask is not None:
            r = jnp.where(lev.mask[None] > 0, r, 0.0)
        lev.F[pl.ds(z0, n)] = r

    unrolled(Z // n, body)

    def finish(z, x):
        lev.C[z + 1] = lev.U[z] + lev.V[z + 1] + OMEGA * x

    sweep(lev, lev.F, finish)


def coarsest(lev):
    Z = lev.Z
    sh = 2 ** lev.index
    f = [lev.F[z] for z in range(Z)]
    a = [lev.A[z] for z in range(Z + 1)]
    m = [lev.M[z] for z in range(Z)]
    w = [(lev.WXM[z], lev.WXP[z], lev.WYM[z], lev.WYP[z]) for z in range(Z)]

    def solved(r):
        y = [r[0]]
        for z in range(1, Z):
            y.append(r[z] + a[z] * y[-1])
        x = [None] * Z
        x[Z - 1] = m[Z - 1] * y[Z - 1]
        for z in range(Z - 2, -1, -1):
            x[z] = m[z] * y[z] + a[z + 1] * x[z + 1]
        return x

    u = [OMEGA * x for x in solved(f)]
    for _ in range(SWEEPS - 1):
        r = []
        for z in range(Z):
            xm, xp, ym, yp = w[z]
            side = xm * roll(u[z], 1, 0) + xp * roll(u[z], -1, 0)
            r.append(f[z] + (side + (ym * roll(u[z], sh, 1) + yp * roll(u[z], -sh, 1))))
        x = solved(r)
        u = [(1.0 - OMEGA) * u[z] + OMEGA * x[z] for z in range(Z)]
    for z in range(Z):
        lev.C[z + 1] = u[z]


def spread_rows(dst, z, c, rows):
    for source, count, target in rows:
        part = c[source : source + count]
        for k in range(2):
            for j in range(2):
                dst[z + k, pl.ds(target + j, count, stride=2), :] = part


def kernel(ngx, ngz, *refs):
    codes_in, charge_in, eps_t, scr_t, out = refs[:5]
    refs = list(refs[5:])

    def take(count):
        got = refs[:count]
        del refs[:count]
        return got

    l0 = Level(0, take(16), False, 4)
    l1 = Level(1, take(16), False, 8)
    l2 = Level(2, take(16), False, 8)
    l3 = Level(3, take(16), True, 4)
    l4 = Level(4, take(16), True, 4)
    l5 = Level(5, take(16), True, 4)
    l6 = Level(6, take(16), True, 2)
    (tmp, codes, charge, s_in, xs, xr, zs, zr, ds, dr, es, f1, red, post_red, ub, rm, ra, av, bv, es3, f3, fh, fr, f2, f2r, ps, rb, pivots, mid) = take(29)
    (s_r1, r_r1, s_es, r_es, s_f1, r_f1, s_red, r_red, s_post, r_post, s_e3, r_e3, s_f3, r_f3, s_f2, r_f2) = take(16)

    gx, gz = lax.axis_index("gx"), lax.axis_index("gz")

    def gx_at(k):
        return lax.rem(gx + (k + ngx), ngx)

    def gz_at(k):
        return lax.rem(gz + (k + ngz), ngz)

    def remote(src, dst, ss, rs, tx, tz):
        return pltpu.make_async_remote_copy(src, dst, ss, rs, device_id=(tx, tz), device_id_type=MESH)

    inputs = (pltpu.make_async_copy(codes_in, codes, s_in.at[0]), pltpu.make_async_copy(charge_in, charge, s_in.at[1]))
    for copy in inputs:
        copy.start()

    barrier = pltpu.get_barrier_semaphore()

    def hello(tx, tz):
        pl.semaphore_signal(barrier, 1, device_id=(tx, tz), device_id_type=MESH)

    loop(ngz - 1, lambda k: hello(gx, gz_at(k + 1)))
    loop(ngz, lambda k: hello(gx_at(1), gz_at(k)))
    loop(ngz, lambda k: hello(gx_at(-1), gz_at(k)))
    loop(ngx - 3, lambda k: hello(gx_at(k + 2), gz))

    row24, row16 = iota((24, 128), 0), iota((16, 128), 0)
    has_right, has_left = gx < ngx - 1, gx > 0
    lane = iota((1, 8, 128), 2)

    table_e = [jnp.full((16, 128), eps_t[k], F32) for k in range(eps_t.shape[0])]
    table_s = [jnp.full((16, 128), scr_t[k], F32) for k in range(eps_t.shape[0])]

    def look(i):
        c = codes[pl.ds(i, 16, stride=16), :]
        e = jnp.zeros((16, 128), F32)
        s = jnp.zeros((16, 128), F32)
        for k in range(eps_t.shape[0]):
            e = jnp.where(c == k, table_e[k], e)
            s = jnp.where(c == k, table_s[k], s)
        l0.E[i + 1, 0:16, :] = e
        l0.S[i, 0:16, :] = s
        l0.F[i, 0:16, :] = charge[pl.ds(i, 16, stride=16), :]

    for copy in inputs:
        copy.wait()
    unrolled(16, look)

    xs[0, :, 0:2, :] = l0.E[1:17, 14:16, :]
    xs[0, :, 2:3, :] = l0.S[:, 15:16, :]
    xs[0, :, 3:4, :] = l0.F[:, 15:16, :]
    xs[1, :, 0:2, :] = l0.E[1:17, 0:2, :]
    xs[1, :, 2:3, :] = l0.S[:, 0:1, :]
    xs[1, :, 3:4, :] = l0.F[:, 0:1, :]
    zs[0] = l0.E[16, 0:16, :]
    zs[1] = l0.E[1, 0:16, :]
    ds[0] = l0.E[16, 8:16, :]
    ds[1] = l0.E[16, 0:8, :]
    ds[2] = l0.E[1, 8:16, :]
    ds[3] = l0.E[1, 0:8, :]

    def pack2(v):
        v = v.reshape(4, 2, 8, 128)
        return jnp.where((lane & 1) == 0, v[:, 0], v[:, 1])

    es[0, gz, 0:4] = pack2(halve(l0.E[1:17, 0:16, :], 0, tmp))
    es[0, gz, 4:8] = pack2(halve(l0.S[:, 0:16, :], 0, tmp, 8))

    def r1_copies():
        return [
            remote(xs.at[0], xr.at[0], s_r1.at[0], r_r1.at[0], gx_at(1), gz),
            remote(xs.at[1], xr.at[1], s_r1.at[1], r_r1.at[1], gx_at(-1), gz),
            remote(zs.at[0], zr.at[0], s_r1.at[2], r_r1.at[2], gx, gz_at(1)),
            remote(zs.at[1], zr.at[1], s_r1.at[3], r_r1.at[3], gx, gz_at(-1)),
            remote(ds.at[0], dr.at[0], s_r1.at[4], r_r1.at[4], gx_at(1), gz_at(1)),
            remote(ds.at[1], dr.at[1], s_r1.at[5], r_r1.at[5], gx_at(-1), gz_at(1)),
            remote(ds.at[2], dr.at[2], s_r1.at[6], r_r1.at[6], gx_at(1), gz_at(-1)),
            remote(ds.at[3], dr.at[3], s_r1.at[7], r_r1.at[7], gx_at(-1), gz_at(-1)),
        ]

    pl.semaphore_wait(barrier, 3 * ngz - 1 + ngx - 3)
    for copy in r1_copies():
        copy.start()

    def f1_copies(act):
        def go(slot, k, src, dst, tx):
            act(remote(src, dst, s_f1.at[slot, k], r_f1.at[slot, gz], tx, gz_at(k)))

        for k in (4, 3, 5, 2, 6, 1, 7, 0):
            if k:
                go(0, k, f1.at[gz], f1.at[gz], gx)
            go(1, k, fh.at[0], fr.at[0, gz], gx_at(1))
            go(2, k, fh.at[1], fr.at[1, gz], gx_at(-1))

    def f1_arrive(k):
        p = gz_at(k)
        for slot, dst in ((0, f1.at[gz]), (1, fr.at[0, gz]), (2, fr.at[1, gz])):
            if slot or k:
                remote(dst, dst, s_f1.at[slot, k], r_f1.at[slot, p], gx, gz_at(1)).wait_recv()

    def es_lines(act):
        for k in FAR_FIRST:
            act(remote(es.at[0, gz], es.at[0, gz], s_es.at[0, k], r_es.at[0, gz], gx, gz_at(k)))

    def es_planes():
        return [
            remote(es.at[0], es.at[2], s_es.at[2, 0], r_es.at[2, 0], gx_at(1), gz),
            remote(es.at[0], es.at[1], s_es.at[1, 0], r_es.at[1, 0], gx_at(-1), gz),
        ]

    es_lines(lambda c: c.start())

    for copy in r1_copies():
        copy.wait_recv()

    above, below = gz > 0, gz < ngz - 1
    zero16 = jnp.zeros((16, 24, 128), F32)
    l0.E[0:1] = zero16[0:1]
    l0.E[17:18] = zero16[0:1]
    l0.E[1:17, 16:24, :] = zero16[:, 0:8]
    l0.S[:, 16:24, :] = jnp.ones((16, 8, 128), F32)
    l0.F[:, 16:24, :] = zero16[:, 0:8]
    l0.E[1:17, 22:24, :] = jnp.where(has_left, xr[0, :, 0:2, :], 0.0)
    l0.S[:, 23:24, :] = jnp.where(has_left, xr[0, :, 2:3, :], 1.0)
    l0.F[:, 23:24, :] = jnp.where(has_left, xr[0, :, 3:4, :], 0.0)
    l0.E[1:17, 16:18, :] = jnp.where(has_right, xr[1, :, 0:2, :], 0.0)
    l0.S[:, 16:17, :] = jnp.where(has_right, xr[1, :, 2:3, :], 1.0)
    l0.F[:, 16:17, :] = jnp.where(has_right, xr[1, :, 3:4, :], 0.0)
    l0.E[0, 0:16, :] = jnp.where(above, zr[0], 0.0)
    l0.E[17, 0:16, :] = jnp.where(below, zr[1], 0.0)
    l0.E[0, 23:24, :] = jnp.where(above & has_left, dr[0, 7:8, :], 0.0)
    l0.E[0, 16:17, :] = jnp.where(above & has_right, dr[1, 0:1, :], 0.0)
    l0.E[17, 23:24, :] = jnp.where(below & has_left, dr[2, 7:8, :], 0.0)
    l0.E[17, 16:17, :] = jnp.where(below & has_right, dr[3, 0:1, :], 0.0)

    for i in range(4):
        wzp = couplings(l0, i * 4, 4)
    l0.WZ[16:17] = wzp[3:4]

    m = 1.0 / l0.D[0]
    l0.M[0] = m
    for z in range(1, 15):
        w = l0.WZ[z]
        a = w * m
        m = 1.0 / (l0.D[z] - w * a)
        l0.A[z] = a
        l0.M[z] = m
    lead = jnp.where(above, l0.WZ[0], 0.0)
    tail = l0.WZ[15]

    y = lead
    av[0] = y
    for z in range(1, 15):
        y = l0.A[z] * y
        av[z] = y
    x = l0.M[14] * y
    b = l0.M[14] * tail
    av[14] = x
    bv[14] = b
    for z in range(13, -1, -1):
        x = l0.M[z] * av[z] + l0.A[z + 1] * x
        b = l0.A[z + 1] * b
        av[z] = x
        bv[z] = b

    def inner(src):
        y = src[0]
        l0.Y[0] = y
        for z in range(1, 15):
            y = src[z] + l0.A[z] * y
            l0.Y[z] = y
        x = l0.M[14] * y
        l0.Y[14] = x
        for z in range(13, -1, -1):
            x = l0.M[z] * l0.Y[z] + l0.A[z + 1] * x
            l0.Y[z] = x

    inner(l0.F)

    def put(k, v):
        red[gz, pl.ds(k * 18, 17), :] = v[0:17]
        red[gz, pl.ds(k * 18 + 17, 1), :] = v[23:24]

    put(0, tail * av[14])
    put(1, l0.D[15] - tail * bv[14])
    put(2, lead * av[0])
    put(3, l0.F[15] + tail * l0.Y[14])
    put(4, lead * l0.Y[0])

    def gather(buf, ss, rs, act):
        for k in FAR_FIRST:
            act(remote(buf.at[gz], buf.at[gz], ss.at[k], rs.at[gz], gx, gz_at(k)))

    def post_copies(act):
        for k in FAR_FIRST:
            side = lax.div(gz + k, ngz)
            act(remote(ps.at[side], post_red.at[gz], s_post.at[k], r_post.at[gz], gx, gz_at(k)))

    def gathered(buf, ss, rs):
        def get(k):
            p = gz_at(k)
            remote(buf.at[gz], buf.at[p], ss.at[k], rs.at[p], gx, p).wait_recv()

        loop(ngz - 1, lambda k: get(k + 1))

    gather(red, s_red, r_red, lambda c: c.start())

    def es_line_in(k):
        p = gz_at(k + 1)
        remote(es.at[0, gz], es.at[0, p], s_es.at[0, k + 1], r_es.at[0, p], gx, p).wait_recv()

    loop(ngz - 1, es_line_in)
    for copy in es_planes():
        copy.start()

    mask1 = jnp.where(row24 < 8, 1.0, jnp.where(row24 < 16, jnp.where(has_right, 1.0, 0.0), jnp.where(has_left, 1.0, 0.0)))
    mask2 = jnp.where(
        row16 < 4,
        1.0,
        jnp.where(row16 < 8, jnp.where(has_right, 1.0, 0.0), jnp.where(row16 < 12, 0.0, jnp.where(has_left, 1.0, 0.0))),
    )
    l1.mask, l2.mask = mask1, mask2

    def unpack2(v):
        even = jnp.where((lane & 1) == 0, v, roll(v, 1, 2))
        odd = jnp.where((lane & 1) == 1, v, roll(v, -1, 2))
        return jnp.stack([even, odd], axis=1).reshape(2 * v.shape[0], 8, 128)

    here = (None, has_right, has_left)

    def place(buf, start, dst, offset, outside, slots):
        for slot in slots:
            for p in range(ngz):
                v = unpack2(buf[slot, p, start : start + 4])
                if slot:
                    v = jnp.where(here[slot], v, outside)
                dst[p * 8 + offset : p * 8 + offset + 8, slot * 8 : slot * 8 + 8, :] = v

    place(es, 0, l1.E, 1, 0.0, (0,))
    place(es, 4, l1.S, 0, 1.0, (0,))

    def coarsen(src, offset, fine, coarse, dst, dst_offset, split):
        n = fine.n

        def body(i):
            v = halve(src[i * n + offset : (i + 1) * n + offset], fine.index, tmp, i * (n // 2))
            at = slice(i * (n // 2) + dst_offset, (i + 1) * (n // 2) + dst_offset)
            if split:
                dst[at, 0:8, :] = v[:, 0:8]
                dst[at, 12:16, :] = v[:, 8:12]
            else:
                dst[at] = v

        unrolled(fine.Z // n, body)

    def filler(ref, value):
        ref[:, 8:12, :] = jnp.full((ref.shape[0], 4, 128), value, F32)

    filler(l2.E, 0.0)
    filler(l2.S, 1.0)
    filler(l2.F, 0.0)

    lane3 = iota((2, 2, 128), 2)

    def pack8(src, offset, buf, first):
        for i in range(2):
            v = halve(src[i * 16 + offset : i * 16 + offset + 16], 2, tmp, i * 8)[:, 0:2]
            tmp[i * 8 : i * 8 + 8, 32:34, :] = v
        v = tmp[0:16, 32:34, :].reshape(2, 8, 2, 128)
        picked = v[:, 7]
        for k in range(7):
            picked = jnp.where((lane3 & 7) == k, v[:, k], picked)
        for zz in range(2):
            buf[gx, first + zz * 2 : first + zz * 2 + 2, :] = picked[zz]

    core, x4, y4 = lax.rem(gx, 2), lax.rem(lax.div(gx, 2), 4), lax.div(gx, 8)
    hops = sorted(((dy, dx, dc) for dy in range(4) for dx in range(4) for dc in range(2)), key=lambda t: -(min(t[0], 4 - t[0]) + min(t[1], 4 - t[1]) + 0.5 * t[2]))
    far_gx = [lax.rem(y4 + dy, 4) * 8 + lax.rem(x4 + dx, 4) * 2 + lax.rem(core + dc, 2) for dy, dx, dc in hops[:-1]]

    def spread(buf, ss, rs, act):
        for i, tx in enumerate(far_gx):
            act(remote(buf.at[gx], buf.at[gx], ss.at[i], rs.at[gx], tx, gz))

    def collected(buf, ss, rs):
        def get(k):
            p = gx_at(k)
            remote(buf.at[gx], buf.at[p], ss.at[k], rs.at[p], p, gz).wait_recv()

        loop(ngx - 1, lambda k: get(k + 1))

    gathered(red, s_red, r_red)

    def got(p, k):
        return red[p, pl.ds(k * 18, 18), :]

    m, y = None, None
    for p in range(ngz):
        diag, right = got(p, 1), got(p, 3)
        if p + 1 < ngz:
            diag, right = diag - got(p + 1, 2), right + got(p + 1, 4)
        if p:
            c = got(p, 0)
            a = c * m
            diag, right = diag - c * a, right + a * y
            ra[p] = a
        m, y = 1.0 / diag, right
        rm[p] = m
        ub[p + 1, 0:18, :] = y
    x = m * y
    for p in range(ngz - 1, -1, -1):
        if p + 1 < ngz:
            x = rm[p] * ub[p + 1, 0:18, :] + ra[p + 1] * x
        ub[p + 1, 0:17, :] = x[0:17]
        ub[p + 1, 23:24, :] = x[17:18]
        ub[p + 1, 17:23, :] = jnp.zeros((6, 128), F32)
    ub[0] = jnp.zeros((24, 128), F32)

    before, own = ub[gz], ub[gz + 1]
    for z in range(15):
        l0.U[z] = OMEGA * (l0.Y[z] + av[z] * before + bv[z] * own)
    l0.U[15] = OMEGA * own

    def first_residual(i):
        z0 = i * 4
        l0.R[pl.ds(z0, 4)] = (1.0 - OMEGA) * l0.F[pl.ds(z0, 4)] + lateral(l0, l0.U[pl.ds(z0, 4)], z0, 4)

    unrolled(4, first_residual)
    packed = pack2(halve(l0.R[:, 0:16, :], 0, tmp))
    f1[gz] = packed
    for zz in range(4):
        fh[0, zz * 4 : zz * 4 + 4, :] = packed[zz, 4:8]
        fh[1, zz * 4 : zz * 4 + 4, :] = packed[zz, 0:4]
    f1_copies(lambda c: c.start())

    q = got(ngz - 1, 1)[0:16]
    pivots[ngz - 1] = q
    for p in range(ngz - 1, 0, -1):
        c = got(p, 0)[0:16]
        b = c * (1.0 / q)
        rb[p] = b
        q = got(p - 1, 1)[0:16] - got(p, 2)[0:16] - c * b
        pivots[p - 1] = q
    rb[0] = jnp.zeros((16, 128), F32)
    c = jnp.where(above, red[gz, 0:16, :], 0.0)
    left = rm[jnp.maximum(gz - 1, 0), 0:16, :]
    mid[0] = left
    mid[1] = c * left
    mid[2] = 1.0 / (pivots[gz] - c * c * left)
    mid[3] = c

    for copy in es_planes():
        copy.wait_recv()
    place(es, 0, l1.E, 1, 0.0, (1, 2))
    place(es, 4, l1.S, 0, 1.0, (1, 2))
    coarsen(l1.E, 1, l1, l2, l2.E, 1, True)
    coarsen(l1.S, 0, l1, l2, l2.S, 0, True)
    pack8(l2.E, 1, es3, 0)
    pack8(l2.S, 0, es3, 4)
    spread(es3, s_e3, r_e3, lambda c: c.start())
    prepare(l1)
    prepare(l2)

    lane32 = iota((32, 128), 1)

    def swap(v, s):
        return jnp.where((lane32 & s) == 0, roll(v, -s, 1), roll(v, s, 1))

    def place8(buf, first, dst, offset):
        for zz in range(2):
            for xp in range(2):
                found = [(buf[:, first + zz * 2 + xp, :], 0)]
                for bit in (1, 2, 4):
                    split = []
                    for v, z in found:
                        w = swap(v, bit)
                        low = (lane32 & bit) == 0
                        split += [(jnp.where(low, v, w), z), (jnp.where(low, w, v), z + bit)]
                    found = split
                for v, z in found:
                    dst[offset + zz * 8 + z, pl.ds(xp, ngx, stride=2), :] = v

    l1.F[:, 8:24, :] = jnp.zeros((l1.Z, 16, 128), F32)
    lane16 = iota((16, 128), 1)
    for k in FAR_FIRST + (0,):
        p = gz_at(k)
        f1_arrive(k)
        l1.F[pl.ds(p * 8, 8), 0:8, :] = unpack2(f1[p])
        for side, present, row in ((0, has_left, 20), (1, has_right, 8)):
            v = jnp.where(present, fr[side, p], 0.0)
            both = (jnp.where((lane16 & 1) == 0, v, roll(v, 1, 1)), jnp.where((lane16 & 1) == 1, v, roll(v, -1, 1)))
            for zz in range(4):
                for j in range(2):
                    l1.F[p * 8 + zz * 2 + j, row : row + 4, :] = both[j][zz * 4 : zz * 4 + 4]
    pre(l1)
    coarsen(l1.R, 0, l1, l2, l2.F, 0, True)
    lane8 = iota((8, 8, 128), 2)
    v = l2.F[:, 0:8, :].reshape(8, 4, 8, 128)
    k = lane8 & 3
    f2[...] = jnp.where(k == 0, v[:, 0], jnp.where(k == 1, v[:, 1], jnp.where(k == 2, v[:, 2], v[:, 3])))

    def f2_copies():
        return [
            remote(f2, f2r.at[0], s_f2.at[0], r_f2.at[0], gx_at(1), gz),
            remote(f2, f2r.at[1], s_f2.at[1], r_f2.at[1], gx_at(-1), gz),
        ]

    for copy in f2_copies():
        copy.start()

    pre(l2)
    pack8(l2.R, 0, f3, 0)
    spread(f3, s_f3, r_f3, lambda c: c.start())

    collected(es3, s_e3, r_e3)
    place8(es3, 0, l3.E, 1)
    place8(es3, 4, l3.S, 0)
    deep = [l3, l4, l5, l6]
    for fine, coarse in zip(deep[:-1], deep[1:]):
        coarsen(fine.E, 1, fine, coarse, coarse.E, 1, False)
        coarsen(fine.S, 0, fine, coarse, coarse.S, 0, False)
    for lev in deep:
        prepare(lev)

    for copy in f2_copies():
        copy.wait_recv()

    def swap8(v, s):
        return jnp.where((lane8 & s) == 0, roll(v, -s, 2), roll(v, s, 2))

    for side, present, source, row in ((0, has_left, 2, 14), (1, has_right, 1, 5)):
        v = jnp.where(present, f2r[side], 0.0)
        w = swap8(v, 1)
        for k0 in range(2):
            v1 = jnp.where((lane8 & 1) == k0, v, w)
            w1 = swap8(v1, 2)
            for k1 in range(2):
                v2 = jnp.where(((lane8 >> 1) & 1) == k1, v1, w1)
                for zz in range(8):
                    l2.F[zz * 4 + k1 * 2 + k0, row : row + 1, :] = v2[zz, source : source + 1]
    pre(l2)

    collected(f3, s_f3, r_f3)
    place8(f3, 0, l3.F, 0)
    for fine, coarse in zip(deep[:-1], deep[1:]):
        pre(fine)
        coarsen(fine.R, 0, fine, coarse, coarse.F, 0, False)
    coarsest(l6)
    for fine, coarse in zip(deep[-2::-1], deep[:0:-1]):
        unrolled(coarse.Z, lambda z, fine=fine, coarse=coarse: spread_rows(fine.V, 2 * z + 1, coarse.C[z + 1], ((0, coarse.X, 0),)))
        post(fine)

    tiles = ngx // 4
    first = gx // 4
    shift = lax.rem(24 - 2 * lax.rem(gx, 4), 24)

    def tile_at(z, k):
        return l3.C[z, pl.ds(pl.multiple_of(lax.rem(first + (k + tiles), tiles) * 8, 8), 8), :]

    right_rows, left_rows = (iota((4, 128), 0) < 2) | has_right, has_left

    def down3(z):
        c = jnp.concatenate([tile_at(z + 1, 0), tile_at(z + 1, 1), tile_at(z + 1, -1)], axis=0)
        c = pltpu.roll(c, shift, 0)
        for k in range(2):
            for j in range(2):
                l2.V[2 * z + 1 + k, pl.ds(j, 4, stride=2), :] = jnp.where(right_rows, c[0:4], 0.0)
                l2.V[2 * z + 1 + k, pl.ds(12 + j, 2, stride=2), :] = jnp.where(left_rows, c[22:24], 0.0)

    filler(l2.V, 0.0)
    unrolled(l3.Z, down3)
    post(l2)
    unrolled(l2.Z, lambda z: spread_rows(l1.V, 2 * z + 1, l2.C[z + 1], ((0, 4, 0), (4, 4, 8), (12, 4, 16))))
    post(l1)
    l1.C[0] = jnp.zeros((24, 128), F32)
    l1.C[l1.Z + 1] = jnp.zeros((24, 128), F32)

    for i in range(10):
        c = l1.C[gz * 8 + i]
        for z in (2 * i - 1, 2 * i):
            if 0 <= z < 18:
                for j in range(2):
                    l0.V[z, pl.ds(j, 8, stride=2), :] = c[0:8]
                l0.V[z, 16:17, :] = c[8:9]
                l0.V[z, 17:23, :] = jnp.zeros((6, 128), F32)
                l0.V[z, 23:24, :] = c[23:24]

    def second_residual(i):
        z0 = i * 4
        v = l0.V[pl.ds(z0 + 1, 4)]
        around = lateral(l0, v, z0, 4) + l0.WZ[pl.ds(z0, 4)] * l0.V[pl.ds(z0, 4)] + l0.WZ[pl.ds(z0 + 1, 4)] * l0.V[pl.ds(z0 + 2, 4)]
        l0.F[pl.ds(z0, 4)] = l0.R[pl.ds(z0, 4)] - (l0.D[pl.ds(z0, 4)] * v - around)

    unrolled(4, second_residual)
    inner(l0.F)
    end_row, first_row = (l0.F[15] + tail * l0.Y[14])[0:16], (lead * l0.Y[0])[0:16]
    ps[0] = end_row + jnp.where(above, ra[gz, 0:16, :], 0.0) * first_row
    ps[1] = first_row + rb[gz] * end_row
    post_red[gz] = jnp.zeros((16, 128), F32)
    post_copies(lambda c: c.start())
    for z in range(16):
        l0.U[z, 0:16, :] = l0.U[z, 0:16, :] + l0.V[z + 1, 0:16, :]
    for copy in r1_copies():
        copy.wait_send()
    es_lines(lambda c: c.wait_send())
    for copy in es_planes():
        copy.wait_send()
    f1_copies(lambda c: c.wait_send())
    for copy in f2_copies():
        copy.wait_send()
    gather(red, s_red, r_red, lambda c: c.wait_send())
    spread(es3, s_e3, r_e3, lambda c: c.wait_send())
    spread(f3, s_f3, r_f3, lambda c: c.wait_send())
    gathered(post_red, s_post, r_post)
    tau = jnp.zeros((16, 128), F32)
    for p in range(ngz - 1):
        took = post_red[p] if p == 0 else post_red[p] + ra[p, 0:16, :] * tau
        tau = jnp.where(p < gz, took, tau)
    sigma = jnp.zeros((16, 128), F32)
    for p in range(ngz - 1, 0, -1):
        sigma = jnp.where(p > gz, post_red[p] + rb[p] * sigma, sigma)
    b1 = first_row + tau
    own = mid[2] * (end_row + sigma + mid[1] * b1)
    before = mid[0] * (b1 + mid[3] * own)
    for z in range(16):
        if z < 15:
            x = l0.Y[z, 0:16, :] + av[z, 0:16, :] * before + bv[z, 0:16, :] * own
        else:
            x = own
        out[pl.ds(z, 16, stride=16), :] = l0.U[z, 0:16, :] + OMEGA * x

    post_copies(lambda c: c.wait_send())


def solution(mesh):
    ngx, ngz = mesh.shape["gx"], mesh.shape["gz"]

    def per_device(charge, codes, eps_table, screen_table):
        nx, nz, ny = charge.shape
        whole_z, whole_x = nz * ngz, nx * ngx
        levels = [
            (nz, 24),
            (whole_z // 2, 24),
            (whole_z // 4, 16),
            (whole_z // 8, whole_x // 8),
            (whole_z // 16, whole_x // 16),
            (whole_z // 32, whole_x // 32),
            (whole_z // 64, whole_x // 64),
        ]
        scratch = []
        for Z, X in levels:
            scratch += Level.scratch(Z, X)
        vm = lambda *shape: pltpu.VMEM(shape, F32)
        scratch += [
            vm(64, 64, 128),
            pltpu.VMEM((nx * nz, ny), jnp.int32),
            vm(nx * nz, ny),
            pltpu.SemaphoreType.DMA((2,)),
            vm(2, 16, 4, 128),
            vm(2, 16, 4, 128),
            vm(2, 16, 128),
            vm(2, 16, 128),
            vm(4, 8, 128),
            vm(4, 8, 128),
            vm(3, ngz, 8, 8, 128),
            vm(ngz, 4, 8, 128),
            vm(ngz, 90, 128),
            vm(ngz, 16, 128),
            vm(ngz + 1, 24, 128),
            vm(ngz, 18, 128),
            vm(ngz, 18, 128),
            vm(16, 24, 128),
            vm(16, 24, 128),
            vm(ngx, 8, 128),
            vm(ngx, 4, 128),
            vm(2, 16, 128),
            vm(2, ngz, 16, 128),
            vm(8, 8, 128),
            vm(2, 8, 8, 128),
            vm(2, 16, 128),
            vm(ngz, 16, 128),
            vm(ngz, 16, 128),
            vm(4, 16, 128),
        ]
        for shape in ((8,), (3, ngz), (3, ngz), (ngz,), (ngz,), (ngx,), (ngx,), (2,)):
            scratch += [pltpu.SemaphoreType.DMA(shape)] * 2
        result = pl.pallas_call(
            lambda *refs: kernel(ngx, ngz, *refs),
            out_shape=jax.ShapeDtypeStruct((nx * nz, ny), F32),
            in_specs=[
                pl.BlockSpec(memory_space=pl.ANY),
                pl.BlockSpec(memory_space=pl.ANY),
                pl.BlockSpec(memory_space=pltpu.SMEM),
                pl.BlockSpec(memory_space=pltpu.SMEM),
            ],
            out_specs=pl.BlockSpec(memory_space=pltpu.VMEM),
            scratch_shapes=scratch,
            compiler_params=pltpu.CompilerParams(collective_id=0, has_side_effects=True, vmem_limit_bytes=55040 << 10),
            name="vcycle",
        )(codes.reshape(nx * nz, ny), charge.reshape(nx * nz, ny), eps_table, screen_table)
        return result.reshape(nx, nz, ny)

    return jax.shard_map(
        per_device,
        mesh=mesh,
        in_specs=(P("gx", "gz", None), P("gx", "gz", None), P(), P()),
        out_specs=P("gx", "gz", None),
        check_vma=False,
    )
```
